32 devices in a mesh: seq: 8 (over z, x), tp: 4 (over y, core).
Axes of the slice: x: 2, y: 2, z: 4, core: 2. Of those that a mesh axis runs over, the one named last changes fastest.
Arguments:
- hidden: bfloat16 [2048, 2048], P('seq', 'tp'), may hold values from -6 to 6
- lengths: int32 [8, 4], P('seq'), may hold values from 1 to 128, 256 in all within a row
- cache_owner: int32 [2], replicated, may hold values from 0 to 3, as said below
- cache_pool: bfloat16 [8, 1024, 2, 2048], P('seq', None, None, 'tp'), may hold values from -6 to 6
- norm_gain: float32 [2048], replicated, may hold values from 0.1 to 1.9
- route_idx: int32 [2048, 2], P('seq'), may hold values from 0 to 3, all different within a row
- route_gate: float32 [2048, 2], P('seq'), may hold values from 0.25 to 1
- w_query: bfloat16 [2048, 4, 2048], P('seq', None, 'tp'), may hold values from -0.13258252 to 0.13258252
- w_keyval: bfloat16 [2048, 2, 2048], P('seq', None, 'tp'), may hold values from -3.535534 to 3.535534
- w_out: bfloat16 [4, 2048, 2048], P(None, 'tp', 'seq'), may hold values from -2 to 2
Outputs:
- attn_out: bfloat16 [2048, 2048], P('seq', 'tp')
The draws below stay inside these ranges and needn't reach their ends.
Inputs may be any that keep to these rules, and one draw needn't show every extreme that they name: `cache_owner`: index, within its group's block of 4 devices, of the device whose cache slot holds the group's prefix.
All inputs are finite; a program needn't handle non-finite values.
Results may differ from the reference program's by a relative error of at most 0.0075.
Values may be sent and summed in bfloat16 or wider, within the bound.
A program may use at most 128 MiB of HBM per device.

```python
import math
import jax
import jax.numpy as jnp
import numpy as np
from jax import lax

D = 2048
HEADS = 16
HD = 128
ATT_EXP = 4
TOPK = 2
GROUP_DEVS = 4
REQ_DEV = 4
PREFIX = 1024
TOK_DEV = 256
MOST = 128
GROUPS = 2
TOKENS = 2048
N_SEQ = 8


def draw_w_query(key, part):
    values = jax.random.truncated_normal(jax.random.fold_in(key, 201), -4.0, 4.0, (D, ATT_EXP, HEADS * HD), jnp.float32) / D ** 0.5
    return values.astype(jnp.bfloat16)


def draw_w_keyval(key, part):
    value_map = jax.random.truncated_normal(jax.random.fold_in(key, 104), -4.0, 4.0, (D, HEADS * HD), jnp.float32) / D ** 0.5
    key_map = jax.random.truncated_normal(jax.random.fold_in(key, 202), -4.0, 4.0, (D, HEADS * HD), jnp.float32) / D ** 0.5
    return jnp.stack([key_map, value_map], axis=1).astype(jnp.bfloat16)


def draw_cache_owner(key, part):
    others = jax.random.randint(jax.random.fold_in(key, 311), (GROUPS,), 0, GROUP_DEVS - 1)
    spot = jax.random.randint(jax.random.fold_in(key, 312), (), 0, GROUPS)
    return jnp.where(jnp.arange(GROUPS) == spot, GROUP_DEVS - 1, others).astype(jnp.int32)


def shard_levels(rng, extent, cuts, low, largest):
    def one(axis_at, parts):
        steps = jax.random.uniform(jax.random.fold_in(jax.random.fold_in(rng, 6), axis_at), (parts,), jnp.float32, low / len(cuts), largest / len(cuts))
        return jnp.repeat(jnp.exp(steps), extent[axis_at] // parts).reshape((-1,) + (1,) * (len(extent) - axis_at - 1))

    factor_of = one(*cuts[0])
    for cut in cuts[1:]:
        factor_of = factor_of * one(*cut)
    return factor_of


def different_ones(stream_key, rows, number_of, top, lift):
    sequence = jax.random.permutation(jax.random.fold_in(stream_key, 1), number_of)
    favour = sequence
    for power in range(3):
        favour = favour * favour // number_of
    favour = favour * lift // number_of
    chance = jax.random.randint(jax.random.fold_in(stream_key, 2), (rows, number_of), 0, 4096) + favour
    fixed_rows = jax.random.permutation(jax.random.fold_in(stream_key, 3), rows)[jnp.arange(number_of) % rows]
    chance = jnp.where(jnp.arange(rows)[:, None] == fixed_rows[None, :], 1 << 14, chance)
    merit = chance * number_of + jnp.arange(number_of)
    return lax.top_k(merit.astype(jnp.int32), top)[1].astype(jnp.int32)


def length_profile(amount, total, bound, skew):
    loads = [(1 << 20) // math.isqrt(standing ** skew) + 1 for standing in range(2, amount + 1)]
    spare, holding = total - bound - (amount - 1), [1] * (amount - 1)
    while spare > 0:
        candidates = [i for i in range(amount - 1) if holding[i] < bound]
        whole, left = sum([loads[i] for i in candidates]), spare
        for i in candidates:
            extra = min(bound - holding[i], max(1, left * loads[i] // whole), spare)
            holding[i] = holding[i] + extra
            spare = spare - extra
    return np.array([bound] + holding)


def ragged_sizes(rng, number_of, total, reach, slope):
    if number_of == 2:
        one = jax.random.randint(rng, (), max(1, total - reach), min(reach, total - 1) + 1)
        return jnp.stack([one, total - one])
    sizes = jnp.asarray(length_profile(number_of, total, reach, slope), jnp.int32)
    twos = (number_of - 1) // 2
    giver, taker = sizes[1:1 + 2 * twos:2], sizes[2:2 + 2 * twos:2]
    margin = jnp.minimum(giver - 1, reach - taker)
    shifted = jax.random.randint(jax.random.fold_in(rng, 1), (twos,), 0, 1 << 20) % (margin + 1)
    sizes = sizes.at[1:1 + 2 * twos:2].set(giver - shifted).at[2:2 + 2 * twos:2].set(taker + shifted)
    return sizes[jax.random.permutation(jax.random.fold_in(rng, 2), number_of)]


def centred(own_key, extent, scale, reach, pieces=(), kind=jnp.bfloat16):
    values = scale * jax.random.normal(own_key, extent, jnp.float32)
    if pieces:
        values = values * shard_levels(own_key, extent, pieces, -0.22, 0.18)
    return jnp.clip(values, -reach, reach).astype(kind)


def setup_inputs(seed: int = 0) -> dict:
    key_list = jax.random.split(jax.random.key(seed), 11)
    hidden = centred(key_list[0], (TOKENS, D), 1.0, 6.0, ((0, 8), (1, 4)))
    lengths = jax.vmap(lambda own: ragged_sizes(own, REQ_DEV, TOK_DEV, MOST, 2))(jax.random.split(key_list[1], N_SEQ)).reshape((N_SEQ, REQ_DEV)).astype(jnp.int32)
    cache_owner = draw_cache_owner(jax.random.fold_in(key_list[10], 71), 0)
    cache_pool = centred(key_list[3], (N_SEQ, PREFIX, 2, HEADS * HD), 1.0, 6.0, ((0, 8), (3, 4)))
    norm_gain = jnp.clip(1.0 + 0.18 * jax.random.normal(key_list[4], (D,), jnp.float32), 0.1, 1.9)
    route_idx = different_ones(key_list[5], TOKENS, ATT_EXP, TOPK, 4096)
    route_gate = jnp.clip(0.25 + 0.75 * jax.random.uniform(key_list[6], (TOKENS, TOPK), jnp.float32) ** shard_levels(key_list[6], (TOKENS, TOPK), ((0, 8),), -0.2, 0.2), 0.25, 1.0)
    w_query = draw_w_query(jax.random.fold_in(key_list[10], 71), 0)
    w_keyval = draw_w_keyval(jax.random.fold_in(key_list[10], 71), 0)
    w_out = centred(key_list[9], (ATT_EXP, HEADS * HD, D), 8 ** -0.5, 2.0, ((1, 4), (2, 8)))
    return dict(hidden=hidden, lengths=lengths, cache_owner=cache_owner, cache_pool=cache_pool, norm_gain=norm_gain, route_idx=route_idx, route_gate=route_gate, w_query=w_query, w_keyval=w_keyval, w_out=w_out)


EPSILON = 1e-05
THETA = 10000.0

def rotate(vectors, cosine, sine):
    half = vectors.shape[-1] // 2
    first = vectors[..., :half]
    second = vectors[..., half:]
    return jnp.concatenate([first * cosine - second * sine, second * cosine + first * sine], axis=-1)

def request_layout(lengths_row, count):
    ends = jnp.cumsum(lengths_row).astype(jnp.int32)
    starts = (ends - lengths_row).astype(jnp.int32)
    token_ids = jnp.arange(count, dtype=jnp.int32)
    segment = lax.optimization_barrier(jnp.sum((token_ids[:, None] >= ends[None, :]).astype(jnp.int32), axis=1))
    request_ids = jnp.arange(lengths_row.shape[0], dtype=jnp.int32)
    begin = lax.optimization_barrier(jnp.sum(jnp.where(segment[:, None] == request_ids[None, :], starts[None, :], 0), axis=1))
    position = (token_ids - begin).astype(jnp.int32)
    visible = (segment[:, None] == segment[None, :]) & (token_ids[None, :] <= token_ids[:, None])
    return (position, visible)

def rope_tables(position, prefix_len, head_dim):
    freqs = THETA ** (-(jnp.arange(head_dim // 2, dtype=jnp.float32) * 2.0) / head_dim)
    angles = (position + prefix_len).astype(jnp.float32)[:, None] * freqs[None, :]
    return (jnp.cos(angles), jnp.sin(angles))

def attend_head(query, keys, values, visible):
    scale = query.shape[-1] ** (-0.5)
    scores = jnp.einsum('tkd,sd->tks', query.astype(jnp.float32), keys.astype(jnp.float32), precision=lax.Precision.HIGHEST) * scale
    seen = visible[:, None, :]
    scores = jnp.where(seen, scores, -1e+30)
    top = lax.optimization_barrier(jnp.max(scores, axis=-1, keepdims=True))
    weights = jnp.where(seen, jnp.exp(scores - top), 0.0)
    total = lax.optimization_barrier(jnp.sum(weights, axis=-1, keepdims=True))
    rounded = weights.astype(jnp.bfloat16)
    numer = jnp.einsum('tks,sd->tkd', rounded.astype(jnp.float32), values.astype(jnp.float32), precision=lax.Precision.HIGHEST)
    return numer / total

def reference(hidden, lengths, cache_owner, cache_pool, norm_gain, route_idx, route_gate, w_query, w_keyval, w_out):
    width = HEADS * HD
    query_mat = w_query.reshape(D, ATT_EXP * width)
    keyval_mat = w_keyval.reshape(D, 2 * width)
    out_mat = w_out.reshape(ATT_EXP * width, D)
    expert_ids = jnp.arange(ATT_EXP, dtype=jnp.int32)

    def one_device(device):
        first_row = (device * TOK_DEV).astype(jnp.int32)
        rows = lax.dynamic_slice_in_dim(hidden, first_row, TOK_DEV, 0).astype(jnp.float32)
        normed = (rows * lax.rsqrt(lax.optimization_barrier(jnp.mean(rows * rows, axis=1, keepdims=True)) + EPSILON) * norm_gain[None, :]).astype(jnp.bfloat16)
        all_queries = jnp.dot(normed, query_mat, preferred_element_type=jnp.float32).reshape(TOK_DEV, ATT_EXP, width)
        keyval = jnp.dot(normed, keyval_mat, preferred_element_type=jnp.float32).reshape(TOK_DEV, 2, HEADS, HD)
        lengths_row = lax.dynamic_index_in_dim(lengths, device, 0, keepdims=False)
        position, visible = request_layout(lengths_row, TOK_DEV)
        cosine, sine = rope_tables(position, PREFIX, HD)
        chosen_idx = lax.dynamic_slice_in_dim(route_idx, first_row, TOK_DEV, 0)
        gates = lax.dynamic_slice_in_dim(route_gate, first_row, TOK_DEV, 0)
        onehot = (chosen_idx[:, :, None] == expert_ids[None, None, :]).astype(jnp.float32)
        chosen = lax.optimization_barrier(jnp.sum(onehot[:, :, :, None] * all_queries[:, None, :, :], axis=2))
        queries = rotate(chosen.reshape(TOK_DEV, TOPK, HEADS, HD), cosine[:, None, None, :], sine[:, None, None, :]).astype(jnp.bfloat16)
        new_keys = rotate(keyval[:, 0], cosine[:, None, :], sine[:, None, :]).astype(jnp.bfloat16)
        new_values = keyval[:, 1].astype(jnp.bfloat16)
        group = device // GROUP_DEVS
        owner_dev = (group * GROUP_DEVS + lax.dynamic_index_in_dim(cache_owner, group, 0, keepdims=False)).astype(jnp.int32)
        prefix = lax.dynamic_index_in_dim(cache_pool, owner_dev, 0, keepdims=False).reshape(PREFIX, 2, HEADS, HD)
        keys_all = jnp.concatenate([prefix[:, 0], new_keys], axis=0)
        values_all = jnp.concatenate([prefix[:, 1], new_values], axis=0)
        visible_all = jnp.concatenate([jnp.ones((TOK_DEV, PREFIX), dtype=bool), visible], axis=1)

        def per_head(operands):
            return attend_head(operands[0], operands[1], operands[2], visible_all)
        att = lax.map(per_head, (jnp.moveaxis(queries, 2, 0), jnp.moveaxis(keys_all, 1, 0), jnp.moveaxis(values_all, 1, 0)))
        att = jnp.moveaxis(att, 0, 2).reshape(TOK_DEV, TOPK, width)
        blend = gates[:, :, None] * onehot
        mixed = lax.optimization_barrier(jnp.sum(blend[:, :, :, None] * att[:, :, None, :], axis=1)).astype(jnp.bfloat16).reshape(TOK_DEV, ATT_EXP * width)
        return jnp.dot(mixed, out_mat, preferred_element_type=jnp.float32).astype(jnp.bfloat16)
    blocks = lax.map(one_device, jnp.arange(N_SEQ, dtype=jnp.int32))
    return blocks.reshape(TOKENS, D)
```

```python
import functools

import jax
import jax.numpy as jnp
import ml_dtypes
import numpy as np
from jax import lax
from jax.experimental import pallas as pl
from jax.experimental.pallas import tpu as pltpu
from jax.sharding import PartitionSpec as P

HD = 128
GROUP = 4
EPSILON = 1e-05
THETA = 10000.0
LOG2E = 1.4426950408889634
MESH = pl.DeviceIdType.MESH
ANY = pl.BlockSpec(memory_space=pl.ANY)


def remote(src, dst, send_sem, recv_sem, device):
    return pltpu.make_async_remote_copy(
        src_ref=src,
        dst_ref=dst,
        send_sem=send_sem,
        recv_sem=recv_sem,
        device_id=device,
        device_id_type=MESH,
    )


def fused_kernel(
    n_seq, n_tp, slots, merged,
    owner_ref, lengths_ref, w_query, w_keyval, pool, hid, w_out, gain, table, route_idx, route_gate, out,
    w_all, pre_all, pre_own, hid_all, meta, meta_all, w_outs, gathered, spread, staged, landed,
    local_sem, w_send, w_recv, p_send, p_recv, h_send, h_recv, m_send, m_recv, t_send, t_recv,
    x_send, x_recv, a_send, a_recv, o_send, o_recv, o_local,
):
    groups = n_seq // GROUP
    seq = lax.axis_index("seq")
    tp = lax.axis_index("tp")
    group = seq // GROUP
    base = group * GROUP
    rank = seq % GROUP
    count, width = hid_all.shape[2:]
    experts = w_query.shape[0]
    chunks, _, wide = w_outs.shape
    places = landed.shape[0]
    cuts = chunks // groups

    def lanes(index):
        return pl.ds(pl.multiple_of(index * HD, HD), HD)

    tokens = lax.broadcasted_iota(jnp.int32, (1, count), 1)
    segment = jnp.zeros((1, count), jnp.int32)
    position = tokens
    end = 0
    for j in range(lengths_ref.shape[1]):
        length = lengths_ref[0, j]
        end = end + length
        past = tokens >= end
        segment = segment + jnp.where(past, 1, 0)
        position = position - jnp.where(past, length, 0)
    meta[0:slots] = route_idx[...].astype(jnp.float32)
    meta[slots : 2 * slots] = route_gate[...]
    meta[4:5] = position.astype(jnp.float32)
    meta[5:6] = segment.astype(jnp.float32)
    meta[6:8] = jnp.zeros((2, count), jnp.float32)

    def member(step):
        return ((group + step // GROUP) % groups) * GROUP + (rank + step % GROUP) % GROUP

    def peer(step):
        return (rank + step) % GROUP

    barrier = pltpu.get_barrier_semaphore()

    def greet(step, carry):
        pl.semaphore_signal(barrier, inc=1, device_id=(member(step), tp), device_id_type=MESH)
        return carry

    lax.fori_loop(1, n_seq, greet, 0)
    for step in range(GROUP):
        for turn in range(1, n_tp):
            pl.semaphore_signal(
                barrier, inc=1, device_id=(base + peer(step), (tp + turn) % n_tp), device_id_type=MESH
            )
    pl.semaphore_wait(barrier, n_seq - 1 + GROUP * (n_tp - 1))

    def hid_copy(step):
        return remote(hid, hid_all.at[tp, rank], h_send.at[step], h_recv.at[rank], (base + peer(step), tp))

    def meta_copy(step):
        return remote(meta, meta_all.at[rank], m_send.at[step], m_recv.at[rank], (base + peer(step), tp))

    beside = rank + 1 - 2 * (rank % 2)
    across = (rank + 2) % GROUP
    owner = owner_ref[group]

    def pool_copy(step):
        if step == 0:
            head, place, partner = beside, 0, beside
        elif step == 1:
            head, place, partner = (beside + 2) % GROUP, 1, beside
        else:
            return remote(
                pre_all.at[3], pre_all.at[2], p_send.at[2], p_recv.at[2], (base + across, tp)
            )
        return remote(
            pool.at[:, :, lanes(head)], pre_all.at[place], p_send.at[step], p_recv.at[step], (base + partner, tp)
        )

    def w_part(part, head, place):
        if part == 0:
            return w_query.at[:, :, lanes(head)], w_all.at[place, 0:experts]
        return w_keyval.at[:, :, lanes(head)], w_all.at[place, experts : experts + 2]

    def w_copy(part, step):
        dest = member(step)
        src, dst = w_part(part, dest % GROUP, seq)
        return remote(src, dst, w_send.at[part, step], w_recv.at[part, seq], (dest, tp))

    def tp_copy(block, src, back, step):
        return remote(
            src, hid_all.at[tp, block], t_send.at[back, step], t_recv.at[tp, back], (seq, (tp + step) % n_tp)
        )

    def out_map_copy(step, cut):
        dest = ((group + step) % groups) * GROUP + rank
        chunk = group * cuts + cut
        return remote(
            w_out.at[:, cut * wide : (cut + 1) * wide], w_outs.at[chunk],
            x_send.at[step * cuts + cut], x_recv.at[chunk], (dest, tp),
        )

    def w_start(step, carry):
        for part in range(2):
            w_copy(part, step).start()
        return carry

    def w_wait(step, carry):
        source = member(step)
        for part in range(2):
            src, dst = w_part(part, 0, source)
            remote(src, dst, w_send.at[part, step], w_recv.at[part, source], (source, tp)).wait_recv()
        return carry

    for step in range(1, GROUP):
        hid_copy(step).start()
    for step in range(1, n_tp):
        tp_copy(rank, hid, 0, step).start()
    for step in range(1, GROUP):
        meta_copy(step).start()
    for step in (1, 0):
        pool_copy(step).start()
    lax.fori_loop(GROUP, n_seq, w_start, 0)
    lax.fori_loop(1, GROUP, w_start, 0)
    own = [
        pltpu.make_async_copy(hid, hid_all.at[tp, rank], local_sem.at[0]),
        pltpu.make_async_copy(meta, meta_all.at[rank], local_sem.at[1]),
        pltpu.make_async_copy(*w_part(0, rank, seq), local_sem.at[2]),
        pltpu.make_async_copy(*w_part(1, rank, seq), local_sem.at[3]),
        pltpu.make_async_copy(pool.at[:, :, lanes(rank)], pre_own.at[0], local_sem.at[4]),
        pltpu.make_async_copy(pool.at[:, :, lanes(across)], pre_own.at[1], local_sem.at[5 + cuts]),
    ]
    if merged:
        own.append(pltpu.make_async_copy(w_out, w_outs, local_sem.at[5]))
    else:
        for cut in range(cuts):
            own.append(
                pltpu.make_async_copy(
                    w_out.at[:, cut * wide : (cut + 1) * wide],
                    w_outs.at[group * cuts + cut],
                    local_sem.at[5 + cut],
                )
            )
    for copy in own:
        copy.start()

    for back in range(1, GROUP):
        source = (rank + GROUP - back) % GROUP
        remote(hid, hid_all.at[tp, source], h_send.at[back], h_recv.at[source], (base + source, tp)).wait_recv()
        for step in range(1, n_tp):
            tp_copy(source, hid_all.at[tp, source], back, step).start()

    for copy in own:
        copy.wait()
    pool_copy(0).wait_recv()
    pool_copy(1).wait_recv()
    pre_all[3] = jnp.where(owner == rank, pre_own[1], pre_all[1])
    pool_copy(2).start()
    near_owner = jnp.where(owner == rank, pre_own[0], pre_all[0])
    pre_own[0] = near_owner
    lax.fori_loop(GROUP, n_seq, w_wait, 0)
    if not merged:
        for cut in range(cuts):
            for step in range(1, groups):
                out_map_copy(step, cut).start()
    for step in range(1, GROUP):
        source = peer(step)
        from_peer = (base + source, tp)
        remote(meta, meta_all.at[source], m_send.at[step], m_recv.at[source], from_peer).wait_recv()
    for back in range(GROUP):
        block = (rank + GROUP - back) % GROUP
        for step in range(1, n_tp):
            source = (tp + step) % n_tp
            remote(
                hid, hid_all.at[source, block], t_send.at[back, step], t_recv.at[source, back], (seq, source)
            ).wait_recv()
    lax.fori_loop(1, GROUP, w_wait, 0)
    pool_copy(2).wait_recv()
    pre_own[0] = jnp.where(owner // 2 == rank // 2, pre_own[0], pre_all[2])

    def att_copy(b, step):
        return remote(
            gathered.at[rank, b], gathered.at[rank, b], a_send.at[b, step], a_recv.at[rank, b],
            (base + peer(step), tp),
        )

    share = n_seq // n_tp
    contract = (((1,), (1,)), ((), ()))
    factor = LOG2E * HD ** (-0.5)

    def attend(b, carry):
        rows = [hid_all[t, b].astype(jnp.float32) for t in range(n_tp)]
        squares = sum(jnp.sum(x * x, axis=1, keepdims=True) for x in rows)
        inverse = lax.rsqrt(squares * (1.0 / (n_tp * width)) + EPSILON)
        acc = None
        for t in range(n_tp):
            normed = (rows[t] * inverse * gain[t]).astype(jnp.bfloat16)
            piece = jnp.concatenate(
                [w_all[t * share : (t + 1) * share, e].reshape(width, HD) for e in range(experts + 2)], axis=1
            )
            part = jnp.dot(normed, piece, preferred_element_type=jnp.float32)
            acc = part if acc is None else acc + part
        row = meta_all[b]
        col = row.T
        first = lax.broadcasted_iota(jnp.int32, (count, count), 0)
        second = lax.broadcasted_iota(jnp.int32, (count, count), 1)
        hot = (col[:, 4:5] == second.astype(jnp.float32)).astype(jnp.bfloat16)
        looked = jnp.dot(hot, table[...], preferred_element_type=jnp.float32)
        looked = looked[:, : 2 * HD] + looked[:, 2 * HD : 4 * HD] + looked[:, 4 * HD :]
        cos = looked[:, :HD]
        sin = looked[:, HD:]

        def rotate(value):
            return value * cos + pltpu.roll(value, HD // 2, 1) * sin

        new_key = rotate(acc[:, experts * HD : (experts + 1) * HD]).astype(jnp.bfloat16)
        new_value = acc[:, (experts + 1) * HD :].astype(jnp.bfloat16)
        seen = (col[:, 5:6] == row[5:6, :]) & (second <= first)
        for k in range(slots):
            index = col[:, k : k + 1]
            chosen = jnp.zeros((count, HD), jnp.float32)
            for e in range(experts):
                chosen = jnp.where(index == float(e), acc[:, e * HD : (e + 1) * HD], chosen)
            query = rotate(chosen).astype(jnp.bfloat16)
            far = lax.dot_general(query, pre_own[0, 0], contract, preferred_element_type=jnp.float32)
            near = lax.dot_general(query, new_key, contract, preferred_element_type=jnp.float32)
            near = jnp.where(seen, near, -1e30)
            top = jnp.maximum(jnp.max(far, axis=1, keepdims=True), jnp.max(near, axis=1, keepdims=True))
            far = jnp.exp2((far - top) * factor)
            near = jnp.where(seen, jnp.exp2((near - top) * factor), 0.0)
            total = jnp.sum(far, axis=1, keepdims=True) + jnp.sum(near, axis=1, keepdims=True)
            numer = jnp.dot(far.astype(jnp.bfloat16), pre_own[0, 1], preferred_element_type=jnp.float32)
            numer += jnp.dot(near.astype(jnp.bfloat16), new_value, preferred_element_type=jnp.float32)
            gathered[rank, b, k] = (numer * (col[:, slots + k : slots + k + 1] / total)).astype(jnp.bfloat16)
        for step in range(1, GROUP):
            att_copy(b, step).start()
        return carry

    lax.fori_loop(0, GROUP, attend, 0)

    def target(c):
        if merged:
            return c, rank
        feature = (c // cuts) * GROUP + rank
        return feature // groups, (feature % groups) * cuts + c % cuts

    def out_copy(b, c):
        column, place = target(c)
        return remote(
            staged.at[b, c], landed.at[place, tp], o_send.at[b, c], o_recv.at[place, tp], (base + b, column)
        )

    def own_copy(b, c):
        column, place = target(c)
        return pltpu.make_async_copy(staged.at[b, c], landed.at[place, tp], o_local.at[c])

    def is_own(b, c):
        return (b == rank) & (target(c)[0] == tp)

    def expand(i, carry):
        b = (rank + 1 + i) % GROUP
        for step in range(1, GROUP):
            source = peer(step)
            remote(
                gathered.at[rank, b], gathered.at[source, b], a_send.at[b, step], a_recv.at[source, b],
                (base + source, tp),
            ).wait_recv()
        col = meta_all[b].T
        depth = GROUP * HD
        for e in range(experts):
            hot = [(col[:, k : k + 1] == float(e)).astype(jnp.bfloat16) for k in range(slots)]
            for s in range(GROUP):
                spread[b, :, e * depth + s * HD : e * depth + (s + 1) * HD] = sum(
                    gathered[s, b, k] * hot[k] for k in range(slots)
                )
        return carry

    lax.fori_loop(0, GROUP, expand, 0)

    for j in range(chunks):
        c = j if merged else (group * cuts + j) % chunks
        if not merged and j >= cuts:
            remote(
                w_out.at[:, 0:wide], w_outs.at[c], x_send.at[0], x_recv.at[c], ((c // cuts) * GROUP + rank, tp)
            ).wait_recv()

        def project(i, carry):
            b = (rank + 1 + i) % GROUP
            staged[b, c] = jnp.dot(spread[b], w_outs[c], preferred_element_type=jnp.float32).astype(
                staged.dtype
            )

            @pl.when(is_own(b, c))
            def _():
                own_copy(b, c).start()

            @pl.when(jnp.logical_not(is_own(b, c)))
            def _():
                out_copy(b, c).start()

            return carry

        lax.fori_loop(0, GROUP, project, 0)

    for step in range(1, GROUP):
        hid_copy(step).wait_send()
        meta_copy(step).wait_send()
        for b in range(GROUP):
            att_copy(b, step).wait_send()

    for step in range(3):
        pool_copy(step).wait_send()

    def w_sent(step, carry):
        for part in range(2):
            w_copy(part, step).wait_send()
        return carry

    lax.fori_loop(1, n_seq, w_sent, 0)
    for back in range(GROUP):
        for step in range(1, n_tp):
            tp_copy((rank + GROUP - back) % GROUP, hid, back, step).wait_send()
    if not merged:
        for cut in range(cuts):
            for step in range(1, groups):
                out_map_copy(step, cut).wait_send()

    for place in range(places):
        if merged:
            source_rank, chunk = place, tp
        else:
            feature = tp * groups + place // cuts
            source_rank, chunk = feature % GROUP, (feature // GROUP) * cuts + place % cuts
        total = None
        for t in range(n_tp):
            mine = (source_rank == rank) & (tp == t)

            @pl.when(mine)
            def _():
                pltpu.make_async_copy(
                    staged.at[rank, chunk], landed.at[place, t], o_local.at[chunk]
                ).wait()

            @pl.when(jnp.logical_not(mine))
            def _():
                remote(
                    staged.at[0, 0], landed.at[place, t], o_send.at[0, 0], o_recv.at[place, t],
                    (base + source_rank, t),
                ).wait_recv()

            value = landed[place, t].astype(jnp.float32)
            total = value if total is None else total + value
        out[:, place * wide : (place + 1) * wide] = total.astype(out.dtype)

    for b in range(GROUP):
        for c in range(chunks):

            @pl.when(jnp.logical_not(is_own(b, c)))
            def _():
                out_copy(b, c).wait_send()


def fused(
    n_seq, n_tp, merged, owner, lengths, w_query, w_keyval, pool, hid, w_out, gain, table, route_idx, route_gate
):
    groups = n_seq // GROUP
    count = hid.shape[0]
    slots = route_idx.shape[0]
    experts, rows, _ = w_query.shape
    depth = w_out.shape[-2]
    dma = pltpu.SemaphoreType.DMA
    vmem = pl.BlockSpec(memory_space=pltpu.VMEM)
    smem = pl.BlockSpec(memory_space=pltpu.SMEM)
    wide = HD
    cuts = 1 if merged else w_out.shape[1] // wide
    chunks = w_out.shape[0] if merged else groups * cuts
    places = GROUP if merged else groups * cuts
    return pl.pallas_call(
        functools.partial(fused_kernel, n_seq, n_tp, slots, merged),
        out_shape=jax.ShapeDtypeStruct((count, places * wide), jnp.bfloat16),
        in_specs=[smem] * 2 + [ANY] * 5 + [vmem] * 4,
        out_specs=vmem,
        scratch_shapes=[
            pltpu.VMEM((n_seq, experts + 2, rows, HD), w_query.dtype),
            pltpu.VMEM((4, 2, pool.shape[1], HD), pool.dtype),
            pltpu.VMEM((2, 2, pool.shape[1], HD), pool.dtype),
            pltpu.VMEM((n_tp, GROUP) + hid.shape, hid.dtype),
            pltpu.VMEM((8, count), jnp.float32),
            pltpu.VMEM((GROUP, 8, count), jnp.float32),
            pltpu.VMEM((chunks, depth, wide), w_out.dtype),
            pltpu.VMEM((GROUP, GROUP, slots, count, HD), jnp.bfloat16),
            pltpu.VMEM((GROUP, count, depth), jnp.bfloat16),
            pltpu.VMEM((GROUP, chunks, count, wide), jnp.bfloat16),
            pltpu.VMEM((places, n_tp, count, wide), jnp.bfloat16),
            dma((6 + cuts,)),
            dma((2, n_seq)),
            dma((2, n_seq)),
            dma((GROUP,)),
            dma((GROUP,)),
            dma((GROUP,)),
            dma((GROUP,)),
            dma((GROUP,)),
            dma((GROUP,)),
            dma((GROUP, n_tp)),
            dma((n_tp, GROUP)),
            dma((groups * cuts,)),
            dma((chunks,)),
            dma((GROUP, GROUP)),
            dma((GROUP, GROUP)),
            dma((GROUP, chunks)),
            dma((places, n_tp)),
            dma((chunks,)),
        ],
        compiler_params=pltpu.CompilerParams(
            collective_id=0, has_side_effects=True, vmem_limit_bytes=48 << 20
        ),
        name="fused",
    )(owner, lengths, w_query, w_keyval, pool, hid, w_out, gain, table, route_idx, route_gate)


def paired_kernel(
    n_seq, n_tp, slots,
    owner_ref, lengths_ref, w_query, w_keyval, pool, hid, w_out, gain, table, route_idx, route_gate, out,
    w_all, pre_all, pre_own, hid_all, meta, meta_all, w_outs, att, spread, kept, y_out, y_in, r_out, r_in, f_out, f_in,
    local_sem, w_send, w_recv, p_send, p_recv, h_send, h_recv, m_send, m_recv, t_send, t_recv,
    x_send, x_recv, a_send, a_recv, k_send, k_recv, y_send, y_recv, r_send, r_recv, f_send, f_recv,
):
    groups = n_seq // GROUP
    seq = lax.axis_index("seq")
    tp = lax.axis_index("tp")
    group = seq // GROUP
    base = group * GROUP
    rank = seq % GROUP
    count, width = hid_all.shape[2:]
    experts = w_query.shape[0]
    core = tp % 2
    across_y = tp // 2
    other_core = tp + 1 - 2 * core
    other_y = (tp + 2) % n_tp
    other = (base + GROUP) % n_seq
    keep = (across_y + group) % 2
    half = w_outs.shape[-1]

    def lanes(index):
        return pl.ds(pl.multiple_of(index * HD, HD), HD)

    tokens = lax.broadcasted_iota(jnp.int32, (1, count), 1)
    segment = jnp.zeros((1, count), jnp.int32)
    position = tokens
    end = 0
    for j in range(lengths_ref.shape[1]):
        length = lengths_ref[0, j]
        end = end + length
        past = tokens >= end
        segment = segment + jnp.where(past, 1, 0)
        position = position - jnp.where(past, length, 0)
    meta[0:slots] = route_idx[...].astype(jnp.float32)
    meta[slots : 2 * slots] = route_gate[...]
    meta[4:5] = position.astype(jnp.float32)
    meta[5:6] = segment.astype(jnp.float32)
    meta[6:8] = jnp.zeros((2, count), jnp.float32)

    def member(step):
        return ((group + step // GROUP) % groups) * GROUP + (rank + step % GROUP) % GROUP

    def peer(step):
        return (rank + step) % GROUP

    barrier = pltpu.get_barrier_semaphore()

    def greet(step, carry):
        pl.semaphore_signal(barrier, inc=1, device_id=(member(step), tp), device_id_type=MESH)
        return carry

    lax.fori_loop(1, n_seq, greet, 0)
    for step in range(GROUP):
        for turn in range(1, n_tp):
            pl.semaphore_signal(
                barrier, inc=1, device_id=(base + peer(step), (tp + turn) % n_tp), device_id_type=MESH
            )
    pl.semaphore_signal(barrier, inc=1, device_id=(other + rank, other_y), device_id_type=MESH)
    pl.semaphore_wait(barrier, n_seq + GROUP * (n_tp - 1))

    def hid_copy(step):
        return remote(hid, hid_all.at[tp, rank], h_send.at[step], h_recv.at[rank], (base + peer(step), tp))

    def meta_copy(step):
        return remote(meta, meta_all.at[seq], m_send.at[step], m_recv.at[seq], (member(step), tp))

    beside = rank + 1 - 2 * (rank % 2)
    across = (rank + 2) % GROUP
    owner = owner_ref[group]

    def pool_copy(step):
        if step == 0:
            head, place, partner = beside, 0, beside
        elif step == 1:
            head, place, partner = (beside + 2) % GROUP, 1, beside
        else:
            return remote(
                pre_all.at[3], pre_all.at[2], p_send.at[2], p_recv.at[2], (base + across, tp)
            )
        return remote(
            pool.at[:, :, lanes(head)], pre_all.at[place], p_send.at[step], p_recv.at[step], (base + partner, tp)
        )

    def w_part(part, head, place):
        if part == 0:
            return w_query.at[:, :, lanes(head)], w_all.at[place, 0:experts]
        return w_keyval.at[:, :, lanes(head)], w_all.at[place, experts : experts + 2]

    def w_copy(part, step):
        dest = member(step)
        src, dst = w_part(part, dest % GROUP, seq)
        return remote(src, dst, w_send.at[part, step], w_recv.at[part, seq], (dest, tp))

    def tp_copy(block, src, back, step):
        return remote(
            src, hid_all.at[tp, block], t_send.at[back, step], t_recv.at[tp, back], (seq, (tp + step) % n_tp)
        )

    def out_map_copy(step):
        return remote(
            w_out.at[:, lanes(peer(step))], w_outs.at[rank % 2, core], x_send.at[step], x_recv.at[rank % 2, core],
            (base + peer(step), 2 * across_y + rank // 2),
        )

    def own_map_copy():
        return pltpu.make_async_copy(w_out.at[:, lanes(rank)], w_outs.at[rank % 2, core], local_sem.at[5])

    def w_start(step, carry):
        for part in range(2):
            w_copy(part, step).start()
        return carry

    def w_wait(step, carry):
        source = member(step)
        for part in range(2):
            src, dst = w_part(part, 0, source)
            remote(src, dst, w_send.at[part, step], w_recv.at[part, source], (source, tp)).wait_recv()
        return carry

    for step in range(1, GROUP):
        hid_copy(step).start()
    for step in range(1, n_tp):
        tp_copy(rank, hid, 0, step).start()
    for step in range(1, n_seq):
        meta_copy(step).start()
    for step in (1, 0):
        pool_copy(step).start()
    lax.fori_loop(GROUP, n_seq, w_start, 0)
    lax.fori_loop(1, GROUP, w_start, 0)
    own = [
        pltpu.make_async_copy(hid, hid_all.at[tp, rank], local_sem.at[0]),
        pltpu.make_async_copy(meta, meta_all.at[seq], local_sem.at[1]),
        pltpu.make_async_copy(*w_part(0, rank, seq), local_sem.at[2]),
        pltpu.make_async_copy(*w_part(1, rank, seq), local_sem.at[3]),
        pltpu.make_async_copy(pool.at[:, :, lanes(rank)], pre_own.at[0], local_sem.at[4]),
        pltpu.make_async_copy(pool.at[:, :, lanes(across)], pre_own.at[1], local_sem.at[6]),
    ]
    for copy in own:
        copy.start()
    for step in range(1, GROUP):
        out_map_copy(step).start()

    @pl.when(rank // 2 == core)
    def _():
        own_map_copy().start()

    @pl.when(rank // 2 != core)
    def _():
        out_map_copy(0).start()

    for back in range(1, GROUP):
        source = (rank + GROUP - back) % GROUP
        remote(hid, hid_all.at[tp, source], h_send.at[back], h_recv.at[source], (base + source, tp)).wait_recv()
        for step in range(1, n_tp):
            tp_copy(source, hid_all.at[tp, source], back, step).start()

    for copy in own:
        copy.wait()
    pool_copy(0).wait_recv()
    pool_copy(1).wait_recv()
    pre_all[3] = jnp.where(owner == rank, pre_own[1], pre_all[1])
    pool_copy(2).start()
    near_owner = jnp.where(owner == rank, pre_own[0], pre_all[0])
    pre_own[0] = near_owner
    lax.fori_loop(GROUP, n_seq, w_wait, 0)
    for step in range(1, n_seq):
        source = member(step)
        remote(meta, meta_all.at[source], m_send.at[step], m_recv.at[source], (source, tp)).wait_recv()
    for back in range(GROUP):
        block = (rank + GROUP - back) % GROUP
        for step in range(1, n_tp):
            source = (tp + step) % n_tp
            remote(
                hid, hid_all.at[source, block], t_send.at[back, step], t_recv.at[source, back], (seq, source)
            ).wait_recv()
    lax.fori_loop(1, GROUP, w_wait, 0)
    pool_copy(2).wait_recv()
    pre_own[0] = jnp.where(owner // 2 == rank // 2, pre_own[0], pre_all[2])

    def cross_copy(b):
        return remote(att.at[core, 0, b], att.at[core, 1, b], a_send.at[b], a_recv.at[b], (other + rank, tp))

    def core_copy(side, b):
        return remote(
            att.at[core, side, b], att.at[core, side, b], k_send.at[side, b], k_recv.at[side, b], (seq, other_core)
        )

    def core_wait(side, b):
        remote(
            att.at[core, side, b], att.at[1 - core, side, b], k_send.at[side, b], k_recv.at[side, b],
            (seq, other_core),
        ).wait_recv()

    share = n_seq // n_tp
    contract = (((1,), (1,)), ((), ()))
    factor = LOG2E * HD ** (-0.5)

    def attend(i, carry):
        b = (rank + 1 + i) % GROUP
        rows = [hid_all[t, b].astype(jnp.float32) for t in range(n_tp)]
        squares = sum(jnp.sum(x * x, axis=1, keepdims=True) for x in rows)
        inverse = lax.rsqrt(squares * (1.0 / (n_tp * width)) + EPSILON)
        acc = None
        for t in range(n_tp):
            normed = (rows[t] * inverse * gain[t]).astype(jnp.bfloat16)
            piece = jnp.concatenate(
                [w_all[t * share : (t + 1) * share, e].reshape(width, HD) for e in range(experts + 2)], axis=1
            )
            part = jnp.dot(normed, piece, preferred_element_type=jnp.float32)
            acc = part if acc is None else acc + part
        row = meta_all[base + b]
        col = row.T
        first = lax.broadcasted_iota(jnp.int32, (count, count), 0)
        second = lax.broadcasted_iota(jnp.int32, (count, count), 1)
        hot = (col[:, 4:5] == second.astype(jnp.float32)).astype(jnp.bfloat16)
        looked = jnp.dot(hot, table[...], preferred_element_type=jnp.float32)
        looked = looked[:, : 2 * HD] + looked[:, 2 * HD : 4 * HD] + looked[:, 4 * HD :]
        cos = looked[:, :HD]
        sin = looked[:, HD:]

        def rotate(value):
            return value * cos + pltpu.roll(value, HD // 2, 1) * sin

        new_key = rotate(acc[:, experts * HD : (experts + 1) * HD]).astype(jnp.bfloat16)
        new_value = acc[:, (experts + 1) * HD :].astype(jnp.bfloat16)
        seen = (col[:, 5:6] == row[5:6, :]) & (second <= first)
        for k in range(slots):
            index = col[:, k : k + 1]
            chosen = jnp.zeros((count, HD), jnp.float32)
            for e in range(experts):
                chosen = jnp.where(index == float(e), acc[:, e * HD : (e + 1) * HD], chosen)
            query = rotate(chosen).astype(jnp.bfloat16)
            far = lax.dot_general(query, pre_own[0, 0], contract, preferred_element_type=jnp.float32)
            near = lax.dot_general(query, new_key, contract, preferred_element_type=jnp.float32)
            near = jnp.where(seen, near, -1e30)
            top = jnp.maximum(jnp.max(far, axis=1, keepdims=True), jnp.max(near, axis=1, keepdims=True))
            far = jnp.exp2((far - top) * factor)
            near = jnp.where(seen, jnp.exp2((near - top) * factor), 0.0)
            total = jnp.sum(far, axis=1, keepdims=True) + jnp.sum(near, axis=1, keepdims=True)
            numer = jnp.dot(far.astype(jnp.bfloat16), pre_own[0, 1], preferred_element_type=jnp.float32)
            numer += jnp.dot(near.astype(jnp.bfloat16), new_value, preferred_element_type=jnp.float32)
            att[core, 0, b, k] = (numer * (col[:, slots + k : slots + k + 1] / total)).astype(jnp.bfloat16)
        cross_copy(b).start()
        core_copy(0, b).start()
        return carry

    lax.fori_loop(0, GROUP, attend, 0)

    for place in range(2):
        for source_core in range(2):
            from_rank = 2 * core + place
            mine = (from_rank == rank) & (source_core == core)

            @pl.when(mine)
            def _():
                own_map_copy().wait()

            @pl.when(jnp.logical_not(mine))
            def _():
                remote(
                    w_out.at[:, lanes(rank)], w_outs.at[place, source_core], x_send.at[0],
                    x_recv.at[place, source_core], (base + from_rank, 2 * across_y + source_core),
                ).wait_recv()

    def y_copy(b):
        return remote(y_out.at[b], y_in.at[b], y_send.at[b], y_recv.at[b], (seq, other_y))

    def r_copy(b):
        return remote(r_out.at[b], r_in.at[rank], r_send.at[b], r_recv.at[rank], (base + b, tp))

    def f_copy():
        return remote(f_out, f_in, f_send.at[0], f_recv.at[0], (other + rank, other_y))

    def project(side, b):
        col = meta_all[b + (base if side == 0 else other)].T
        depth = experts * HD
        for e in range(experts):
            hot = [(col[:, k : k + 1] == float(e)).astype(jnp.bfloat16) for k in range(slots)]
            for s in range(2):
                spread[side, :, s * depth + e * HD : s * depth + (e + 1) * HD] = sum(
                    att[s, side, b, k] * hot[k] for k in range(slots)
                )
        for place in range(2):
            part = jnp.dot(
                spread[side], w_outs[place].reshape(2 * depth, half), preferred_element_type=jnp.float32
            )

            @pl.when(keep == side)
            def _():
                kept[b, :, place * half : (place + 1) * half] = part

            @pl.when(keep != side)
            def _():
                y_out[b, :, place * half : (place + 1) * half] = part.astype(y_out.dtype)

        @pl.when(keep != side)
        def _():
            y_copy(b).start()

    def reduce(b):
        y_copy(b).wait_recv()
        return kept[b] + y_in[b].astype(jnp.float32)

    def near(i, carry):
        b = (rank + 1 + i) % GROUP
        core_wait(0, b)
        project(0, b)
        return carry

    lax.fori_loop(0, GROUP, near, 0)

    def scatter(i):
        b = (rank + 1 + i) % GROUP
        r_out[b] = reduce(b).astype(r_out.dtype)
        r_copy(b).start()

    def far(i, carry):
        b = (rank + 1 + i) % GROUP
        cross_copy(b).wait_recv()
        core_copy(1, b).start()
        core_wait(1, b)
        project(1, b)

        @pl.when(i > 0)
        def _():
            scatter(i - 1)

        return carry

    lax.fori_loop(0, GROUP, far, 0)

    total = reduce(rank)
    for step in range(1, GROUP):
        source = peer(step)
        remote(r_out.at[rank], r_in.at[source], r_send.at[rank], r_recv.at[source], (base + source, tp)).wait_recv()
        total = total + r_in[source].astype(jnp.float32)

    @pl.when(keep == 0)
    def _():
        out[...] = total.astype(out.dtype)

    @pl.when(keep == 1)
    def _():
        f_out[...] = total.astype(f_out.dtype)
        f_copy().start()

    for step in range(1, GROUP):
        hid_copy(step).wait_send()
        r_copy(peer(step)).wait_send()
        out_map_copy(step).wait_send()
    for step in range(1, n_seq):
        meta_copy(step).wait_send()

    @pl.when(rank // 2 != core)
    def _():
        out_map_copy(0).wait_send()

    for b in range(GROUP):
        cross_copy(b).wait_send()
        core_copy(0, b).wait_send()
        core_copy(1, b).wait_send()
        y_copy(b).wait_send()

    for step in range(3):
        pool_copy(step).wait_send()

    def w_sent(step, carry):
        for part in range(2):
            w_copy(part, step).wait_send()
        return carry

    lax.fori_loop(1, n_seq, w_sent, 0)
    for back in range(GROUP):
        for step in range(1, n_tp):
            tp_copy((rank + GROUP - back) % GROUP, hid, back, step).wait_send()

    @pl.when(keep == 1)
    def _():
        f_copy().wait_recv()
        out[...] = f_in[...]
        f_copy().wait_send()


def paired(n_seq, n_tp, owner, lengths, w_query, w_keyval, pool, hid, w_out, gain, table, route_idx, route_gate):
    count, width = hid.shape
    slots = route_idx.shape[0]
    experts, rows, _ = w_query.shape
    half = w_out.shape[-1]
    dma = pltpu.SemaphoreType.DMA
    vmem = pl.BlockSpec(memory_space=pltpu.VMEM)
    smem = pl.BlockSpec(memory_space=pltpu.SMEM)
    low = jnp.bfloat16
    return pl.pallas_call(
        functools.partial(paired_kernel, n_seq, n_tp, slots),
        out_shape=jax.ShapeDtypeStruct((count, width), low),
        in_specs=[smem] * 2 + [ANY] * 5 + [vmem] * 4,
        out_specs=vmem,
        scratch_shapes=[
            pltpu.VMEM((n_seq, experts + 2, rows, HD), w_query.dtype),
            pltpu.VMEM((4, 2, pool.shape[1], HD), pool.dtype),
            pltpu.VMEM((2, 2, pool.shape[1], HD), pool.dtype),
            pltpu.VMEM((n_tp, GROUP) + hid.shape, hid.dtype),
            pltpu.VMEM((8, count), jnp.float32),
            pltpu.VMEM((n_seq, 8, count), jnp.float32),
            pltpu.VMEM((2, 2, experts, HD, half), w_out.dtype),
            pltpu.VMEM((2, 2, GROUP, slots, count, HD), low),
            pltpu.VMEM((2, count, 2 * experts * HD), low),
            pltpu.VMEM((GROUP, count, width), jnp.float32),
            pltpu.VMEM((GROUP, count, width), low),
            pltpu.VMEM((GROUP, count, width), low),
            pltpu.VMEM((GROUP, count, width), low),
            pltpu.VMEM((GROUP, count, width), low),
            pltpu.VMEM((count, width), low),
            pltpu.VMEM((count, width), low),
            dma((7,)),
            dma((2, n_seq)),
            dma((2, n_seq)),
            dma((GROUP,)),
            dma((GROUP,)),
            dma((GROUP,)),
            dma((GROUP,)),
            dma((n_seq,)),
            dma((n_seq,)),
            dma((GROUP, n_tp)),
            dma((n_tp, GROUP)),
            dma((GROUP,)),
            dma((2, 2)),
            dma((GROUP,)),
            dma((GROUP,)),
            dma((2, GROUP)),
            dma((2, GROUP)),
            dma((GROUP,)),
            dma((GROUP,)),
            dma((GROUP,)),
            dma((GROUP,)),
            dma((1,)),
            dma((1,)),
        ],
        compiler_params=pltpu.CompilerParams(
            collective_id=0, has_side_effects=True, vmem_limit_bytes=48 << 20
        ),
        name="paired",
    )(owner, lengths, w_query, w_keyval, pool, hid, w_out, gain, table, route_idx, route_gate)


def rope_table(count, prefix):
    freqs = np.float32(THETA) ** (-(np.arange(HD // 2, dtype=np.float32) * np.float32(2.0)) / np.float32(HD))
    angles = (np.arange(count) + prefix).astype(np.float32)[:, None] * freqs[None, :].astype(np.float32)
    cosine = np.cos(angles.astype(np.float64))
    sine = np.sin(angles.astype(np.float64))
    rest = np.concatenate([cosine, cosine, -sine, sine], axis=1).astype(np.float32)
    parts = []
    for _ in range(3):
        part = rest.astype(ml_dtypes.bfloat16)
        parts.append(part)
        rest = rest - part.astype(np.float32)
    return np.concatenate(parts, axis=1)


def per_device(
    n_seq, n_tp, hidden, lengths, cache_owner, cache_pool, norm_gain, route_idx, route_gate,
    w_query, w_keyval, w_out,
):
    groups = n_seq // GROUP
    count = hidden.shape[0]
    rows, experts, width = w_query.shape
    prefix = cache_pool.shape[1]
    assert width == GROUP * HD
    wide = w_out.shape[2]
    merged = wide < HD
    if n_seq == 2 * GROUP and n_tp == 4:
        return paired(
            n_seq, n_tp, cache_owner, lengths, w_query.swapaxes(0, 1), w_keyval.swapaxes(0, 1),
            cache_pool[0].swapaxes(0, 1), hidden, w_out, norm_gain.reshape(n_tp, 1, -1),
            jnp.asarray(rope_table(count, prefix)), route_idx.T, route_gate.T,
        )
    if merged:
        same_rank = [[g * GROUP + r for g in range(groups)] for r in range(GROUP)]
        per = groups // n_tp
        w_out = lax.all_gather(w_out, "seq", axis=0, axis_index_groups=same_rank)
        w_out = w_out.reshape(n_tp, per, experts, width, wide).transpose(0, 2, 3, 1, 4)
        w_out = w_out.reshape(n_tp, experts * width, per * wide)
    else:
        w_out = w_out.reshape(experts * width, wide)
    out = fused(
        n_seq, n_tp, merged, cache_owner, lengths, w_query.swapaxes(0, 1), w_keyval.swapaxes(0, 1),
        cache_pool[0].swapaxes(0, 1), hidden, w_out, norm_gain.reshape(n_tp, 1, -1),
        jnp.asarray(rope_table(count, prefix)), route_idx.T, route_gate.T,
    )
    if merged:
        out = out.reshape(count, GROUP, groups // n_tp, wide).transpose(0, 2, 1, 3).reshape(count, -1)
    return out


def solution(mesh):
    placed = (
        P("seq", "tp"),
        P("seq", None),
        P(),
        P("seq", None, None, "tp"),
        P(),
        P("seq", None),
        P("seq", None),
        P("seq", None, "tp"),
        P("seq", None, "tp"),
        P(None, "tp", "seq"),
    )
    body = functools.partial(per_device, mesh.shape["seq"], mesh.shape["tp"])
    return jax.shard_map(body, mesh=mesh, in_specs=placed, out_specs=P("seq", "tp"), check_vma=False)
```

```python
import functools

import jax
import jax.numpy as jnp
import ml_dtypes
import numpy as np
from jax import lax
from jax.experimental import pallas as pl
from jax.experimental.pallas import tpu as pltpu
from jax.sharding import PartitionSpec as P

HD = 128
GROUP = 4
EPSILON = 1e-05
THETA = 10000.0
LOG2E = 1.4426950408889634
MESH = pl.DeviceIdType.MESH
ANY = pl.BlockSpec(memory_space=pl.ANY)


def remote(src, dst, send_sem, recv_sem, device):
    return pltpu.make_async_remote_copy(
        src_ref=src,
        dst_ref=dst,
        send_sem=send_sem,
        recv_sem=recv_sem,
        device_id=device,
        device_id_type=MESH,
    )


def fused_kernel(
    n_seq, n_tp, slots, merged,
    owner_ref, lengths_ref, w_query, w_keyval, pool, hid, w_out, gain, table, route_idx, route_gate, out,
    w_all, pre_all, pre_own, hid_all, meta, meta_all, w_outs, gathered, spread, staged, landed,
    local_sem, w_send, w_recv, p_send, p_recv, h_send, h_recv, m_send, m_recv, t_send, t_recv,
    x_send, x_recv, a_send, a_recv, o_send, o_recv, o_local,
):
    groups = n_seq // GROUP
    seq = lax.axis_index("seq")
    tp = lax.axis_index("tp")
    group = seq // GROUP
    base = group * GROUP
    rank = seq % GROUP
    count, width = hid_all.shape[2:]
    experts = w_query.shape[0]
    chunks, _, wide = w_outs.shape
    places = landed.shape[0]
    cuts = chunks // groups

    def lanes(index):
        return pl.ds(pl.multiple_of(index * HD, HD), HD)

    tokens = lax.broadcasted_iota(jnp.int32, (1, count), 1)
    segment = jnp.zeros((1, count), jnp.int32)
    position = tokens
    end = 0
    for j in range(lengths_ref.shape[1]):
        length = lengths_ref[0, j]
        end = end + length
        past = tokens >= end
        segment = segment + jnp.where(past, 1, 0)
        position = position - jnp.where(past, length, 0)
    meta[0:slots] = route_idx[...].astype(jnp.float32)
    meta[slots : 2 * slots] = route_gate[...]
    meta[4:5] = position.astype(jnp.float32)
    meta[5:6] = segment.astype(jnp.float32)
    meta[6:8] = jnp.zeros((2, count), jnp.float32)

    def member(step):
        return ((group + step // GROUP) % groups) * GROUP + (rank + step % GROUP) % GROUP

    def peer(step):
        return (rank + step) % GROUP

    barrier = pltpu.get_barrier_semaphore()

    def greet(step, carry):
        pl.semaphore_signal(barrier, inc=1, device_id=(member(step), tp), device_id_type=MESH)
        return carry

    lax.fori_loop(1, n_seq, greet, 0)
    for step in range(GROUP):
        for turn in range(1, n_tp):
            pl.semaphore_signal(
                barrier, inc=1, device_id=(base + peer(step), (tp + turn) % n_tp), device_id_type=MESH
            )
    pl.semaphore_wait(barrier, n_seq - 1 + GROUP * (n_tp - 1))

    def hid_copy(step):
        return remote(hid, hid_all.at[tp, rank], h_send.at[step], h_recv.at[rank], (base + peer(step), tp))

    def meta_copy(step):
        return remote(meta, meta_all.at[rank], m_send.at[step], m_recv.at[rank], (base + peer(step), tp))

    beside = rank + 1 - 2 * (rank % 2)
    across = (rank + 2) % GROUP
    owner = owner_ref[group]

    def pool_copy(step):
        if step == 0:
            head, place, partner = beside, 0, beside
        elif step == 1:
            head, place, partner = (beside + 2) % GROUP, 1, beside
        else:
            return remote(
                pre_all.at[3], pre_all.at[2], p_send.at[2], p_recv.at[2], (base + across, tp)
            )
        return remote(
            pool.at[:, :, lanes(head)], pre_all.at[place], p_send.at[step], p_recv.at[step], (base + partner, tp)
        )

    def w_part(part, head, place):
        if part == 0:
            return w_query.at[:, :, lanes(head)], w_all.at[place, 0:experts]
        return w_keyval.at[:, :, lanes(head)], w_all.at[place, experts : experts + 2]

    def w_copy(part, step):
        dest = member(step)
        src, dst = w_part(part, dest % GROUP, seq)
        return remote(src, dst, w_send.at[part, step], w_recv.at[part, seq], (dest, tp))

    def tp_copy(block, src, back, step):
        return remote(
            src, hid_all.at[tp, block], t_send.at[back, step], t_recv.at[tp, back], (seq, (tp + step) % n_tp)
        )

    def out_map_copy(step, cut):
        dest = ((group + step) % groups) * GROUP + rank
        chunk = group * cuts + cut
        return remote(
            w_out.at[:, cut * wide : (cut + 1) * wide], w_outs.at[chunk],
            x_send.at[step * cuts + cut], x_recv.at[chunk], (dest, tp),
        )

    def w_start(step, carry):
        for part in range(2):
            w_copy(part, step).start()
        return carry

    def w_wait(step, carry):
        source = member(step)
        for part in range(2):
            src, dst = w_part(part, 0, source)
            remote(src, dst, w_send.at[part, step], w_recv.at[part, source], (source, tp)).wait_recv()
        return carry

    for step in range(1, GROUP):
        hid_copy(step).start()
    for step in range(1, n_tp):
        tp_copy(rank, hid, 0, step).start()
    for step in range(1, GROUP):
        meta_copy(step).start()
    for step in (1, 0):
        pool_copy(step).start()
    lax.fori_loop(GROUP, n_seq, w_start, 0)
    lax.fori_loop(1, GROUP, w_start, 0)
    own = [
        pltpu.make_async_copy(hid, hid_all.at[tp, rank], local_sem.at[0]),
        pltpu.make_async_copy(meta, meta_all.at[rank], local_sem.at[1]),
        pltpu.make_async_copy(*w_part(0, rank, seq), local_sem.at[2]),
        pltpu.make_async_copy(*w_part(1, rank, seq), local_sem.at[3]),
        pltpu.make_async_copy(pool.at[:, :, lanes(rank)], pre_own.at[0], local_sem.at[4]),
        pltpu.make_async_copy(pool.at[:, :, lanes(across)], pre_own.at[1], local_sem.at[5 + cuts]),
    ]
    if merged:
        own.append(pltpu.make_async_copy(w_out, w_outs, local_sem.at[5]))
    else:
        for cut in range(cuts):
            own.append(
                pltpu.make_async_copy(
                    w_out.at[:, cut * wide : (cut + 1) * wide],
                    w_outs.at[group * cuts + cut],
                    local_sem.at[5 + cut],
                )
            )
    for copy in own:
        copy.start()

    for back in range(1, GROUP):
        source = (rank + GROUP - back) % GROUP
        remote(hid, hid_all.at[tp, source], h_send.at[back], h_recv.at[source], (base + source, tp)).wait_recv()
        for step in range(1, n_tp):
            tp_copy(source, hid_all.at[tp, source], back, step).start()

    for copy in own:
        copy.wait()
    pool_copy(0).wait_recv()
    pool_copy(1).wait_recv()
    pre_all[3] = jnp.where(owner == rank, pre_own[1], pre_all[1])
    pool_copy(2).start()
    near_owner = jnp.where(owner == rank, pre_own[0], pre_all[0])
    pre_own[0] = near_owner
    lax.fori_loop(GROUP, n_seq, w_wait, 0)
    if not merged:
        for cut in range(cuts):
            for step in range(1, groups):
                out_map_copy(step, cut).start()
    for step in range(1, GROUP):
        source = peer(step)
        from_peer = (base + source, tp)
        remote(meta, meta_all.at[source], m_send.at[step], m_recv.at[source], from_peer).wait_recv()
    for back in range(GROUP):
        block = (rank + GROUP - back) % GROUP
        for step in range(1, n_tp):
            source = (tp + step) % n_tp
            remote(
                hid, hid_all.at[source, block], t_send.at[back, step], t_recv.at[source, back], (seq, source)
            ).wait_recv()
    lax.fori_loop(1, GROUP, w_wait, 0)
    pool_copy(2).wait_recv()
    pre_own[0] = jnp.where(owner // 2 == rank // 2, pre_own[0], pre_all[2])

    def att_copy(b, step):
        return remote(
            gathered.at[rank, b], gathered.at[rank, b], a_send.at[b, step], a_recv.at[rank, b],
            (base + peer(step), tp),
        )

    share = n_seq // n_tp
    contract = (((1,), (1,)), ((), ()))
    factor = LOG2E * HD ** (-0.5)

    def attend(b, carry):
        rows = [hid_all[t, b].astype(jnp.float32) for t in range(n_tp)]
        squares = sum(jnp.sum(x * x, axis=1, keepdims=True) for x in rows)
        inverse = lax.rsqrt(squares * (1.0 / (n_tp * width)) + EPSILON)
        acc = None
        for t in range(n_tp):
            normed = (rows[t] * inverse * gain[t]).astype(jnp.bfloat16)
            piece = jnp.concatenate(
                [w_all[t * share : (t + 1) * share, e].reshape(width, HD) for e in range(experts + 2)], axis=1
            )
            part = jnp.dot(normed, piece, preferred_element_type=jnp.float32)
            acc = part if acc is None else acc + part
        row = meta_all[b]
        col = row.T
        first = lax.broadcasted_iota(jnp.int32, (count, count), 0)
        second = lax.broadcasted_iota(jnp.int32, (count, count), 1)
        hot = (col[:, 4:5] == second.astype(jnp.float32)).astype(jnp.bfloat16)
        looked = jnp.dot(hot, table[...], preferred_element_type=jnp.float32)
        looked = looked[:, : 2 * HD] + looked[:, 2 * HD : 4 * HD] + looked[:, 4 * HD :]
        cos = looked[:, :HD]
        sin = looked[:, HD:]

        def rotate(value):
            return value * cos + pltpu.roll(value, HD // 2, 1) * sin

        new_key = rotate(acc[:, experts * HD : (experts + 1) * HD]).astype(jnp.bfloat16)
        new_value = acc[:, (experts + 1) * HD :].astype(jnp.bfloat16)
        seen = (col[:, 5:6] == row[5:6, :]) & (second <= first)
        for k in range(slots):
            index = col[:, k : k + 1]
            chosen = jnp.zeros((count, HD), jnp.float32)
            for e in range(experts):
                chosen = jnp.where(index == float(e), acc[:, e * HD : (e + 1) * HD], chosen)
            query = rotate(chosen).astype(jnp.bfloat16)
            far = lax.dot_general(query, pre_own[0, 0], contract, preferred_element_type=jnp.float32)
            near = lax.dot_general(query, new_key, contract, preferred_element_type=jnp.float32)
            near = jnp.where(seen, near, -1e30)
            top = jnp.maximum(jnp.max(far, axis=1, keepdims=True), jnp.max(near, axis=1, keepdims=True))
            far = jnp.exp2((far - top) * factor)
            near = jnp.where(seen, jnp.exp2((near - top) * factor), 0.0)
            total = jnp.sum(far, axis=1, keepdims=True) + jnp.sum(near, axis=1, keepdims=True)
            numer = jnp.dot(far.astype(jnp.bfloat16), pre_own[0, 1], preferred_element_type=jnp.float32)
            numer += jnp.dot(near.astype(jnp.bfloat16), new_value, preferred_element_type=jnp.float32)
            gathered[rank, b, k] = (numer * (col[:, slots + k : slots + k + 1] / total)).astype(jnp.bfloat16)
        for step in range(1, GROUP):
            att_copy(b, step).start()
        return carry

    lax.fori_loop(0, GROUP, attend, 0)

    def target(c):
        if merged:
            return c, rank
        feature = (c // cuts) * GROUP + rank
        return feature // groups, (feature % groups) * cuts + c % cuts

    def out_copy(b, c):
        column, place = target(c)
        return remote(
            staged.at[b, c], landed.at[place, tp], o_send.at[b, c], o_recv.at[place, tp], (base + b, column)
        )

    def own_copy(b, c):
        column, place = target(c)
        return pltpu.make_async_copy(staged.at[b, c], landed.at[place, tp], o_local.at[c])

    def is_own(b, c):
        return (b == rank) & (target(c)[0] == tp)

    def expand(i, carry):
        b = (rank + 1 + i) % GROUP
        for step in range(1, GROUP):
            source = peer(step)
            remote(
                gathered.at[rank, b], gathered.at[source, b], a_send.at[b, step], a_recv.at[source, b],
                (base + source, tp),
            ).wait_recv()
        col = meta_all[b].T
        depth = GROUP * HD
        for e in range(experts):
            hot = [(col[:, k : k + 1] == float(e)).astype(jnp.bfloat16) for k in range(slots)]
            for s in range(GROUP):
                spread[b, :, e * depth + s * HD : e * depth + (s + 1) * HD] = sum(
                    gathered[s, b, k] * hot[k] for k in range(slots)
                )
        return carry

    lax.fori_loop(0, GROUP, expand, 0)

    for j in range(chunks):
        c = j if merged else (group * cuts + j) % chunks
        if not merged and j >= cuts:
            remote(
                w_out.at[:, 0:wide], w_outs.at[c], x_send.at[0], x_recv.at[c], ((c // cuts) * GROUP + rank, tp)
            ).wait_recv()

        def project(i, carry):
            b = (rank + 1 + i) % GROUP
            staged[b, c] = jnp.dot(spread[b], w_outs[c], preferred_element_type=jnp.float32).astype(
                staged.dtype
            )

            @pl.when(is_own(b, c))
            def _():
                own_copy(b, c).start()

            @pl.when(jnp.logical_not(is_own(b, c)))
            def _():
                out_copy(b, c).start()

            return carry

        lax.fori_loop(0, GROUP, project, 0)

    for step in range(1, GROUP):
        hid_copy(step).wait_send()
        meta_copy(step).wait_send()
        for b in range(GROUP):
            att_copy(b, step).wait_send()

    for step in range(3):
        pool_copy(step).wait_send()

    def w_sent(step, carry):
        for part in range(2):
            w_copy(part, step).wait_send()
        return carry

    lax.fori_loop(1, n_seq, w_sent, 0)
    for back in range(GROUP):
        for step in range(1, n_tp):
            tp_copy((rank + GROUP - back) % GROUP, hid, back, step).wait_send()
    if not merged:
        for cut in range(cuts):
            for step in range(1, groups):
                out_map_copy(step, cut).wait_send()

    for place in range(places):
        if merged:
            source_rank, chunk = place, tp
        else:
            feature = tp * groups + place // cuts
            source_rank, chunk = feature % GROUP, (feature // GROUP) * cuts + place % cuts
        total = None
        for t in range(n_tp):
            mine = (source_rank == rank) & (tp == t)

            @pl.when(mine)
            def _():
                pltpu.make_async_copy(
                    staged.at[rank, chunk], landed.at[place, t], o_local.at[chunk]
                ).wait()

            @pl.when(jnp.logical_not(mine))
            def _():
                remote(
                    staged.at[0, 0], landed.at[place, t], o_send.at[0, 0], o_recv.at[place, t],
                    (base + source_rank, t),
                ).wait_recv()

            value = landed[place, t].astype(jnp.float32)
            total = value if total is None else total + value
        out[:, place * wide : (place + 1) * wide] = total.astype(out.dtype)

    for b in range(GROUP):
        for c in range(chunks):

            @pl.when(jnp.logical_not(is_own(b, c)))
            def _():
                out_copy(b, c).wait_send()


def fused(
    n_seq, n_tp, merged, owner, lengths, w_query, w_keyval, pool, hid, w_out, gain, table, route_idx, route_gate
):
    groups = n_seq // GROUP
    count = hid.shape[0]
    slots = route_idx.shape[0]
    experts, rows, _ = w_query.shape
    depth = w_out.shape[-2]
    dma = pltpu.SemaphoreType.DMA
    vmem = pl.BlockSpec(memory_space=pltpu.VMEM)
    smem = pl.BlockSpec(memory_space=pltpu.SMEM)
    wide = HD
    cuts = 1 if merged else w_out.shape[1] // wide
    chunks = w_out.shape[0] if merged else groups * cuts
    places = GROUP if merged else groups * cuts
    return pl.pallas_call(
        functools.partial(fused_kernel, n_seq, n_tp, slots, merged),
        out_shape=jax.ShapeDtypeStruct((count, places * wide), jnp.bfloat16),
        in_specs=[smem] * 2 + [ANY] * 5 + [vmem] * 4,
        out_specs=vmem,
        scratch_shapes=[
            pltpu.VMEM((n_seq, experts + 2, rows, HD), w_query.dtype),
            pltpu.VMEM((4, 2, pool.shape[1], HD), pool.dtype),
            pltpu.VMEM((2, 2, pool.shape[1], HD), pool.dtype),
            pltpu.VMEM((n_tp, GROUP) + hid.shape, hid.dtype),
            pltpu.VMEM((8, count), jnp.float32),
            pltpu.VMEM((GROUP, 8, count), jnp.float32),
            pltpu.VMEM((chunks, depth, wide), w_out.dtype),
            pltpu.VMEM((GROUP, GROUP, slots, count, HD), jnp.bfloat16),
            pltpu.VMEM((GROUP, count, depth), jnp.bfloat16),
            pltpu.VMEM((GROUP, chunks, count, wide), jnp.bfloat16),
            pltpu.VMEM((places, n_tp, count, wide), jnp.bfloat16),
            dma((6 + cuts,)),
            dma((2, n_seq)),
            dma((2, n_seq)),
            dma((GROUP,)),
            dma((GROUP,)),
            dma((GROUP,)),
            dma((GROUP,)),
            dma((GROUP,)),
            dma((GROUP,)),
            dma((GROUP, n_tp)),
            dma((n_tp, GROUP)),
            dma((groups * cuts,)),
            dma((chunks,)),
            dma((GROUP, GROUP)),
            dma((GROUP, GROUP)),
            dma((GROUP, chunks)),
            dma((places, n_tp)),
            dma((chunks,)),
        ],
        compiler_params=pltpu.CompilerParams(
            collective_id=0, has_side_effects=True, vmem_limit_bytes=48 << 20
        ),
        name="fused",
    )(owner, lengths, w_query, w_keyval, pool, hid, w_out, gain, table, route_idx, route_gate)


def paired_kernel(
    n_seq, n_tp, slots,
    owner_ref, lengths_ref, w_query, w_keyval, pool, hid, w_out, gain, table, route_idx, route_gate, out,
    w_all, pre_all, pre_own, hid_all, meta, meta_all, w_outs, gathered, spread, staged, crossed, landed,
    local_sem, w_send, w_recv, p_send, p_recv, h_send, h_recv, m_send, m_recv, t_send, t_recv,
    x_send, x_recv, a_send, a_recv, e_send, e_recv, o_send, o_recv, o_local,
):
    groups = n_seq // GROUP
    seq = lax.axis_index("seq")
    tp = lax.axis_index("tp")
    group = seq // GROUP
    base = group * GROUP
    rank = seq % GROUP
    count, width = hid_all.shape[2:]
    experts = w_query.shape[0]
    chunks, _, wide = w_outs.shape
    places = landed.shape[0]
    cuts = chunks // groups
    core = tp % 2
    inner = rank // 2 != group % 2

    def lanes(index):
        return pl.ds(pl.multiple_of(index * HD, HD), HD)

    tokens = lax.broadcasted_iota(jnp.int32, (1, count), 1)
    segment = jnp.zeros((1, count), jnp.int32)
    position = tokens
    end = 0
    for j in range(lengths_ref.shape[1]):
        length = lengths_ref[0, j]
        end = end + length
        past = tokens >= end
        segment = segment + jnp.where(past, 1, 0)
        position = position - jnp.where(past, length, 0)
    meta[0:slots] = route_idx[...].astype(jnp.float32)
    meta[slots : 2 * slots] = route_gate[...]
    meta[4:5] = position.astype(jnp.float32)
    meta[5:6] = segment.astype(jnp.float32)
    meta[6:8] = jnp.zeros((2, count), jnp.float32)

    def member(step):
        return ((group + step // GROUP) % groups) * GROUP + (rank + step % GROUP) % GROUP

    def peer(step):
        return (rank + step) % GROUP

    barrier = pltpu.get_barrier_semaphore()

    def greet(step, carry):
        pl.semaphore_signal(barrier, inc=1, device_id=(member(step), tp), device_id_type=MESH)
        return carry

    lax.fori_loop(1, n_seq, greet, 0)
    for step in range(GROUP):
        for turn in range(1, n_tp):
            pl.semaphore_signal(
                barrier, inc=1, device_id=(base + peer(step), (tp + turn) % n_tp), device_id_type=MESH
            )
    pl.semaphore_wait(barrier, n_seq - 1 + GROUP * (n_tp - 1))

    def meta_copy(step):
        return remote(meta, meta_all.at[rank], m_send.at[step], m_recv.at[rank], (base + peer(step), tp))

    beside = rank + 1 - 2 * (rank % 2)
    across = (rank + 2) % GROUP
    corner = (beside + 2) % GROUP
    owner = owner_ref[group]

    def hid_copy(step):
        if step == 2:
            block, to = across, beside
        else:
            block, to = rank, across if step == 0 else beside
        return remote(
            hid if step < 2 else hid_all.at[tp, block], hid_all.at[tp, block],
            h_send.at[step], h_recv.at[block], (base + to, tp),
        )

    def hid_arrive(source):
        remote(hid, hid_all.at[tp, source], h_send.at[0], h_recv.at[source], (base + source, tp)).wait_recv()

    def hid_spread(source):
        for step in range(1, n_tp):
            tp_copy(source, hid_all.at[tp, source], (rank + GROUP - source) % GROUP, step).start()


    def pool_copy(step):
        if step == 0:
            head, place, partner = beside, 0, beside
        elif step == 1:
            head, place, partner = (beside + 2) % GROUP, 1, beside
        else:
            return remote(
                pre_all.at[3], pre_all.at[2], p_send.at[2], p_recv.at[2], (base + across, tp)
            )
        return remote(
            pool.at[:, :, lanes(head)], pre_all.at[place], p_send.at[step], p_recv.at[step], (base + partner, tp)
        )

    def w_part(part, head, place):
        if part == 0:
            return w_query.at[:, :, lanes(head)], w_all.at[place, 0:experts]
        return w_keyval.at[:, :, lanes(head)], w_all.at[place, experts : experts + 2]

    def w_copy(part, step):
        dest = member(step)
        src, dst = w_part(part, dest % GROUP, seq)
        return remote(src, dst, w_send.at[part, step], w_recv.at[part, seq], (dest, tp))

    def tp_copy(block, src, back, step):
        return remote(
            src, hid_all.at[tp, block], t_send.at[back, step], t_recv.at[tp, back], (seq, (tp + step) % n_tp)
        )

    def out_map_copy(step, cut):
        dest = ((group + step) % groups) * GROUP + rank
        chunk = group * cuts + cut
        return remote(
            w_out.at[:, cut * wide : (cut + 1) * wide], w_outs.at[chunk],
            x_send.at[step * cuts + cut], x_recv.at[chunk], (dest, tp),
        )

    def w_start(step, carry):
        for part in range(2):
            w_copy(part, step).start()
        return carry

    def w_wait(step, carry):
        source = member(step)
        for part in range(2):
            src, dst = w_part(part, 0, source)
            remote(src, dst, w_send.at[part, step], w_recv.at[part, source], (source, tp)).wait_recv()
        return carry

    for step in range(2):
        hid_copy(step).start()
    for step in range(1, n_tp):
        tp_copy(rank, hid, 0, step).start()
    for step in range(1, GROUP):
        meta_copy(step).start()
    lax.fori_loop(GROUP, n_seq, w_start, 0)
    w_start(2, 0)
    w_start((corner + GROUP - rank) % GROUP, 0)
    hid_arrive(across)
    hid_copy(2).start()
    hid_spread(across)
    for step in (1, 0):
        pool_copy(step).start()
    w_start((beside + GROUP - rank) % GROUP, 0)
    own = [
        pltpu.make_async_copy(hid, hid_all.at[tp, rank], local_sem.at[0]),
        pltpu.make_async_copy(meta, meta_all.at[rank], local_sem.at[1]),
        pltpu.make_async_copy(*w_part(0, rank, seq), local_sem.at[2]),
        pltpu.make_async_copy(*w_part(1, rank, seq), local_sem.at[3]),
        pltpu.make_async_copy(pool.at[:, :, lanes(rank)], pre_own.at[0], local_sem.at[4]),
        pltpu.make_async_copy(pool.at[:, :, lanes(across)], pre_own.at[1], local_sem.at[5 + cuts]),
    ]
    for cut in range(cuts):
        own.append(
            pltpu.make_async_copy(
                w_out.at[:, cut * wide : (cut + 1) * wide], w_outs.at[group * cuts + cut], local_sem.at[5 + cut]
            )
        )
    for copy in own:
        copy.start()

    for source in (beside, corner):
        hid_arrive(source)
        hid_spread(source)

    for copy in own:
        copy.wait()
    pool_copy(0).wait_recv()
    pool_copy(1).wait_recv()
    pre_all[3] = jnp.where(owner == rank, pre_own[1], pre_all[1])
    pool_copy(2).start()
    near_owner = jnp.where(owner == rank, pre_own[0], pre_all[0])
    pre_own[0] = near_owner
    def w_left(step, carry):
        for part in range(2):
            w_copy(part, step).wait_send()
        return carry

    lax.fori_loop(GROUP, n_seq, w_left, 0)
    def out_map_start(cut):
        for step in range(1, groups):
            out_map_copy(step, cut).start()

    @pl.when(jnp.logical_not(inner))
    def _():
        for cut in range(cuts):
            out_map_start(cut)

    lax.fori_loop(GROUP, n_seq, w_wait, 0)
    for step in range(1, GROUP):
        source = peer(step)
        from_peer = (base + source, tp)
        remote(meta, meta_all.at[source], m_send.at[step], m_recv.at[source], from_peer).wait_recv()
    for back in range(GROUP):
        block = (rank + GROUP - back) % GROUP
        for step in range(1, n_tp):
            source = (tp + step) % n_tp
            remote(
                hid, hid_all.at[source, block], t_send.at[back, step], t_recv.at[source, back], (seq, source)
            ).wait_recv()
    lax.fori_loop(1, GROUP, w_wait, 0)
    pool_copy(2).wait_recv()
    pre_own[0] = jnp.where(owner // 2 == rank // 2, pre_own[0], pre_all[2])

    def att_copy(b, step):
        block = across if step == 2 else rank
        return remote(
            gathered.at[block, b], gathered.at[block, b], a_send.at[b, step], a_recv.at[block, b],
            (base + (across if step == 0 else beside), tp),
        )

    def att_wait(b, source):
        remote(
            gathered.at[rank, b], gathered.at[source, b], a_send.at[b, 0], a_recv.at[source, b], (base + source, tp)
        ).wait_recv()

    share = n_seq // n_tp
    contract = (((1,), (1,)), ((), ()))
    factor = LOG2E * HD ** (-0.5)

    def attend(b, carry):
        rows = [hid_all[t, b].astype(jnp.float32) for t in range(n_tp)]
        squares = sum(jnp.sum(x * x, axis=1, keepdims=True) for x in rows)
        inverse = lax.rsqrt(squares * (1.0 / (n_tp * width)) + EPSILON)
        acc = None
        for t in range(n_tp):
            normed = (rows[t] * inverse * gain[t]).astype(jnp.bfloat16)
            piece = jnp.concatenate(
                [w_all[t * share : (t + 1) * share, e].reshape(width, HD) for e in range(experts + 2)], axis=1
            )
            part = jnp.dot(normed, piece, preferred_element_type=jnp.float32)
            acc = part if acc is None else acc + part
        row = meta_all[b]
        col = row.T
        first = lax.broadcasted_iota(jnp.int32, (count, count), 0)
        second = lax.broadcasted_iota(jnp.int32, (count, count), 1)
        hot = (col[:, 4:5] == second.astype(jnp.float32)).astype(jnp.bfloat16)
        looked = jnp.dot(hot, table[...], preferred_element_type=jnp.float32)
        looked = looked[:, : 2 * HD] + looked[:, 2 * HD : 4 * HD] + looked[:, 4 * HD :]
        cos = looked[:, :HD]
        sin = looked[:, HD:]

        def rotate(value):
            return value * cos + pltpu.roll(value, HD // 2, 1) * sin

        new_key = rotate(acc[:, experts * HD : (experts + 1) * HD]).astype(jnp.bfloat16)
        new_value = acc[:, (experts + 1) * HD :].astype(jnp.bfloat16)
        seen = (col[:, 5:6] == row[5:6, :]) & (second <= first)
        for k in range(slots):
            index = col[:, k : k + 1]
            chosen = jnp.zeros((count, HD), jnp.float32)
            for e in range(experts):
                chosen = jnp.where(index == float(e), acc[:, e * HD : (e + 1) * HD], chosen)
            query = rotate(chosen).astype(jnp.bfloat16)
            far = lax.dot_general(query, pre_own[0, 0], contract, preferred_element_type=jnp.float32)
            near = lax.dot_general(query, new_key, contract, preferred_element_type=jnp.float32)
            near = jnp.where(seen, near, -1e30)
            top = jnp.maximum(jnp.max(far, axis=1, keepdims=True), jnp.max(near, axis=1, keepdims=True))
            far = jnp.exp2((far - top) * factor)
            near = jnp.where(seen, jnp.exp2((near - top) * factor), 0.0)
            total = jnp.sum(far, axis=1, keepdims=True) + jnp.sum(near, axis=1, keepdims=True)
            numer = jnp.dot(far.astype(jnp.bfloat16), pre_own[0, 1], preferred_element_type=jnp.float32)
            numer += jnp.dot(near.astype(jnp.bfloat16), new_value, preferred_element_type=jnp.float32)
            gathered[rank, b, k] = (numer * (col[:, slots + k : slots + k + 1] / total)).astype(jnp.bfloat16)
        for step in range(2):
            att_copy(b, step).start()

        @pl.when(inner & (b == 0))
        def _():
            out_map_start(0)

        @pl.when(inner & (b == 2))
        def _():
            for cut in range(1, cuts):
                out_map_start(cut)

        return carry

    lax.fori_loop(0, GROUP, attend, 0)

    def att_relay(b, carry):
        att_wait(b, across)
        att_copy(b, 2).start()
        return carry

    lax.fori_loop(0, GROUP, att_relay, 0)

    def target(c):
        feature = (c // cuts) * GROUP + rank
        return feature // groups, (feature % groups) * cuts + c % cuts

    def core_copy(b, c):
        return remote(
            staged.at[b, c], crossed.at[b, c], e_send.at[b, c], e_recv.at[b, c], (seq, tp + 1 - 2 * core)
        )

    def out_copy(b, c):
        column, place = target(c)
        return remote(
            staged.at[b, c], landed.at[place, tp // 2], o_send.at[b, c], o_recv.at[place, tp // 2],
            (base + b, column),
        )

    def own_copy(b, c):
        column, place = target(c)
        return pltpu.make_async_copy(staged.at[b, c], landed.at[place, tp // 2], o_local.at[c])

    def is_own(b, c):
        return (b == rank) & (target(c)[0] == tp)

    def expand(i, carry):
        b = i
        for source in (beside, corner):
            att_wait(b, source)
        col = meta_all[b].T
        depth = GROUP * HD
        for e in range(experts):
            hot = [(col[:, k : k + 1] == float(e)).astype(jnp.bfloat16) for k in range(slots)]
            for s in range(GROUP):
                spread[b, :, e * depth + s * HD : e * depth + (s + 1) * HD] = sum(
                    gathered[s, b, k] * hot[k] for k in range(slots)
                )
        return carry

    lax.fori_loop(0, GROUP, expand, 0)

    for j in range(chunks):
        c = (group * cuts + j) % chunks
        if j >= cuts:
            remote(
                w_out.at[:, 0:wide], w_outs.at[c], x_send.at[0], x_recv.at[c], ((c // cuts) * GROUP + rank, tp)
            ).wait_recv()

        def lend(i, carry):
            b = 1 - core + 2 * ((rank // 2 + 1 + i) % 2)
            staged[b, c] = jnp.dot(spread[b], w_outs[c], preferred_element_type=jnp.float32).astype(
                staged.dtype
            )
            core_copy(b, c).start()
            return carry

        def project(i, carry):
            b = core + 2 * ((rank // 2 + 1 + i) % 2)
            part = jnp.dot(spread[b], w_outs[c], preferred_element_type=jnp.float32)
            core_copy(b, c).wait_recv()
            staged[b, c] = (part + crossed[b, c].astype(jnp.float32)).astype(staged.dtype)

            @pl.when(is_own(b, c))
            def _():
                own_copy(b, c).start()

            @pl.when(jnp.logical_not(is_own(b, c)))
            def _():
                out_copy(b, c).start()

            return carry

        lax.fori_loop(0, 2, lend, 0)
        lax.fori_loop(0, 2, project, 0)

    for step in range(3):
        hid_copy(step).wait_send()
        for b in range(GROUP):
            att_copy(b, step).wait_send()
    for step in range(1, GROUP):
        meta_copy(step).wait_send()

    for step in range(3):
        pool_copy(step).wait_send()

    def w_sent(step, carry):
        for part in range(2):
            w_copy(part, step).wait_send()
        return carry

    lax.fori_loop(1, GROUP, w_sent, 0)
    for back in range(GROUP):
        for step in range(1, n_tp):
            tp_copy((rank + GROUP - back) % GROUP, hid, back, step).wait_send()
    for cut in range(cuts):
        for step in range(1, groups):
            out_map_copy(step, cut).wait_send()

    for place in range(places):
        feature = tp * groups + place // cuts
        source_rank, chunk = feature % GROUP, (feature // GROUP) * cuts + place % cuts
        total = None
        for y in range(n_tp // 2):
            source = 2 * y + rank % 2
            mine = (source_rank == rank) & (tp == source)

            @pl.when(mine)
            def _():
                pltpu.make_async_copy(
                    staged.at[rank, chunk], landed.at[place, y], o_local.at[chunk]
                ).wait()

            @pl.when(jnp.logical_not(mine))
            def _():
                remote(
                    staged.at[0, 0], landed.at[place, y], o_send.at[0, 0], o_recv.at[place, y],
                    (base + source_rank, source),
                ).wait_recv()

            value = landed[place, y].astype(jnp.float32)
            total = value if total is None else total + value
        out[:, place * wide : (place + 1) * wide] = total.astype(out.dtype)

    for c in range(chunks):
        for i in range(2):
            core_copy(1 - core + 2 * i, c).wait_send()

            @pl.when(jnp.logical_not(is_own(core + 2 * i, c)))
            def _():
                out_copy(core + 2 * i, c).wait_send()


def paired(
    n_seq, n_tp, owner, lengths, w_query, w_keyval, pool, hid, w_out, gain, table, route_idx, route_gate
):
    groups = n_seq // GROUP
    count = hid.shape[0]
    slots = route_idx.shape[0]
    experts, rows, _ = w_query.shape
    depth = w_out.shape[-2]
    dma = pltpu.SemaphoreType.DMA
    vmem = pl.BlockSpec(memory_space=pltpu.VMEM)
    smem = pl.BlockSpec(memory_space=pltpu.SMEM)
    wide = HD
    cuts = w_out.shape[1] // wide
    chunks = places = groups * cuts
    return pl.pallas_call(
        functools.partial(paired_kernel, n_seq, n_tp, slots),
        out_shape=jax.ShapeDtypeStruct((count, places * wide), jnp.bfloat16),
        in_specs=[smem] * 2 + [ANY] * 5 + [vmem] * 4,
        out_specs=vmem,
        scratch_shapes=[
            pltpu.VMEM((n_seq, experts + 2, rows, HD), w_query.dtype),
            pltpu.VMEM((4, 2, pool.shape[1], HD), pool.dtype),
            pltpu.VMEM((2, 2, pool.shape[1], HD), pool.dtype),
            pltpu.VMEM((n_tp, GROUP) + hid.shape, hid.dtype),
            pltpu.VMEM((8, count), jnp.float32),
            pltpu.VMEM((GROUP, 8, count), jnp.float32),
            pltpu.VMEM((chunks, depth, wide), w_out.dtype),
            pltpu.VMEM((GROUP, GROUP, slots, count, HD), jnp.bfloat16),
            pltpu.VMEM((GROUP, count, depth), jnp.bfloat16),
            pltpu.VMEM((GROUP, chunks, count, wide), jnp.bfloat16),
            pltpu.VMEM((GROUP, chunks, count, wide), jnp.bfloat16),
            pltpu.VMEM((places, n_tp // 2, count, wide), jnp.bfloat16),
            dma((6 + cuts,)),
            dma((2, n_seq)),
            dma((2, n_seq)),
            dma((GROUP,)),
            dma((GROUP,)),
            dma((GROUP,)),
            dma((GROUP,)),
            dma((GROUP,)),
            dma((GROUP,)),
            dma((GROUP, n_tp)),
            dma((n_tp, GROUP)),
            dma((groups * cuts,)),
            dma((chunks,)),
            dma((GROUP, GROUP)),
            dma((GROUP, GROUP)),
            dma((GROUP, chunks)),
            dma((GROUP, chunks)),
            dma((GROUP, chunks)),
            dma((places, n_tp // 2)),
            dma((chunks,)),
        ],
        compiler_params=pltpu.CompilerParams(
            collective_id=0, has_side_effects=True, vmem_limit_bytes=48 << 20
        ),
        name="paired",
    )(owner, lengths, w_query, w_keyval, pool, hid, w_out, gain, table, route_idx, route_gate)


def rope_table(count, prefix):
    freqs = np.float32(THETA) ** (-(np.arange(HD // 2, dtype=np.float32) * np.float32(2.0)) / np.float32(HD))
    angles = (np.arange(count) + prefix).astype(np.float32)[:, None] * freqs[None, :].astype(np.float32)
    cosine = np.cos(angles.astype(np.float64))
    sine = np.sin(angles.astype(np.float64))
    rest = np.concatenate([cosine, cosine, -sine, sine], axis=1).astype(np.float32)
    parts = []
    for _ in range(3):
        part = rest.astype(ml_dtypes.bfloat16)
        parts.append(part)
        rest = rest - part.astype(np.float32)
    return np.concatenate(parts, axis=1)


def per_device(
    n_seq, n_tp, hidden, lengths, cache_owner, cache_pool, norm_gain, route_idx, route_gate,
    w_query, w_keyval, w_out,
):
    groups = n_seq // GROUP
    count = hidden.shape[0]
    rows, experts, width = w_query.shape
    prefix = cache_pool.shape[1]
    assert width == GROUP * HD
    wide = w_out.shape[2]
    merged = wide < HD
    if n_seq == 2 * GROUP and n_tp == 4 and not merged:
        return paired(
            n_seq, n_tp, cache_owner, lengths, w_query.swapaxes(0, 1), w_keyval.swapaxes(0, 1),
            cache_pool[0].swapaxes(0, 1), hidden, w_out.reshape(experts * width, wide), norm_gain.reshape(n_tp, 1, -1),
            jnp.asarray(rope_table(count, prefix)), route_idx.T, route_gate.T,
        )
    if merged:
        same_rank = [[g * GROUP + r for g in range(groups)] for r in range(GROUP)]
        per = groups // n_tp
        w_out = lax.all_gather(w_out, "seq", axis=0, axis_index_groups=same_rank)
        w_out = w_out.reshape(n_tp, per, experts, width, wide).transpose(0, 2, 3, 1, 4)
        w_out = w_out.reshape(n_tp, experts * width, per * wide)
    else:
        w_out = w_out.reshape(experts * width, wide)
    out = fused(
        n_seq, n_tp, merged, cache_owner, lengths, w_query.swapaxes(0, 1), w_keyval.swapaxes(0, 1),
        cache_pool[0].swapaxes(0, 1), hidden, w_out, norm_gain.reshape(n_tp, 1, -1),
        jnp.asarray(rope_table(count, prefix)), route_idx.T, route_gate.T,
    )
    if merged:
        out = out.reshape(count, GROUP, groups // n_tp, wide).transpose(0, 2, 1, 3).reshape(count, -1)
    return out


def solution(mesh):
    placed = (
        P("seq", "tp"),
        P("seq", None),
        P(),
        P("seq", None, None, "tp"),
        P(),
        P("seq", None),
        P("seq", None),
        P("seq", None, "tp"),
        P("seq", None, "tp"),
        P(None, "tp", "seq"),
    )
    body = functools.partial(per_device, mesh.shape["seq"], mesh.shape["tp"])
    return jax.shard_map(body, mesh=mesh, in_specs=placed, out_specs=P("seq", "tp"), check_vma=False)
```

```python
import functools

import jax
import jax.numpy as jnp
import ml_dtypes
import numpy as np
from jax import lax
from jax.experimental import pallas as pl
from jax.experimental.pallas import tpu as pltpu
from jax.sharding import PartitionSpec as P

HD = 128
GROUP = 4
EPSILON = 1e-05
THETA = 10000.0
LOG2E = 1.4426950408889634
MESH = pl.DeviceIdType.MESH
ANY = pl.BlockSpec(memory_space=pl.ANY)


def remote(src, dst, send_sem, recv_sem, device):
    return pltpu.make_async_remote_copy(
        src_ref=src,
        dst_ref=dst,
        send_sem=send_sem,
        recv_sem=recv_sem,
        device_id=device,
        device_id_type=MESH,
    )


def fused_kernel(
    n_seq, n_tp, slots, merged,
    owner_ref, lengths_ref, w_query, w_keyval, pool, hid, w_out, gain, table, route_idx, route_gate, out,
    w_all, pre_all, pre_own, hid_all, meta, meta_all, w_outs, gathered, spread, staged, landed,
    local_sem, w_send, w_recv, p_send, p_recv, h_send, h_recv, m_send, m_recv, t_send, t_recv,
    x_send, x_recv, a_send, a_recv, o_send, o_recv, o_local,
):
    groups = n_seq // GROUP
    seq = lax.axis_index("seq")
    tp = lax.axis_index("tp")
    group = seq // GROUP
    base = group * GROUP
    rank = seq % GROUP
    count, width = hid_all.shape[2:]
    experts = w_query.shape[0]
    chunks, _, wide = w_outs.shape
    places = landed.shape[0]
    cuts = chunks // groups

    def lanes(index):
        return pl.ds(pl.multiple_of(index * HD, HD), HD)

    tokens = lax.broadcasted_iota(jnp.int32, (1, count), 1)
    segment = jnp.zeros((1, count), jnp.int32)
    position = tokens
    end = 0
    for j in range(lengths_ref.shape[1]):
        length = lengths_ref[0, j]
        end = end + length
        past = tokens >= end
        segment = segment + jnp.where(past, 1, 0)
        position = position - jnp.where(past, length, 0)
    meta[0:slots] = route_idx[...].astype(jnp.float32)
    meta[slots : 2 * slots] = route_gate[...]
    meta[4:5] = position.astype(jnp.float32)
    meta[5:6] = segment.astype(jnp.float32)
    meta[6:8] = jnp.zeros((2, count), jnp.float32)

    def member(step):
        return ((group + step // GROUP) % groups) * GROUP + (rank + step % GROUP) % GROUP

    def peer(step):
        return (rank + step) % GROUP

    barrier = pltpu.get_barrier_semaphore()

    def greet(step, carry):
        pl.semaphore_signal(barrier, inc=1, device_id=(member(step), tp), device_id_type=MESH)
        return carry

    lax.fori_loop(1, n_seq, greet, 0)
    for step in range(GROUP):
        for turn in range(1, n_tp):
            pl.semaphore_signal(
                barrier, inc=1, device_id=(base + peer(step), (tp + turn) % n_tp), device_id_type=MESH
            )
    pl.semaphore_wait(barrier, n_seq - 1 + GROUP * (n_tp - 1))

    def hid_copy(step):
        return remote(hid, hid_all.at[tp, rank], h_send.at[step], h_recv.at[rank], (base + peer(step), tp))

    def meta_copy(step):
        return remote(meta, meta_all.at[rank], m_send.at[step], m_recv.at[rank], (base + peer(step), tp))

    beside = rank + 1 - 2 * (rank % 2)
    across = (rank + 2) % GROUP
    owner = owner_ref[group]

    def pool_copy(step):
        if step == 0:
            head, place, partner = beside, 0, beside
        elif step == 1:
            head, place, partner = (beside + 2) % GROUP, 1, beside
        else:
            return remote(
                pre_all.at[3], pre_all.at[2], p_send.at[2], p_recv.at[2], (base + across, tp)
            )
        return remote(
            pool.at[:, :, lanes(head)], pre_all.at[place], p_send.at[step], p_recv.at[step], (base + partner, tp)
        )

    def w_part(part, head, place):
        if part == 0:
            return w_query.at[:, :, lanes(head)], w_all.at[place, 0:experts]
        return w_keyval.at[:, :, lanes(head)], w_all.at[place, experts : experts + 2]

    def w_copy(part, step):
        dest = member(step)
        src, dst = w_part(part, dest % GROUP, seq)
        return remote(src, dst, w_send.at[part, step], w_recv.at[part, seq], (dest, tp))

    def tp_copy(block, src, back, step):
        return remote(
            src, hid_all.at[tp, block], t_send.at[back, step], t_recv.at[tp, back], (seq, (tp + step) % n_tp)
        )

    def out_map_copy(step, cut):
        dest = ((group + step) % groups) * GROUP + rank
        chunk = group * cuts + cut
        return remote(
            w_out.at[:, cut * wide : (cut + 1) * wide], w_outs.at[chunk],
            x_send.at[step * cuts + cut], x_recv.at[chunk], (dest, tp),
        )

    def w_start(step, carry):
        for part in range(2):
            w_copy(part, step).start()
        return carry

    def w_wait(step, carry):
        source = member(step)
        for part in range(2):
            src, dst = w_part(part, 0, source)
            remote(src, dst, w_send.at[part, step], w_recv.at[part, source], (source, tp)).wait_recv()
        return carry

    for step in range(1, GROUP):
        hid_copy(step).start()
    for step in range(1, n_tp):
        tp_copy(rank, hid, 0, step).start()
    for step in range(1, GROUP):
        meta_copy(step).start()
    for step in (1, 0):
        pool_copy(step).start()
    lax.fori_loop(GROUP, n_seq, w_start, 0)
    lax.fori_loop(1, GROUP, w_start, 0)
    own = [
        pltpu.make_async_copy(hid, hid_all.at[tp, rank], local_sem.at[0]),
        pltpu.make_async_copy(meta, meta_all.at[rank], local_sem.at[1]),
        pltpu.make_async_copy(*w_part(0, rank, seq), local_sem.at[2]),
        pltpu.make_async_copy(*w_part(1, rank, seq), local_sem.at[3]),
        pltpu.make_async_copy(pool.at[:, :, lanes(rank)], pre_own.at[0], local_sem.at[4]),
        pltpu.make_async_copy(pool.at[:, :, lanes(across)], pre_own.at[1], local_sem.at[5 + cuts]),
    ]
    if merged:
        own.append(pltpu.make_async_copy(w_out, w_outs, local_sem.at[5]))
    else:
        for cut in range(cuts):
            own.append(
                pltpu.make_async_copy(
                    w_out.at[:, cut * wide : (cut + 1) * wide],
                    w_outs.at[group * cuts + cut],
                    local_sem.at[5 + cut],
                )
            )
    for copy in own:
        copy.start()

    for back in range(1, GROUP):
        source = (rank + GROUP - back) % GROUP
        remote(hid, hid_all.at[tp, source], h_send.at[back], h_recv.at[source], (base + source, tp)).wait_recv()
        for step in range(1, n_tp):
            tp_copy(source, hid_all.at[tp, source], back, step).start()

    for copy in own:
        copy.wait()
    pool_copy(0).wait_recv()
    pool_copy(1).wait_recv()
    pre_all[3] = jnp.where(owner == rank, pre_own[1], pre_all[1])
    pool_copy(2).start()
    near_owner = jnp.where(owner == rank, pre_own[0], pre_all[0])
    pre_own[0] = near_owner
    lax.fori_loop(GROUP, n_seq, w_wait, 0)
    if not merged:
        for cut in range(cuts):
            for step in range(1, groups):
                out_map_copy(step, cut).start()
    for step in range(1, GROUP):
        source = peer(step)
        from_peer = (base + source, tp)
        remote(meta, meta_all.at[source], m_send.at[step], m_recv.at[source], from_peer).wait_recv()
    for back in range(GROUP):
        block = (rank + GROUP - back) % GROUP
        for step in range(1, n_tp):
            source = (tp + step) % n_tp
            remote(
                hid, hid_all.at[source, block], t_send.at[back, step], t_recv.at[source, back], (seq, source)
            ).wait_recv()
    lax.fori_loop(1, GROUP, w_wait, 0)
    pool_copy(2).wait_recv()
    pre_own[0] = jnp.where(owner // 2 == rank // 2, pre_own[0], pre_all[2])

    def att_copy(b, step):
        return remote(
            gathered.at[rank, b], gathered.at[rank, b], a_send.at[b, step], a_recv.at[rank, b],
            (base + peer(step), tp),
        )

    share = n_seq // n_tp
    contract = (((1,), (1,)), ((), ()))
    factor = LOG2E * HD ** (-0.5)

    def attend(b, carry):
        rows = [hid_all[t, b].astype(jnp.float32) for t in range(n_tp)]
        squares = sum(jnp.sum(x * x, axis=1, keepdims=True) for x in rows)
        inverse = lax.rsqrt(squares * (1.0 / (n_tp * width)) + EPSILON)
        acc = None
        for t in range(n_tp):
            normed = (rows[t] * inverse * gain[t]).astype(jnp.bfloat16)
            piece = jnp.concatenate(
                [w_all[t * share : (t + 1) * share, e].reshape(width, HD) for e in range(experts + 2)], axis=1
            )
            part = jnp.dot(normed, piece, preferred_element_type=jnp.float32)
            acc = part if acc is None else acc + part
        row = meta_all[b]
        col = row.T
        first = lax.broadcasted_iota(jnp.int32, (count, count), 0)
        second = lax.broadcasted_iota(jnp.int32, (count, count), 1)
        hot = (col[:, 4:5] == second.astype(jnp.float32)).astype(jnp.bfloat16)
        looked = jnp.dot(hot, table[...], preferred_element_type=jnp.float32)
        looked = looked[:, : 2 * HD] + looked[:, 2 * HD : 4 * HD] + looked[:, 4 * HD :]
        cos = looked[:, :HD]
        sin = looked[:, HD:]

        def rotate(value):
            return value * cos + pltpu.roll(value, HD // 2, 1) * sin

        new_key = rotate(acc[:, experts * HD : (experts + 1) * HD]).astype(jnp.bfloat16)
        new_value = acc[:, (experts + 1) * HD :].astype(jnp.bfloat16)
        seen = (col[:, 5:6] == row[5:6, :]) & (second <= first)
        for k in range(slots):
            index = col[:, k : k + 1]
            chosen = jnp.zeros((count, HD), jnp.float32)
            for e in range(experts):
                chosen = jnp.where(index == float(e), acc[:, e * HD : (e + 1) * HD], chosen)
            query = rotate(chosen).astype(jnp.bfloat16)
            far = lax.dot_general(query, pre_own[0, 0], contract, preferred_element_type=jnp.float32)
            near = lax.dot_general(query, new_key, contract, preferred_element_type=jnp.float32)
            near = jnp.where(seen, near, -1e30)
            top = jnp.maximum(jnp.max(far, axis=1, keepdims=True), jnp.max(near, axis=1, keepdims=True))
            far = jnp.exp2((far - top) * factor)
            near = jnp.where(seen, jnp.exp2((near - top) * factor), 0.0)
            total = jnp.sum(far, axis=1, keepdims=True) + jnp.sum(near, axis=1, keepdims=True)
            numer = jnp.dot(far.astype(jnp.bfloat16), pre_own[0, 1], preferred_element_type=jnp.float32)
            numer += jnp.dot(near.astype(jnp.bfloat16), new_value, preferred_element_type=jnp.float32)
            gathered[rank, b, k] = (numer * (col[:, slots + k : slots + k + 1] / total)).astype(jnp.bfloat16)
        for step in range(1, GROUP):
            att_copy(b, step).start()
        return carry

    lax.fori_loop(0, GROUP, attend, 0)

    def target(c):
        if merged:
            return c, rank
        feature = (c // cuts) * GROUP + rank
        return feature // groups, (feature % groups) * cuts + c % cuts

    def out_copy(b, c):
        column, place = target(c)
        return remote(
            staged.at[b, c], landed.at[place, tp], o_send.at[b, c], o_recv.at[place, tp], (base + b, column)
        )

    def own_copy(b, c):
        column, place = target(c)
        return pltpu.make_async_copy(staged.at[b, c], landed.at[place, tp], o_local.at[c])

    def is_own(b, c):
        return (b == rank) & (target(c)[0] == tp)

    def expand(i, carry):
        b = (rank + 1 + i) % GROUP
        for step in range(1, GROUP):
            source = peer(step)
            remote(
                gathered.at[rank, b], gathered.at[source, b], a_send.at[b, step], a_recv.at[source, b],
                (base + source, tp),
            ).wait_recv()
        col = meta_all[b].T
        depth = GROUP * HD
        for e in range(experts):
            hot = [(col[:, k : k + 1] == float(e)).astype(jnp.bfloat16) for k in range(slots)]
            for s in range(GROUP):
                spread[b, :, e * depth + s * HD : e * depth + (s + 1) * HD] = sum(
                    gathered[s, b, k] * hot[k] for k in range(slots)
                )
        return carry

    lax.fori_loop(0, GROUP, expand, 0)

    for j in range(chunks):
        c = j if merged else (group * cuts + j) % chunks
        if not merged and j >= cuts:
            remote(
                w_out.at[:, 0:wide], w_outs.at[c], x_send.at[0], x_recv.at[c], ((c // cuts) * GROUP + rank, tp)
            ).wait_recv()

        def project(i, carry):
            b = (rank + 1 + i) % GROUP
            staged[b, c] = jnp.dot(spread[b], w_outs[c], preferred_element_type=jnp.float32).astype(
                staged.dtype
            )

            @pl.when(is_own(b, c))
            def _():
                own_copy(b, c).start()

            @pl.when(jnp.logical_not(is_own(b, c)))
            def _():
                out_copy(b, c).start()

            return carry

        lax.fori_loop(0, GROUP, project, 0)

    for step in range(1, GROUP):
        hid_copy(step).wait_send()
        meta_copy(step).wait_send()
        for b in range(GROUP):
            att_copy(b, step).wait_send()

    for step in range(3):
        pool_copy(step).wait_send()

    def w_sent(step, carry):
        for part in range(2):
            w_copy(part, step).wait_send()
        return carry

    lax.fori_loop(1, n_seq, w_sent, 0)
    for back in range(GROUP):
        for step in range(1, n_tp):
            tp_copy((rank + GROUP - back) % GROUP, hid, back, step).wait_send()
    if not merged:
        for cut in range(cuts):
            for step in range(1, groups):
                out_map_copy(step, cut).wait_send()

    for place in range(places):
        if merged:
            source_rank, chunk = place, tp
        else:
            feature = tp * groups + place // cuts
            source_rank, chunk = feature % GROUP, (feature // GROUP) * cuts + place % cuts
        total = None
        for t in range(n_tp):
            mine = (source_rank == rank) & (tp == t)

            @pl.when(mine)
            def _():
                pltpu.make_async_copy(
                    staged.at[rank, chunk], landed.at[place, t], o_local.at[chunk]
                ).wait()

            @pl.when(jnp.logical_not(mine))
            def _():
                remote(
                    staged.at[0, 0], landed.at[place, t], o_send.at[0, 0], o_recv.at[place, t],
                    (base + source_rank, t),
                ).wait_recv()

            value = landed[place, t].astype(jnp.float32)
            total = value if total is None else total + value
        out[:, place * wide : (place + 1) * wide] = total.astype(out.dtype)

    for b in range(GROUP):
        for c in range(chunks):

            @pl.when(jnp.logical_not(is_own(b, c)))
            def _():
                out_copy(b, c).wait_send()


def fused(
    n_seq, n_tp, merged, owner, lengths, w_query, w_keyval, pool, hid, w_out, gain, table, route_idx, route_gate
):
    groups = n_seq // GROUP
    count = hid.shape[0]
    slots = route_idx.shape[0]
    experts, rows, _ = w_query.shape
    depth = w_out.shape[-2]
    dma = pltpu.SemaphoreType.DMA
    vmem = pl.BlockSpec(memory_space=pltpu.VMEM)
    smem = pl.BlockSpec(memory_space=pltpu.SMEM)
    wide = HD
    cuts = 1 if merged else w_out.shape[1] // wide
    chunks = w_out.shape[0] if merged else groups * cuts
    places = GROUP if merged else groups * cuts
    return pl.pallas_call(
        functools.partial(fused_kernel, n_seq, n_tp, slots, merged),
        out_shape=jax.ShapeDtypeStruct((count, places * wide), jnp.bfloat16),
        in_specs=[smem] * 2 + [ANY] * 5 + [vmem] * 4,
        out_specs=vmem,
        scratch_shapes=[
            pltpu.VMEM((n_seq, experts + 2, rows, HD), w_query.dtype),
            pltpu.VMEM((4, 2, pool.shape[1], HD), pool.dtype),
            pltpu.VMEM((2, 2, pool.shape[1], HD), pool.dtype),
            pltpu.VMEM((n_tp, GROUP) + hid.shape, hid.dtype),
            pltpu.VMEM((8, count), jnp.float32),
            pltpu.VMEM((GROUP, 8, count), jnp.float32),
            pltpu.VMEM((chunks, depth, wide), w_out.dtype),
            pltpu.VMEM((GROUP, GROUP, slots, count, HD), jnp.bfloat16),
            pltpu.VMEM((GROUP, count, depth), jnp.bfloat16),
            pltpu.VMEM((GROUP, chunks, count, wide), jnp.bfloat16),
            pltpu.VMEM((places, n_tp, count, wide), jnp.bfloat16),
            dma((6 + cuts,)),
            dma((2, n_seq)),
            dma((2, n_seq)),
            dma((GROUP,)),
            dma((GROUP,)),
            dma((GROUP,)),
            dma((GROUP,)),
            dma((GROUP,)),
            dma((GROUP,)),
            dma((GROUP, n_tp)),
            dma((n_tp, GROUP)),
            dma((groups * cuts,)),
            dma((chunks,)),
            dma((GROUP, GROUP)),
            dma((GROUP, GROUP)),
            dma((GROUP, chunks)),
            dma((places, n_tp)),
            dma((chunks,)),
        ],
        compiler_params=pltpu.CompilerParams(
            collective_id=0, has_side_effects=True, vmem_limit_bytes=48 << 20
        ),
        name="fused",
    )(owner, lengths, w_query, w_keyval, pool, hid, w_out, gain, table, route_idx, route_gate)


def paired_kernel(
    n_seq, n_tp, slots,
    owner_ref, lengths_ref, w_query, w_keyval, pool, hid, w_out, gain, table, route_idx, route_gate, out,
    w_all, pre_all, pre_own, hid_all, meta, meta_all, w_outs, normed, acc, att, spread, kept, y_out, y_in, r_out, r_in, f_out, f_in,
    local_sem, w_send, w_recv, p_send, p_recv, h_send, h_recv, m_send, m_recv, t_send, t_recv,
    x_send, x_recv, a_send, a_recv, k_send, k_recv, y_send, y_recv, r_send, r_recv, f_send, f_recv,
):
    groups = n_seq // GROUP
    seq = lax.axis_index("seq")
    tp = lax.axis_index("tp")
    group = seq // GROUP
    base = group * GROUP
    rank = seq % GROUP
    count, width = hid_all.shape[2:]
    experts = w_query.shape[0]
    core = tp % 2
    across_y = tp // 2
    other_core = tp + 1 - 2 * core
    other_y = (tp + 2) % n_tp
    other = (base + GROUP) % n_seq
    half = w_outs.shape[-1]

    def lanes(index):
        return pl.ds(pl.multiple_of(index * HD, HD), HD)

    tokens = lax.broadcasted_iota(jnp.int32, (1, count), 1)
    segment = jnp.zeros((1, count), jnp.int32)
    position = tokens
    end = 0
    for j in range(lengths_ref.shape[1]):
        length = lengths_ref[0, j]
        end = end + length
        past = tokens >= end
        segment = segment + jnp.where(past, 1, 0)
        position = position - jnp.where(past, length, 0)
    meta[0:slots] = route_idx[...].astype(jnp.float32)
    meta[slots : 2 * slots] = route_gate[...]
    meta[4:5] = position.astype(jnp.float32)
    meta[5:6] = segment.astype(jnp.float32)
    meta[6:8] = jnp.zeros((2, count), jnp.float32)

    def member(step):
        return ((group + step // GROUP) % groups) * GROUP + (rank + step % GROUP) % GROUP

    def peer(step):
        return (rank + step) % GROUP

    barrier = pltpu.get_barrier_semaphore()

    def greet(step, carry):
        pl.semaphore_signal(barrier, inc=1, device_id=(member(step), tp), device_id_type=MESH)
        return carry

    lax.fori_loop(1, n_seq, greet, 0)
    for step in range(GROUP):
        for turn in range(1, n_tp):
            pl.semaphore_signal(
                barrier, inc=1, device_id=(base + peer(step), (tp + turn) % n_tp), device_id_type=MESH
            )
    pl.semaphore_signal(barrier, inc=1, device_id=(other + rank, other_y), device_id_type=MESH)
    pl.semaphore_wait(barrier, n_seq + GROUP * (n_tp - 1))

    def hid_copy(step):
        return remote(hid, hid_all.at[tp, rank], h_send.at[step], h_recv.at[rank], (base + peer(step), tp))

    def meta_copy(step):
        return remote(meta, meta_all.at[seq], m_send.at[step], m_recv.at[seq], (member(step), tp))

    beside = rank + 1 - 2 * (rank % 2)
    across = (rank + 2) % GROUP
    owner = owner_ref[group]

    def pool_copy(step):
        if step == 0:
            head, place, partner = beside, 0, beside
        elif step == 1:
            head, place, partner = (beside + 2) % GROUP, 1, beside
        else:
            return remote(
                pre_all.at[3], pre_all.at[2], p_send.at[2], p_recv.at[2], (base + across, tp)
            )
        return remote(
            pool.at[:, :, lanes(head)], pre_all.at[place], p_send.at[step], p_recv.at[step], (base + partner, tp)
        )

    def w_part(part, head, place):
        if part == 0:
            return w_query.at[:, :, lanes(head)], w_all.at[place, 0:experts]
        return w_keyval.at[:, :, lanes(head)], w_all.at[place, experts : experts + 2]

    def w_copy(part, step):
        dest = member(step)
        src, dst = w_part(part, dest % GROUP, seq)
        return remote(src, dst, w_send.at[part, step], w_recv.at[part, seq], (dest, tp))

    def tp_copy(block, src, back, step):
        return remote(
            src, hid_all.at[tp, block], t_send.at[back, step], t_recv.at[tp, back], (seq, (tp + step) % n_tp)
        )

    def out_map_copy(step):
        return remote(
            w_out.at[:, lanes(peer(step))], w_outs.at[rank % 2, core], x_send.at[step], x_recv.at[rank % 2, core],
            (base + peer(step), 2 * across_y + rank // 2),
        )

    def own_map_copy():
        return pltpu.make_async_copy(w_out.at[:, lanes(rank)], w_outs.at[rank % 2, core], local_sem.at[5])

    def w_start(step, carry):
        for part in range(2):
            w_copy(part, step).start()
        return carry

    def w_wait(step, carry):
        source = member(step)
        for part in range(2):
            src, dst = w_part(part, 0, source)
            remote(src, dst, w_send.at[part, step], w_recv.at[part, source], (source, tp)).wait_recv()
        return carry

    for step in range(1, GROUP):
        hid_copy(step).start()
    for step in range(1, n_tp):
        tp_copy(rank, hid, 0, step).start()
    for step in range(1, n_seq):
        meta_copy(step).start()
    for step in (1, 0):
        pool_copy(step).start()
    lax.fori_loop(GROUP, n_seq, w_start, 0)
    lax.fori_loop(1, GROUP, w_start, 0)
    own = [
        pltpu.make_async_copy(hid, hid_all.at[tp, rank], local_sem.at[0]),
        pltpu.make_async_copy(meta, meta_all.at[seq], local_sem.at[1]),
        pltpu.make_async_copy(*w_part(0, rank, seq), local_sem.at[2]),
        pltpu.make_async_copy(*w_part(1, rank, seq), local_sem.at[3]),
        pltpu.make_async_copy(pool.at[:, :, lanes(rank)], pre_own.at[0], local_sem.at[4]),
        pltpu.make_async_copy(pool.at[:, :, lanes(across)], pre_own.at[1], local_sem.at[6]),
    ]
    for copy in own:
        copy.start()

    for back in range(1, GROUP):
        source = (rank + GROUP - back) % GROUP
        remote(hid, hid_all.at[tp, source], h_send.at[back], h_recv.at[source], (base + source, tp)).wait_recv()
        for step in range(1, n_tp):
            tp_copy(source, hid_all.at[tp, source], back, step).start()

    for copy in own:
        copy.wait()
    pool_copy(0).wait_recv()
    pool_copy(1).wait_recv()
    pre_all[3] = jnp.where(owner == rank, pre_own[1], pre_all[1])
    pool_copy(2).start()
    for step in range(1, GROUP):
        out_map_copy(step).start()

    @pl.when(rank // 2 == core)
    def _():
        own_map_copy().start()

    @pl.when(rank // 2 != core)
    def _():
        out_map_copy(0).start()

    near_owner = jnp.where(owner == rank, pre_own[0], pre_all[0])
    pre_own[0] = near_owner
    for step in range(1, n_seq):
        source = member(step)
        remote(meta, meta_all.at[source], m_send.at[step], m_recv.at[source], (source, tp)).wait_recv()
    for back in range(GROUP):
        block = (rank + GROUP - back) % GROUP
        for step in range(1, n_tp):
            source = (tp + step) % n_tp
            remote(
                hid, hid_all.at[source, block], t_send.at[back, step], t_recv.at[source, back], (seq, source)
            ).wait_recv()
    share = n_seq // n_tp

    def normalise(b, carry):
        rows = [hid_all[t, b].astype(jnp.float32) for t in range(n_tp)]
        squares = sum(jnp.sum(x * x, axis=1, keepdims=True) for x in rows)
        inverse = lax.rsqrt(squares * (1.0 / (n_tp * width)) + EPSILON)
        for t in range(n_tp):
            normed[t, b] = (rows[t] * inverse * gain[t]).astype(normed.dtype)
        return carry

    lax.fori_loop(0, GROUP, normalise, 0)

    def project_rows(first, b):
        total = None
        for i in range(n_tp // 2):
            t = first + i
            piece = jnp.concatenate(
                [w_all[pl.ds(t * share, share), e].reshape(width, HD) for e in range(experts + 2)], axis=1
            )
            part = jnp.dot(normed[t, b], piece, preferred_element_type=jnp.float32)
            total = part if total is None else total + part
        return total

    def project_near(b, carry):
        acc[b] = project_rows(group * (n_tp // 2), b)
        return carry

    lax.fori_loop(1, GROUP, w_wait, 0)
    lax.fori_loop(0, GROUP, project_near, 0)
    lax.fori_loop(GROUP, n_seq, w_wait, 0)
    pool_copy(2).wait_recv()
    pre_own[0] = jnp.where(owner // 2 == rank // 2, pre_own[0], pre_all[2])

    def cross_copy(b):
        return remote(att.at[core, 0, b], att.at[core, 1, b], a_send.at[b], a_recv.at[b], (other + rank, tp))

    def core_copy(side, b):
        return remote(
            att.at[core, side, b], att.at[core, side, b], k_send.at[side, b], k_recv.at[side, b], (seq, other_core)
        )

    def core_wait(side, b):
        remote(
            att.at[core, side, b], att.at[1 - core, side, b], k_send.at[side, b], k_recv.at[side, b],
            (seq, other_core),
        ).wait_recv()

    contract = (((1,), (1,)), ((), ()))
    factor = LOG2E * HD ** (-0.5)

    def attend(i, carry):
        b = (rank + 1 + i) % GROUP
        both = acc[b] + project_rows((1 - group) * (n_tp // 2), b)
        row = meta_all[base + b]
        col = row.T
        first = lax.broadcasted_iota(jnp.int32, (count, count), 0)
        second = lax.broadcasted_iota(jnp.int32, (count, count), 1)
        hot = (col[:, 4:5] == second.astype(jnp.float32)).astype(jnp.bfloat16)
        looked = jnp.dot(hot, table[...], preferred_element_type=jnp.float32)
        looked = looked[:, : 2 * HD] + looked[:, 2 * HD : 4 * HD] + looked[:, 4 * HD :]
        cos = looked[:, :HD]
        sin = looked[:, HD:]

        def rotate(value):
            return value * cos + pltpu.roll(value, HD // 2, 1) * sin

        new_key = rotate(both[:, experts * HD : (experts + 1) * HD]).astype(jnp.bfloat16)
        new_value = both[:, (experts + 1) * HD :].astype(jnp.bfloat16)
        seen = (col[:, 5:6] == row[5:6, :]) & (second <= first)
        for k in range(slots):
            index = col[:, k : k + 1]
            chosen = jnp.zeros((count, HD), jnp.float32)
            for e in range(experts):
                chosen = jnp.where(index == float(e), both[:, e * HD : (e + 1) * HD], chosen)
            query = rotate(chosen).astype(jnp.bfloat16)
            far = lax.dot_general(query, pre_own[0, 0], contract, preferred_element_type=jnp.float32)
            near = lax.dot_general(query, new_key, contract, preferred_element_type=jnp.float32)
            near = jnp.where(seen, near, -1e30)
            top = jnp.maximum(jnp.max(far, axis=1, keepdims=True), jnp.max(near, axis=1, keepdims=True))
            far = jnp.exp2((far - top) * factor)
            near = jnp.where(seen, jnp.exp2((near - top) * factor), 0.0)
            total = jnp.sum(far, axis=1, keepdims=True) + jnp.sum(near, axis=1, keepdims=True)
            numer = jnp.dot(far.astype(jnp.bfloat16), pre_own[0, 1], preferred_element_type=jnp.float32)
            numer += jnp.dot(near.astype(jnp.bfloat16), new_value, preferred_element_type=jnp.float32)
            att[core, 0, b, k] = (numer * (col[:, slots + k : slots + k + 1] / total)).astype(jnp.bfloat16)
        cross_copy(b).start()
        core_copy(0, b).start()
        return carry

    def y_copy(side, b):
        return remote(
            y_out.at[side, b], y_in.at[side, b], y_send.at[side, b], y_recv.at[side, b], (seq, other_y)
        )

    def r_copy(side, b):
        return remote(
            r_out.at[side, b], r_in.at[side, rank], r_send.at[side, b], r_recv.at[side, rank], (base + b, tp)
        )

    def f_copy(side):
        return remote(
            f_out.at[side], f_in.at[side, across_y], f_send.at[side], f_recv.at[side, across_y],
            ((base if side == 0 else other) + rank, 2 * group + core),
        )

    def project(side, b):
        col = meta_all[b + (base if side == 0 else other)].T
        depth = experts * HD
        for e in range(experts):
            hot = [(col[:, k : k + 1] == float(e)).astype(jnp.bfloat16) for k in range(slots)]
            for s in range(2):
                spread[side, :, s * depth + e * HD : s * depth + (e + 1) * HD] = sum(
                    att[s, side, b, k] * hot[k] for k in range(slots)
                )
        y_out[side, b] = jnp.dot(
            spread[side], w_outs[1 - across_y].reshape(2 * depth, half), preferred_element_type=jnp.float32
        ).astype(y_out.dtype)
        y_copy(side, b).start()
        kept[side, b] = jnp.dot(
            spread[side], w_outs[across_y].reshape(2 * depth, half), preferred_element_type=jnp.float32
        )

    def reduce(side, b):
        y_copy(side, b).wait_recv()
        return kept[side, b] + y_in[side, b].astype(jnp.float32)

    def map_wait():
        for place in range(2):
            for source_core in range(2):
                from_rank = 2 * core + place
                mine = (from_rank == rank) & (source_core == core)

                @pl.when(mine)
                def _():
                    own_map_copy().wait()

                @pl.when(jnp.logical_not(mine))
                def _():
                    remote(
                        w_out.at[:, lanes(rank)], w_outs.at[place, source_core], x_send.at[0],
                        x_recv.at[place, source_core], (base + from_rank, 2 * across_y + source_core),
                    ).wait_recv()

    def near(i, carry):
        b = (rank + 1 + i) % GROUP
        core_wait(0, b)
        project(0, b)
        return carry

    def both(i, carry):
        attend(i, carry)

        return carry

    lax.fori_loop(0, GROUP, both, 0)
    map_wait()
    lax.fori_loop(0, GROUP, near, 0)

    def scatter(side, i):
        b = (rank + 1 + i) % GROUP
        r_out[side, b] = reduce(side, b).astype(r_out.dtype)
        r_copy(side, b).start()

    def finish(side):
        total = reduce(side, rank)
        for step in range(1, GROUP):
            source = peer(step)
            remote(
                r_out.at[side, rank], r_in.at[side, source], r_send.at[side, rank], r_recv.at[side, source],
                (base + source, tp),
            ).wait_recv()
            total = total + r_in[side, source].astype(jnp.float32)
        f_out[side] = total.astype(f_out.dtype)

    def far(i, carry):
        b = (rank + 1 + i) % GROUP
        cross_copy(b).wait_recv()
        core_copy(1, b).start()

        @pl.when(i < GROUP - 1)
        def _():
            scatter(0, i)

        core_wait(1, b)
        project(1, b)

        @pl.when(i > 0)
        def _():
            scatter(1, i - 1)

        return carry

    lax.fori_loop(0, GROUP, far, 0)
    finish(0)

    @pl.when(across_y != group)
    def _():
        f_copy(0).start()

    finish(1)
    f_copy(1).start()

    for step in range(1, GROUP):
        hid_copy(step).wait_send()
        for side in range(2):
            r_copy(side, peer(step)).wait_send()
        out_map_copy(step).wait_send()
    for step in range(1, n_seq):
        meta_copy(step).wait_send()

    @pl.when(rank // 2 != core)
    def _():
        out_map_copy(0).wait_send()

    for b in range(GROUP):
        cross_copy(b).wait_send()
        core_copy(0, b).wait_send()
        core_copy(1, b).wait_send()
        for side in range(2):
            y_copy(side, b).wait_send()

    for step in range(3):
        pool_copy(step).wait_send()

    def w_sent(step, carry):
        for part in range(2):
            w_copy(part, step).wait_send()
        return carry

    lax.fori_loop(1, n_seq, w_sent, 0)
    for back in range(GROUP):
        for step in range(1, n_tp):
            tp_copy((rank + GROUP - back) % GROUP, hid, back, step).wait_send()

    def land(side, y, column):
        remote(
            f_out.at[0], f_in.at[side, y], f_send.at[0], f_recv.at[side, y],
            (seq if side == 0 else other + rank, 2 * y + core),
        ).wait_recv()
        out[:, column * half : (column + 1) * half] = f_in[side, y]

    @pl.when(across_y == group)
    def _():
        for y in range(2):
            @pl.when(across_y == y)
            def _():
                out[:, y * half : (y + 1) * half] = f_out[0]

            @pl.when(across_y != y)
            def _():
                land(0, y, y)

    @pl.when(across_y != group)
    def _():
        for y in range(2):
            land(1, y, y)
        f_copy(0).wait_send()

    f_copy(1).wait_send()


def paired(n_seq, n_tp, owner, lengths, w_query, w_keyval, pool, hid, w_out, gain, table, route_idx, route_gate):
    count, width = hid.shape
    slots = route_idx.shape[0]
    experts, rows, _ = w_query.shape
    half = w_out.shape[-1]
    dma = pltpu.SemaphoreType.DMA
    vmem = pl.BlockSpec(memory_space=pltpu.VMEM)
    smem = pl.BlockSpec(memory_space=pltpu.SMEM)
    low = jnp.bfloat16
    return pl.pallas_call(
        functools.partial(paired_kernel, n_seq, n_tp, slots),
        out_shape=jax.ShapeDtypeStruct((count, width), low),
        in_specs=[smem] * 2 + [ANY] * 5 + [vmem] * 4,
        out_specs=vmem,
        scratch_shapes=[
            pltpu.VMEM((n_seq, experts + 2, rows, HD), w_query.dtype),
            pltpu.VMEM((4, 2, pool.shape[1], HD), pool.dtype),
            pltpu.VMEM((2, 2, pool.shape[1], HD), pool.dtype),
            pltpu.VMEM((n_tp, GROUP) + hid.shape, hid.dtype),
            pltpu.VMEM((8, count), jnp.float32),
            pltpu.VMEM((n_seq, 8, count), jnp.float32),
            pltpu.VMEM((2, 2, experts, HD, half), w_out.dtype),
            pltpu.VMEM((n_tp, GROUP) + hid.shape, low),
            pltpu.VMEM((GROUP, count, (experts + 2) * HD), jnp.float32),
            pltpu.VMEM((2, 2, GROUP, slots, count, HD), low),
            pltpu.VMEM((2, count, 2 * experts * HD), low),
            pltpu.VMEM((2, GROUP, count, half), jnp.float32),
            pltpu.VMEM((2, GROUP, count, half), low),
            pltpu.VMEM((2, GROUP, count, half), low),
            pltpu.VMEM((2, GROUP, count, half), low),
            pltpu.VMEM((2, GROUP, count, half), low),
            pltpu.VMEM((2, count, half), low),
            pltpu.VMEM((2, 2, count, half), low),
            dma((7,)),
            dma((2, n_seq)),
            dma((2, n_seq)),
            dma((GROUP,)),
            dma((GROUP,)),
            dma((GROUP,)),
            dma((GROUP,)),
            dma((n_seq,)),
            dma((n_seq,)),
            dma((GROUP, n_tp)),
            dma((n_tp, GROUP)),
            dma((GROUP,)),
            dma((2, 2)),
            dma((GROUP,)),
            dma((GROUP,)),
            dma((2, GROUP)),
            dma((2, GROUP)),
            dma((2, GROUP)),
            dma((2, GROUP)),
            dma((2, GROUP)),
            dma((2, GROUP)),
            dma((2,)),
            dma((2, 2)),
        ],
        compiler_params=pltpu.CompilerParams(
            collective_id=0, has_side_effects=True, vmem_limit_bytes=48 << 20
        ),
        name="paired",
    )(owner, lengths, w_query, w_keyval, pool, hid, w_out, gain, table, route_idx, route_gate)


def rope_table(count, prefix):
    freqs = np.float32(THETA) ** (-(np.arange(HD // 2, dtype=np.float32) * np.float32(2.0)) / np.float32(HD))
    angles = (np.arange(count) + prefix).astype(np.float32)[:, None] * freqs[None, :].astype(np.float32)
    cosine = np.cos(angles.astype(np.float64))
    sine = np.sin(angles.astype(np.float64))
    rest = np.concatenate([cosine, cosine, -sine, sine], axis=1).astype(np.float32)
    parts = []
    for _ in range(3):
        part = rest.astype(ml_dtypes.bfloat16)
        parts.append(part)
        rest = rest - part.astype(np.float32)
    return np.concatenate(parts, axis=1)


def per_device(
    n_seq, n_tp, hidden, lengths, cache_owner, cache_pool, norm_gain, route_idx, route_gate,
    w_query, w_keyval, w_out,
):
    groups = n_seq // GROUP
    count = hidden.shape[0]
    rows, experts, width = w_query.shape
    prefix = cache_pool.shape[1]
    assert width == GROUP * HD
    wide = w_out.shape[2]
    merged = wide < HD
    if n_seq == 2 * GROUP and n_tp == 4:
        return paired(
            n_seq, n_tp, cache_owner, lengths, w_query.swapaxes(0, 1), w_keyval.swapaxes(0, 1),
            cache_pool[0].swapaxes(0, 1), hidden, w_out, norm_gain.reshape(n_tp, 1, -1),
            jnp.asarray(rope_table(count, prefix)), route_idx.T, route_gate.T,
        )
    if merged:
        same_rank = [[g * GROUP + r for g in range(groups)] for r in range(GROUP)]
        per = groups // n_tp
        w_out = lax.all_gather(w_out, "seq", axis=0, axis_index_groups=same_rank)
        w_out = w_out.reshape(n_tp, per, experts, width, wide).transpose(0, 2, 3, 1, 4)
        w_out = w_out.reshape(n_tp, experts * width, per * wide)
    else:
        w_out = w_out.reshape(experts * width, wide)
    out = fused(
        n_seq, n_tp, merged, cache_owner, lengths, w_query.swapaxes(0, 1), w_keyval.swapaxes(0, 1),
        cache_pool[0].swapaxes(0, 1), hidden, w_out, norm_gain.reshape(n_tp, 1, -1),
        jnp.asarray(rope_table(count, prefix)), route_idx.T, route_gate.T,
    )
    if merged:
        out = out.reshape(count, GROUP, groups // n_tp, wide).transpose(0, 2, 1, 3).reshape(count, -1)
    return out


def solution(mesh):
    placed = (
        P("seq", "tp"),
        P("seq", None),
        P(),
        P("seq", None, None, "tp"),
        P(),
        P("seq", None),
        P("seq", None),
        P("seq", None, "tp"),
        P("seq", None, "tp"),
        P(None, "tp", "seq"),
    )
    body = functools.partial(per_device, mesh.shape["seq"], mesh.shape["tp"])
    return jax.shard_map(body, mesh=mesh, in_specs=placed, out_specs=P("seq", "tp"), check_vma=False)
```

```python
import functools

import jax
import jax.numpy as jnp
import ml_dtypes
import numpy as np
from jax import lax
from jax.experimental import pallas as pl
from jax.experimental.pallas import tpu as pltpu
from jax.sharding import PartitionSpec as P

HD = 128
GROUP = 4
EPSILON = 1e-05
THETA = 10000.0
LOG2E = 1.4426950408889634
MESH = pl.DeviceIdType.MESH
ANY = pl.BlockSpec(memory_space=pl.ANY)


def remote(src, dst, send_sem, recv_sem, device):
    return pltpu.make_async_remote_copy(
        src_ref=src,
        dst_ref=dst,
        send_sem=send_sem,
        recv_sem=recv_sem,
        device_id=device,
        device_id_type=MESH,
    )


def fused_kernel(
    n_seq, n_tp, slots, merged,
    owner_ref, lengths_ref, w_query, w_keyval, pool, hid, w_out, gain, table, route_idx, route_gate, out,
    w_all, pre_all, pre_own, hid_all, meta, meta_all, w_outs, gathered, spread, staged, landed,
    local_sem, w_send, w_recv, p_send, p_recv, h_send, h_recv, m_send, m_recv, t_send, t_recv,
    x_send, x_recv, a_send, a_recv, o_send, o_recv, o_local,
):
    groups = n_seq // GROUP
    seq = lax.axis_index("seq")
    tp = lax.axis_index("tp")
    group = seq // GROUP
    base = group * GROUP
    rank = seq % GROUP
    count, width = hid_all.shape[2:]
    experts = w_query.shape[0]
    chunks, _, wide = w_outs.shape
    places = landed.shape[0]
    cuts = chunks // groups

    def lanes(index):
        return pl.ds(pl.multiple_of(index * HD, HD), HD)

    tokens = lax.broadcasted_iota(jnp.int32, (1, count), 1)
    segment = jnp.zeros((1, count), jnp.int32)
    position = tokens
    end = 0
    for j in range(lengths_ref.shape[1]):
        length = lengths_ref[0, j]
        end = end + length
        past = tokens >= end
        segment = segment + jnp.where(past, 1, 0)
        position = position - jnp.where(past, length, 0)
    meta[0:slots] = route_idx[...].astype(jnp.float32)
    meta[slots : 2 * slots] = route_gate[...]
    meta[4:5] = position.astype(jnp.float32)
    meta[5:6] = segment.astype(jnp.float32)
    meta[6:8] = jnp.zeros((2, count), jnp.float32)

    def member(step):
        return ((group + step // GROUP) % groups) * GROUP + (rank + step % GROUP) % GROUP

    def peer(step):
        return (rank + step) % GROUP

    barrier = pltpu.get_barrier_semaphore()

    def greet(step, carry):
        pl.semaphore_signal(barrier, inc=1, device_id=(member(step), tp), device_id_type=MESH)
        return carry

    lax.fori_loop(1, n_seq, greet, 0)
    for step in range(GROUP):
        for turn in range(1, n_tp):
            pl.semaphore_signal(
                barrier, inc=1, device_id=(base + peer(step), (tp + turn) % n_tp), device_id_type=MESH
            )
    pl.semaphore_wait(barrier, n_seq - 1 + GROUP * (n_tp - 1))

    def hid_copy(step):
        return remote(hid, hid_all.at[tp, rank], h_send.at[step], h_recv.at[rank], (base + peer(step), tp))

    def meta_copy(step):
        return remote(meta, meta_all.at[rank], m_send.at[step], m_recv.at[rank], (base + peer(step), tp))

    beside = rank + 1 - 2 * (rank % 2)
    across = (rank + 2) % GROUP
    owner = owner_ref[group]

    def pool_copy(step):
        if step == 0:
            head, place, partner = beside, 0, beside
        elif step == 1:
            head, place, partner = (beside + 2) % GROUP, 1, beside
        else:
            return remote(
                pre_all.at[3], pre_all.at[2], p_send.at[2], p_recv.at[2], (base + across, tp)
            )
        return remote(
            pool.at[:, :, lanes(head)], pre_all.at[place], p_send.at[step], p_recv.at[step], (base + partner, tp)
        )

    def w_part(part, head, place):
        if part == 0:
            return w_query.at[:, :, lanes(head)], w_all.at[place, 0:experts]
        return w_keyval.at[:, :, lanes(head)], w_all.at[place, experts : experts + 2]

    def w_copy(part, step):
        dest = member(step)
        src, dst = w_part(part, dest % GROUP, seq)
        return remote(src, dst, w_send.at[part, step], w_recv.at[part, seq], (dest, tp))

    def tp_copy(block, src, back, step):
        return remote(
            src, hid_all.at[tp, block], t_send.at[back, step], t_recv.at[tp, back], (seq, (tp + step) % n_tp)
        )

    def out_map_copy(step, cut):
        dest = ((group + step) % groups) * GROUP + rank
        chunk = group * cuts + cut
        return remote(
            w_out.at[:, cut * wide : (cut + 1) * wide], w_outs.at[chunk],
            x_send.at[step * cuts + cut], x_recv.at[chunk], (dest, tp),
        )

    def w_start(step, carry):
        for part in range(2):
            w_copy(part, step).start()
        return carry

    def w_wait(step, carry):
        source = member(step)
        for part in range(2):
            src, dst = w_part(part, 0, source)
            remote(src, dst, w_send.at[part, step], w_recv.at[part, source], (source, tp)).wait_recv()
        return carry

    for step in range(1, GROUP):
        hid_copy(step).start()
    for step in range(1, n_tp):
        tp_copy(rank, hid, 0, step).start()
    for step in range(1, GROUP):
        meta_copy(step).start()
    for step in (1, 0):
        pool_copy(step).start()
    lax.fori_loop(GROUP, n_seq, w_start, 0)
    lax.fori_loop(1, GROUP, w_start, 0)
    own = [
        pltpu.make_async_copy(hid, hid_all.at[tp, rank], local_sem.at[0]),
        pltpu.make_async_copy(meta, meta_all.at[rank], local_sem.at[1]),
        pltpu.make_async_copy(*w_part(0, rank, seq), local_sem.at[2]),
        pltpu.make_async_copy(*w_part(1, rank, seq), local_sem.at[3]),
        pltpu.make_async_copy(pool.at[:, :, lanes(rank)], pre_own.at[0], local_sem.at[4]),
        pltpu.make_async_copy(pool.at[:, :, lanes(across)], pre_own.at[1], local_sem.at[5 + cuts]),
    ]
    if merged:
        own.append(pltpu.make_async_copy(w_out, w_outs, local_sem.at[5]))
    else:
        for cut in range(cuts):
            own.append(
                pltpu.make_async_copy(
                    w_out.at[:, cut * wide : (cut + 1) * wide],
                    w_outs.at[group * cuts + cut],
                    local_sem.at[5 + cut],
                )
            )
    for copy in own:
        copy.start()

    for back in range(1, GROUP):
        source = (rank + GROUP - back) % GROUP
        remote(hid, hid_all.at[tp, source], h_send.at[back], h_recv.at[source], (base + source, tp)).wait_recv()
        for step in range(1, n_tp):
            tp_copy(source, hid_all.at[tp, source], back, step).start()

    for copy in own:
        copy.wait()
    pool_copy(0).wait_recv()
    pool_copy(1).wait_recv()
    pre_all[3] = jnp.where(owner == rank, pre_own[1], pre_all[1])
    pool_copy(2).start()
    near_owner = jnp.where(owner == rank, pre_own[0], pre_all[0])
    pre_own[0] = near_owner
    lax.fori_loop(GROUP, n_seq, w_wait, 0)
    if not merged:
        for cut in range(cuts):
            for step in range(1, groups):
                out_map_copy(step, cut).start()
    for step in range(1, GROUP):
        source = peer(step)
        from_peer = (base + source, tp)
        remote(meta, meta_all.at[source], m_send.at[step], m_recv.at[source], from_peer).wait_recv()
    for back in range(GROUP):
        block = (rank + GROUP - back) % GROUP
        for step in range(1, n_tp):
            source = (tp + step) % n_tp
            remote(
                hid, hid_all.at[source, block], t_send.at[back, step], t_recv.at[source, back], (seq, source)
            ).wait_recv()
    lax.fori_loop(1, GROUP, w_wait, 0)
    pool_copy(2).wait_recv()
    pre_own[0] = jnp.where(owner // 2 == rank // 2, pre_own[0], pre_all[2])

    def att_copy(b, step):
        return remote(
            gathered.at[rank, b], gathered.at[rank, b], a_send.at[b, step], a_recv.at[rank, b],
            (base + peer(step), tp),
        )

    share = n_seq // n_tp
    contract = (((1,), (1,)), ((), ()))
    factor = LOG2E * HD ** (-0.5)

    def attend(b, carry):
        rows = [hid_all[t, b].astype(jnp.float32) for t in range(n_tp)]
        squares = sum(jnp.sum(x * x, axis=1, keepdims=True) for x in rows)
        inverse = lax.rsqrt(squares * (1.0 / (n_tp * width)) + EPSILON)
        acc = None
        for t in range(n_tp):
            normed = (rows[t] * inverse * gain[t]).astype(jnp.bfloat16)
            piece = jnp.concatenate(
                [w_all[t * share : (t + 1) * share, e].reshape(width, HD) for e in range(experts + 2)], axis=1
            )
            part = jnp.dot(normed, piece, preferred_element_type=jnp.float32)
            acc = part if acc is None else acc + part
        row = meta_all[b]
        col = row.T
        first = lax.broadcasted_iota(jnp.int32, (count, count), 0)
        second = lax.broadcasted_iota(jnp.int32, (count, count), 1)
        hot = (col[:, 4:5] == second.astype(jnp.float32)).astype(jnp.bfloat16)
        looked = jnp.dot(hot, table[...], preferred_element_type=jnp.float32)
        looked = looked[:, : 2 * HD] + looked[:, 2 * HD : 4 * HD] + looked[:, 4 * HD :]
        cos = looked[:, :HD]
        sin = looked[:, HD:]

        def rotate(value):
            return value * cos + pltpu.roll(value, HD // 2, 1) * sin

        new_key = rotate(acc[:, experts * HD : (experts + 1) * HD]).astype(jnp.bfloat16)
        new_value = acc[:, (experts + 1) * HD :].astype(jnp.bfloat16)
        seen = (col[:, 5:6] == row[5:6, :]) & (second <= first)
        for k in range(slots):
            index = col[:, k : k + 1]
            chosen = jnp.zeros((count, HD), jnp.float32)
            for e in range(experts):
                chosen = jnp.where(index == float(e), acc[:, e * HD : (e + 1) * HD], chosen)
            query = rotate(chosen).astype(jnp.bfloat16)
            far = lax.dot_general(query, pre_own[0, 0], contract, preferred_element_type=jnp.float32)
            near = lax.dot_general(query, new_key, contract, preferred_element_type=jnp.float32)
            near = jnp.where(seen, near, -1e30)
            top = jnp.maximum(jnp.max(far, axis=1, keepdims=True), jnp.max(near, axis=1, keepdims=True))
            far = jnp.exp2((far - top) * factor)
            near = jnp.where(seen, jnp.exp2((near - top) * factor), 0.0)
            total = jnp.sum(far, axis=1, keepdims=True) + jnp.sum(near, axis=1, keepdims=True)
            numer = jnp.dot(far.astype(jnp.bfloat16), pre_own[0, 1], preferred_element_type=jnp.float32)
            numer += jnp.dot(near.astype(jnp.bfloat16), new_value, preferred_element_type=jnp.float32)
            gathered[rank, b, k] = (numer * (col[:, slots + k : slots + k + 1] / total)).astype(jnp.bfloat16)
        for step in range(1, GROUP):
            att_copy(b, step).start()
        return carry

    lax.fori_loop(0, GROUP, attend, 0)

    def target(c):
        if merged:
            return c, rank
        feature = (c // cuts) * GROUP + rank
        return feature // groups, (feature % groups) * cuts + c % cuts

    def out_copy(b, c):
        column, place = target(c)
        return remote(
            staged.at[b, c], landed.at[place, tp], o_send.at[b, c], o_recv.at[place, tp], (base + b, column)
        )

    def own_copy(b, c):
        column, place = target(c)
        return pltpu.make_async_copy(staged.at[b, c], landed.at[place, tp], o_local.at[c])

    def is_own(b, c):
        return (b == rank) & (target(c)[0] == tp)

    def expand(i, carry):
        b = (rank + 1 + i) % GROUP
        for step in range(1, GROUP):
            source = peer(step)
            remote(
                gathered.at[rank, b], gathered.at[source, b], a_send.at[b, step], a_recv.at[source, b],
                (base + source, tp),
            ).wait_recv()
        col = meta_all[b].T
        depth = GROUP * HD
        for e in range(experts):
            hot = [(col[:, k : k + 1] == float(e)).astype(jnp.bfloat16) for k in range(slots)]
            for s in range(GROUP):
                spread[b, :, e * depth + s * HD : e * depth + (s + 1) * HD] = sum(
                    gathered[s, b, k] * hot[k] for k in range(slots)
                )
        return carry

    lax.fori_loop(0, GROUP, expand, 0)

    for j in range(chunks):
        c = j if merged else (group * cuts + j) % chunks
        if not merged and j >= cuts:
            remote(
                w_out.at[:, 0:wide], w_outs.at[c], x_send.at[0], x_recv.at[c], ((c // cuts) * GROUP + rank, tp)
            ).wait_recv()

        def project(i, carry):
            b = (rank + 1 + i) % GROUP
            staged[b, c] = jnp.dot(spread[b], w_outs[c], preferred_element_type=jnp.float32).astype(
                staged.dtype
            )

            @pl.when(is_own(b, c))
            def _():
                own_copy(b, c).start()

            @pl.when(jnp.logical_not(is_own(b, c)))
            def _():
                out_copy(b, c).start()

            return carry

        lax.fori_loop(0, GROUP, project, 0)

    for step in range(1, GROUP):
        hid_copy(step).wait_send()
        meta_copy(step).wait_send()
        for b in range(GROUP):
            att_copy(b, step).wait_send()

    for step in range(3):
        pool_copy(step).wait_send()

    def w_sent(step, carry):
        for part in range(2):
            w_copy(part, step).wait_send()
        return carry

    lax.fori_loop(1, n_seq, w_sent, 0)
    for back in range(GROUP):
        for step in range(1, n_tp):
            tp_copy((rank + GROUP - back) % GROUP, hid, back, step).wait_send()
    if not merged:
        for cut in range(cuts):
            for step in range(1, groups):
                out_map_copy(step, cut).wait_send()

    for place in range(places):
        if merged:
            source_rank, chunk = place, tp
        else:
            feature = tp * groups + place // cuts
            source_rank, chunk = feature % GROUP, (feature // GROUP) * cuts + place % cuts
        total = None
        for t in range(n_tp):
            mine = (source_rank == rank) & (tp == t)

            @pl.when(mine)
            def _():
                pltpu.make_async_copy(
                    staged.at[rank, chunk], landed.at[place, t], o_local.at[chunk]
                ).wait()

            @pl.when(jnp.logical_not(mine))
            def _():
                remote(
                    staged.at[0, 0], landed.at[place, t], o_send.at[0, 0], o_recv.at[place, t],
                    (base + source_rank, t),
                ).wait_recv()

            value = landed[place, t].astype(jnp.float32)
            total = value if total is None else total + value
        out[:, place * wide : (place + 1) * wide] = total.astype(out.dtype)

    for b in range(GROUP):
        for c in range(chunks):

            @pl.when(jnp.logical_not(is_own(b, c)))
            def _():
                out_copy(b, c).wait_send()


def fused(
    n_seq, n_tp, merged, owner, lengths, w_query, w_keyval, pool, hid, w_out, gain, table, route_idx, route_gate
):
    groups = n_seq // GROUP
    count = hid.shape[0]
    slots = route_idx.shape[0]
    experts, rows, _ = w_query.shape
    depth = w_out.shape[-2]
    dma = pltpu.SemaphoreType.DMA
    vmem = pl.BlockSpec(memory_space=pltpu.VMEM)
    smem = pl.BlockSpec(memory_space=pltpu.SMEM)
    wide = HD
    cuts = 1 if merged else w_out.shape[1] // wide
    chunks = w_out.shape[0] if merged else groups * cuts
    places = GROUP if merged else groups * cuts
    return pl.pallas_call(
        functools.partial(fused_kernel, n_seq, n_tp, slots, merged),
        out_shape=jax.ShapeDtypeStruct((count, places * wide), jnp.bfloat16),
        in_specs=[smem] * 2 + [ANY] * 5 + [vmem] * 4,
        out_specs=vmem,
        scratch_shapes=[
            pltpu.VMEM((n_seq, experts + 2, rows, HD), w_query.dtype),
            pltpu.VMEM((4, 2, pool.shape[1], HD), pool.dtype),
            pltpu.VMEM((2, 2, pool.shape[1], HD), pool.dtype),
            pltpu.VMEM((n_tp, GROUP) + hid.shape, hid.dtype),
            pltpu.VMEM((8, count), jnp.float32),
            pltpu.VMEM((GROUP, 8, count), jnp.float32),
            pltpu.VMEM((chunks, depth, wide), w_out.dtype),
            pltpu.VMEM((GROUP, GROUP, slots, count, HD), jnp.bfloat16),
            pltpu.VMEM((GROUP, count, depth), jnp.bfloat16),
            pltpu.VMEM((GROUP, chunks, count, wide), jnp.bfloat16),
            pltpu.VMEM((places, n_tp, count, wide), jnp.bfloat16),
            dma((6 + cuts,)),
            dma((2, n_seq)),
            dma((2, n_seq)),
            dma((GROUP,)),
            dma((GROUP,)),
            dma((GROUP,)),
            dma((GROUP,)),
            dma((GROUP,)),
            dma((GROUP,)),
            dma((GROUP, n_tp)),
            dma((n_tp, GROUP)),
            dma((groups * cuts,)),
            dma((chunks,)),
            dma((GROUP, GROUP)),
            dma((GROUP, GROUP)),
            dma((GROUP, chunks)),
            dma((places, n_tp)),
            dma((chunks,)),
        ],
        compiler_params=pltpu.CompilerParams(
            collective_id=0, has_side_effects=True, vmem_limit_bytes=48 << 20
        ),
        name="fused",
    )(owner, lengths, w_query, w_keyval, pool, hid, w_out, gain, table, route_idx, route_gate)


def paired_kernel(
    n_seq, n_tp, slots,
    owner_ref, lengths_ref, w_query, w_keyval, pool, hid, w_out, gain, table, route_idx, route_gate, out,
    w_all, pre_all, pre_own, hid_all, meta, meta_all, w_outs, normed, acc, att, spread, kept, y_out, y_in, r_out, r_in, f_out, f_in,
    local_sem, w_send, w_recv, p_send, p_recv, h_send, h_recv, m_send, m_recv, t_send, t_recv,
    x_send, x_recv, a_send, a_recv, k_send, k_recv, y_send, y_recv, r_send, r_recv, f_send, f_recv,
):
    groups = n_seq // GROUP
    seq = lax.axis_index("seq")
    tp = lax.axis_index("tp")
    group = seq // GROUP
    base = group * GROUP
    rank = seq % GROUP
    count, width = hid_all.shape[2:]
    experts = w_query.shape[0]
    core = tp % 2
    across_y = tp // 2
    other_core = tp + 1 - 2 * core
    other_y = (tp + 2) % n_tp
    other = (base + GROUP) % n_seq
    half = w_outs.shape[-1]

    def lanes(index):
        return pl.ds(pl.multiple_of(index * HD, HD), HD)

    tokens = lax.broadcasted_iota(jnp.int32, (1, count), 1)
    segment = jnp.zeros((1, count), jnp.int32)
    position = tokens
    end = 0
    for j in range(lengths_ref.shape[1]):
        length = lengths_ref[0, j]
        end = end + length
        past = tokens >= end
        segment = segment + jnp.where(past, 1, 0)
        position = position - jnp.where(past, length, 0)
    meta[0:slots] = route_idx[...].astype(jnp.float32)
    meta[slots : 2 * slots] = route_gate[...]
    meta[4:5] = position.astype(jnp.float32)
    meta[5:6] = segment.astype(jnp.float32)
    meta[6:8] = jnp.zeros((2, count), jnp.float32)

    def member(step):
        return ((group + step // GROUP) % groups) * GROUP + (rank + step % GROUP) % GROUP

    def peer(step):
        return (rank + step) % GROUP

    barrier = pltpu.get_barrier_semaphore()

    def greet(step, carry):
        pl.semaphore_signal(barrier, inc=1, device_id=(member(step), tp), device_id_type=MESH)
        return carry

    lax.fori_loop(1, n_seq, greet, 0)
    for step in range(GROUP):
        for turn in range(1, n_tp):
            pl.semaphore_signal(
                barrier, inc=1, device_id=(base + peer(step), (tp + turn) % n_tp), device_id_type=MESH
            )
    pl.semaphore_signal(barrier, inc=1, device_id=(other + rank, other_y), device_id_type=MESH)
    pl.semaphore_wait(barrier, n_seq + GROUP * (n_tp - 1))

    def hid_copy(step):
        return remote(hid, hid_all.at[tp, rank], h_send.at[step], h_recv.at[rank], (base + peer(step), tp))

    def meta_copy(step):
        return remote(meta, meta_all.at[seq], m_send.at[step], m_recv.at[seq], (member(step), tp))

    beside = rank + 1 - 2 * (rank % 2)
    across = (rank + 2) % GROUP
    owner = owner_ref[group]

    def pool_copy(step):
        if step == 0:
            head, place, partner = beside, 0, beside
        elif step == 1:
            head, place, partner = (beside + 2) % GROUP, 1, beside
        else:
            return remote(
                pre_all.at[3], pre_all.at[2], p_send.at[2], p_recv.at[2], (base + across, tp)
            )
        return remote(
            pool.at[:, :, lanes(head)], pre_all.at[place], p_send.at[step], p_recv.at[step], (base + partner, tp)
        )

    def w_part(part, head, place):
        if part == 0:
            return w_query.at[:, :, lanes(head)], w_all.at[place, 0:experts]
        return w_keyval.at[:, :, lanes(head)], w_all.at[place, experts : experts + 2]

    def w_copy(part, step):
        dest = member(step)
        src, dst = w_part(part, dest % GROUP, seq)
        return remote(src, dst, w_send.at[part, step], w_recv.at[part, seq], (dest, tp))

    def tp_copy(block, src, back, step):
        return remote(
            src, hid_all.at[tp, block], t_send.at[back, step], t_recv.at[tp, back], (seq, (tp + step) % n_tp)
        )

    def out_map_copy(step):
        return remote(
            w_out.at[:, lanes(peer(step))], w_outs.at[rank % 2, core], x_send.at[step], x_recv.at[rank % 2, core],
            (base + peer(step), 2 * across_y + rank // 2),
        )

    def own_map_copy():
        return pltpu.make_async_copy(w_out.at[:, lanes(rank)], w_outs.at[rank % 2, core], local_sem.at[5])

    def w_start(step, carry):
        for part in range(2):
            w_copy(part, step).start()
        return carry

    def w_wait(step, carry):
        source = member(step)
        for part in range(2):
            src, dst = w_part(part, 0, source)
            remote(src, dst, w_send.at[part, step], w_recv.at[part, source], (source, tp)).wait_recv()
        return carry

    lax.fori_loop(GROUP, n_seq, w_start, 0)
    for step in range(1, GROUP):
        hid_copy(step).start()
    for step in range(1, n_tp):
        tp_copy(rank, hid, 0, step).start()
    for step in range(1, n_seq):
        meta_copy(step).start()
    for step in (1, 0):
        pool_copy(step).start()
    lax.fori_loop(1, GROUP, w_start, 0)
    own = [
        pltpu.make_async_copy(hid, hid_all.at[tp, rank], local_sem.at[0]),
        pltpu.make_async_copy(meta, meta_all.at[seq], local_sem.at[1]),
        pltpu.make_async_copy(*w_part(0, rank, seq), local_sem.at[2]),
        pltpu.make_async_copy(*w_part(1, rank, seq), local_sem.at[3]),
        pltpu.make_async_copy(pool.at[:, :, lanes(rank)], pre_own.at[0], local_sem.at[4]),
        pltpu.make_async_copy(pool.at[:, :, lanes(across)], pre_own.at[1], local_sem.at[6]),
    ]
    for copy in own:
        copy.start()

    for back in range(1, GROUP):
        source = (rank + GROUP - back) % GROUP
        remote(hid, hid_all.at[tp, source], h_send.at[back], h_recv.at[source], (base + source, tp)).wait_recv()
        for step in range(1, n_tp):
            tp_copy(source, hid_all.at[tp, source], back, step).start()

    for copy in own:
        copy.wait()
    pool_copy(0).wait_recv()
    pool_copy(1).wait_recv()
    pre_all[3] = jnp.where(owner == rank, pre_own[1], pre_all[1])
    pool_copy(2).start()
    for step in range(1, GROUP):
        out_map_copy(step).start()

    @pl.when(rank // 2 == core)
    def _():
        own_map_copy().start()

    @pl.when(rank // 2 != core)
    def _():
        out_map_copy(0).start()

    near_owner = jnp.where(owner == rank, pre_own[0], pre_all[0])
    pre_own[0] = near_owner
    for step in range(1, n_seq):
        source = member(step)
        remote(meta, meta_all.at[source], m_send.at[step], m_recv.at[source], (source, tp)).wait_recv()
    for back in range(GROUP):
        block = (rank + GROUP - back) % GROUP
        for step in range(1, n_tp):
            source = (tp + step) % n_tp
            remote(
                hid, hid_all.at[source, block], t_send.at[back, step], t_recv.at[source, back], (seq, source)
            ).wait_recv()
    share = n_seq // n_tp

    def normalise(b, carry):
        rows = [hid_all[t, b].astype(jnp.float32) for t in range(n_tp)]
        squares = sum(jnp.sum(x * x, axis=1, keepdims=True) for x in rows)
        inverse = lax.rsqrt(squares * (1.0 / (n_tp * width)) + EPSILON)
        for t in range(n_tp):
            normed[t, b] = (rows[t] * inverse * gain[t]).astype(normed.dtype)
        return carry

    lax.fori_loop(0, GROUP, normalise, 0)

    def project_rows(first, b):
        total = None
        for i in range(n_tp // 2):
            t = first + i
            piece = jnp.concatenate(
                [w_all[pl.ds(t * share, share), e].reshape(width, HD) for e in range(experts + 2)], axis=1
            )
            part = jnp.dot(normed[t, b], piece, preferred_element_type=jnp.float32)
            total = part if total is None else total + part
        return total

    def project_near(b, carry):
        acc[b] = project_rows(group * (n_tp // 2), b)
        return carry

    lax.fori_loop(1, GROUP, w_wait, 0)
    lax.fori_loop(0, GROUP, project_near, 0)
    lax.fori_loop(GROUP, n_seq, w_wait, 0)
    pool_copy(2).wait_recv()
    pre_own[0] = jnp.where(owner // 2 == rank // 2, pre_own[0], pre_all[2])

    def cross_copy(b):
        return remote(att.at[core, 0, b], att.at[core, 1, b], a_send.at[b], a_recv.at[b], (other + rank, tp))

    def core_copy(side, b):
        return remote(
            att.at[core, side, b], att.at[core, side, b], k_send.at[side, b], k_recv.at[side, b], (seq, other_core)
        )

    def core_wait(side, b):
        remote(
            att.at[core, side, b], att.at[1 - core, side, b], k_send.at[side, b], k_recv.at[side, b],
            (seq, other_core),
        ).wait_recv()

    contract = (((1,), (1,)), ((), ()))
    factor = LOG2E * HD ** (-0.5)

    def attend(i, carry):
        b = (rank + 1 + i) % GROUP
        both = acc[b] + project_rows((1 - group) * (n_tp // 2), b)
        row = meta_all[base + b]
        col = row.T
        first = lax.broadcasted_iota(jnp.int32, (count, count), 0)
        second = lax.broadcasted_iota(jnp.int32, (count, count), 1)
        hot = (col[:, 4:5] == second.astype(jnp.float32)).astype(jnp.bfloat16)
        looked = jnp.dot(hot, table[...], preferred_element_type=jnp.float32)
        looked = looked[:, : 2 * HD] + looked[:, 2 * HD : 4 * HD] + looked[:, 4 * HD :]
        cos = looked[:, :HD]
        sin = looked[:, HD:]

        def rotate(value):
            return value * cos + pltpu.roll(value, HD // 2, 1) * sin

        new_key = rotate(both[:, experts * HD : (experts + 1) * HD]).astype(jnp.bfloat16)
        new_value = both[:, (experts + 1) * HD :].astype(jnp.bfloat16)
        seen = (col[:, 5:6] == row[5:6, :]) & (second <= first)
        for k in range(slots):
            index = col[:, k : k + 1]
            chosen = jnp.zeros((count, HD), jnp.float32)
            for e in range(experts):
                chosen = jnp.where(index == float(e), both[:, e * HD : (e + 1) * HD], chosen)
            query = rotate(chosen).astype(jnp.bfloat16)
            far = lax.dot_general(query, pre_own[0, 0], contract, preferred_element_type=jnp.float32)
            near = lax.dot_general(query, new_key, contract, preferred_element_type=jnp.float32)
            near = jnp.where(seen, near, -1e30)
            top = jnp.maximum(jnp.max(far, axis=1, keepdims=True), jnp.max(near, axis=1, keepdims=True))
            far = jnp.exp2((far - top) * factor)
            near = jnp.where(seen, jnp.exp2((near - top) * factor), 0.0)
            total = jnp.sum(far, axis=1, keepdims=True) + jnp.sum(near, axis=1, keepdims=True)
            numer = jnp.dot(far.astype(jnp.bfloat16), pre_own[0, 1], preferred_element_type=jnp.float32)
            numer += jnp.dot(near.astype(jnp.bfloat16), new_value, preferred_element_type=jnp.float32)
            att[core, 0, b, k] = (numer * (col[:, slots + k : slots + k + 1] / total)).astype(jnp.bfloat16)
        cross_copy(b).start()
        core_copy(0, b).start()
        return carry

    tall = count // 2

    def y_copy(side, b, h):
        rows = pl.ds(h * tall, tall)
        return remote(
            y_out.at[side, b, rows], y_in.at[side, b, rows], y_send.at[side, b, h], y_recv.at[side, b, h],
            (seq, other_y),
        )

    def r_copy(side, b):
        return remote(
            r_out.at[side, b], r_in.at[side, rank], r_send.at[side, b], r_recv.at[side, rank], (base + b, tp)
        )

    def f_copy(side, h):
        return remote(
            f_out.at[side, pl.ds(h * tall, tall)], f_in.at[side, across_y, pl.ds(h * tall, tall)],
            f_send.at[side, h], f_recv.at[side, across_y, h],
            ((base if side == 0 else other) + rank, 2 * group + core),
        )

    def project(side, b):
        col = meta_all[b + (base if side == 0 else other)].T
        depth = experts * HD
        for e in range(experts):
            hot = [(col[:, k : k + 1] == float(e)).astype(jnp.bfloat16) for k in range(slots)]
            for s in range(2):
                spread[side, :, s * depth + e * HD : s * depth + (e + 1) * HD] = sum(
                    att[s, side, b, k] * hot[k] for k in range(slots)
                )
        for h in range(2):
            rows = slice(h * tall, (h + 1) * tall)
            y_out[side, b, rows] = jnp.dot(
                spread[side, rows], w_outs[1 - across_y].reshape(2 * depth, half),
                preferred_element_type=jnp.float32,
            ).astype(y_out.dtype)
            y_copy(side, b, h).start()
        kept[side, b] = jnp.dot(
            spread[side], w_outs[across_y].reshape(2 * depth, half), preferred_element_type=jnp.float32
        )

    def reduce(side, b):
        for h in range(2):
            y_copy(side, b, h).wait_recv()
        return kept[side, b] + y_in[side, b].astype(jnp.float32)

    def map_wait():
        for place in range(2):
            for source_core in range(2):
                from_rank = 2 * core + place
                mine = (from_rank == rank) & (source_core == core)

                @pl.when(mine)
                def _():
                    own_map_copy().wait()

                @pl.when(jnp.logical_not(mine))
                def _():
                    remote(
                        w_out.at[:, lanes(rank)], w_outs.at[place, source_core], x_send.at[0],
                        x_recv.at[place, source_core], (base + from_rank, 2 * across_y + source_core),
                    ).wait_recv()

    def near(i, carry):
        b = (rank + 1 + i) % GROUP
        core_wait(0, b)
        project(0, b)
        return carry

    def both(i, carry):
        attend(i, carry)

        return carry

    lax.fori_loop(0, GROUP, both, 0)
    map_wait()
    lax.fori_loop(0, GROUP, near, 0)

    def scatter(side, i):
        b = (rank + 1 + i) % GROUP
        r_out[side, b] = reduce(side, b).astype(r_out.dtype)
        r_copy(side, b).start()

    def finish(side):
        for step in range(1, GROUP):
            source = peer(step)
            remote(
                r_out.at[side, rank], r_in.at[side, source], r_send.at[side, rank], r_recv.at[side, source],
                (base + source, tp),
            ).wait_recv()
        for h in range(2):
            rows = slice(h * tall, (h + 1) * tall)
            total = kept[side, rank, rows]
            for step in range(1, GROUP):
                total = total + r_in[side, peer(step), rows].astype(jnp.float32)
            y_copy(side, rank, h).wait_recv()
            total = total + y_in[side, rank, rows].astype(jnp.float32)
            f_out[side, rows] = total.astype(f_out.dtype)
            if side == 0:

                @pl.when(across_y != group)
                def _():
                    f_copy(0, h).start()

            else:
                f_copy(1, h).start()

    def far(i, carry):
        b = (rank + 1 + i) % GROUP
        cross_copy(b).wait_recv()
        core_copy(1, b).start()

        @pl.when(i < GROUP - 1)
        def _():
            scatter(0, i)

        core_wait(1, b)
        project(1, b)

        @pl.when(i > 0)
        def _():
            scatter(1, i - 1)

        return carry

    lax.fori_loop(0, GROUP, far, 0)
    finish(0)
    finish(1)

    for step in range(1, GROUP):
        hid_copy(step).wait_send()
        for side in range(2):
            r_copy(side, peer(step)).wait_send()
        out_map_copy(step).wait_send()
    for step in range(1, n_seq):
        meta_copy(step).wait_send()

    @pl.when(rank // 2 != core)
    def _():
        out_map_copy(0).wait_send()

    for b in range(GROUP):
        cross_copy(b).wait_send()
        core_copy(0, b).wait_send()
        core_copy(1, b).wait_send()
        for side in range(2):
            for h in range(2):
                y_copy(side, b, h).wait_send()

    for step in range(3):
        pool_copy(step).wait_send()

    def w_sent(step, carry):
        for part in range(2):
            w_copy(part, step).wait_send()
        return carry

    lax.fori_loop(1, n_seq, w_sent, 0)
    for back in range(GROUP):
        for step in range(1, n_tp):
            tp_copy((rank + GROUP - back) % GROUP, hid, back, step).wait_send()

    def land(side, y, column):
        for h in range(2):
            rows = slice(h * tall, (h + 1) * tall)
            remote(
                f_out.at[0, rows], f_in.at[side, y, rows], f_send.at[0, h], f_recv.at[side, y, h],
                (seq if side == 0 else other + rank, 2 * y + core),
            ).wait_recv()
            out[rows, column * half : (column + 1) * half] = f_in[side, y, rows]

    @pl.when(across_y == group)
    def _():
        for y in range(2):
            @pl.when(across_y == y)
            def _():
                out[:, y * half : (y + 1) * half] = f_out[0]

            @pl.when(across_y != y)
            def _():
                land(0, y, y)

    @pl.when(across_y != group)
    def _():
        for y in range(2):
            land(1, y, y)
        for h in range(2):
            f_copy(0, h).wait_send()

    for h in range(2):
        f_copy(1, h).wait_send()


def paired(n_seq, n_tp, owner, lengths, w_query, w_keyval, pool, hid, w_out, gain, table, route_idx, route_gate):
    count, width = hid.shape
    slots = route_idx.shape[0]
    experts, rows, _ = w_query.shape
    half = w_out.shape[-1]
    dma = pltpu.SemaphoreType.DMA
    vmem = pl.BlockSpec(memory_space=pltpu.VMEM)
    smem = pl.BlockSpec(memory_space=pltpu.SMEM)
    low = jnp.bfloat16
    return pl.pallas_call(
        functools.partial(paired_kernel, n_seq, n_tp, slots),
        out_shape=jax.ShapeDtypeStruct((count, width), low),
        in_specs=[smem] * 2 + [ANY] * 5 + [vmem] * 4,
        out_specs=vmem,
        scratch_shapes=[
            pltpu.VMEM((n_seq, experts + 2, rows, HD), w_query.dtype),
            pltpu.VMEM((4, 2, pool.shape[1], HD), pool.dtype),
            pltpu.VMEM((2, 2, pool.shape[1], HD), pool.dtype),
            pltpu.VMEM((n_tp, GROUP) + hid.shape, hid.dtype),
            pltpu.VMEM((8, count), jnp.float32),
            pltpu.VMEM((n_seq, 8, count), jnp.float32),
            pltpu.VMEM((2, 2, experts, HD, half), w_out.dtype),
            pltpu.VMEM((n_tp, GROUP) + hid.shape, low),
            pltpu.VMEM((GROUP, count, (experts + 2) * HD), jnp.float32),
            pltpu.VMEM((2, 2, GROUP, slots, count, HD), low),
            pltpu.VMEM((2, count, 2 * experts * HD), low),
            pltpu.VMEM((2, GROUP, count, half), jnp.float32),
            pltpu.VMEM((2, GROUP, count, half), low),
            pltpu.VMEM((2, GROUP, count, half), low),
            pltpu.VMEM((2, GROUP, count, half), low),
            pltpu.VMEM((2, GROUP, count, half), low),
            pltpu.VMEM((2, count, half), low),
            pltpu.VMEM((2, 2, count, half), low),
            dma((7,)),
            dma((2, n_seq)),
            dma((2, n_seq)),
            dma((GROUP,)),
            dma((GROUP,)),
            dma((GROUP,)),
            dma((GROUP,)),
            dma((n_seq,)),
            dma((n_seq,)),
            dma((GROUP, n_tp)),
            dma((n_tp, GROUP)),
            dma((GROUP,)),
            dma((2, 2)),
            dma((GROUP,)),
            dma((GROUP,)),
            dma((2, GROUP)),
            dma((2, GROUP)),
            dma((2, GROUP, 2)),
            dma((2, GROUP, 2)),
            dma((2, GROUP)),
            dma((2, GROUP)),
            dma((2, 2)),
            dma((2, 2, 2)),
        ],
        compiler_params=pltpu.CompilerParams(
            collective_id=0, has_side_effects=True, vmem_limit_bytes=48 << 20
        ),
        name="paired",
    )(owner, lengths, w_query, w_keyval, pool, hid, w_out, gain, table, route_idx, route_gate)


def rope_table(count, prefix):
    freqs = np.float32(THETA) ** (-(np.arange(HD // 2, dtype=np.float32) * np.float32(2.0)) / np.float32(HD))
    angles = (np.arange(count) + prefix).astype(np.float32)[:, None] * freqs[None, :].astype(np.float32)
    cosine = np.cos(angles.astype(np.float64))
    sine = np.sin(angles.astype(np.float64))
    rest = np.concatenate([cosine, cosine, -sine, sine], axis=1).astype(np.float32)
    parts = []
    for _ in range(3):
        part = rest.astype(ml_dtypes.bfloat16)
        parts.append(part)
        rest = rest - part.astype(np.float32)
    return np.concatenate(parts, axis=1)


def per_device(
    n_seq, n_tp, hidden, lengths, cache_owner, cache_pool, norm_gain, route_idx, route_gate,
    w_query, w_keyval, w_out,
):
    groups = n_seq // GROUP
    count = hidden.shape[0]
    rows, experts, width = w_query.shape
    prefix = cache_pool.shape[1]
    assert width == GROUP * HD
    wide = w_out.shape[2]
    merged = wide < HD
    if n_seq == 2 * GROUP and n_tp == 4:
        return paired(
            n_seq, n_tp, cache_owner, lengths, w_query.swapaxes(0, 1), w_keyval.swapaxes(0, 1),
            cache_pool[0].swapaxes(0, 1), hidden, w_out, norm_gain.reshape(n_tp, 1, -1),
            jnp.asarray(rope_table(count, prefix)), route_idx.T, route_gate.T,
        )
    if merged:
        same_rank = [[g * GROUP + r for g in range(groups)] for r in range(GROUP)]
        per = groups // n_tp
        w_out = lax.all_gather(w_out, "seq", axis=0, axis_index_groups=same_rank)
        w_out = w_out.reshape(n_tp, per, experts, width, wide).transpose(0, 2, 3, 1, 4)
        w_out = w_out.reshape(n_tp, experts * width, per * wide)
    else:
        w_out = w_out.reshape(experts * width, wide)
    out = fused(
        n_seq, n_tp, merged, cache_owner, lengths, w_query.swapaxes(0, 1), w_keyval.swapaxes(0, 1),
        cache_pool[0].swapaxes(0, 1), hidden, w_out, norm_gain.reshape(n_tp, 1, -1),
        jnp.asarray(rope_table(count, prefix)), route_idx.T, route_gate.T,
    )
    if merged:
        out = out.reshape(count, GROUP, groups // n_tp, wide).transpose(0, 2, 1, 3).reshape(count, -1)
    return out


def solution(mesh):
    placed = (
        P("seq", "tp"),
        P("seq", None),
        P(),
        P("seq", None, None, "tp"),
        P(),
        P("seq", None),
        P("seq", None),
        P("seq", None, "tp"),
        P("seq", None, "tp"),
        P(None, "tp", "seq"),
    )
    body = functools.partial(per_device, mesh.shape["seq"], mesh.shape["tp"])
    return jax.shard_map(body, mesh=mesh, in_specs=placed, out_specs=P("seq", "tp"), check_vma=False)
```

```python
import functools

import jax
import jax.numpy as jnp
import ml_dtypes
import numpy as np
from jax import lax
from jax.experimental import pallas as pl
from jax.experimental.pallas import tpu as pltpu
from jax.sharding import PartitionSpec as P

HD = 128
GROUP = 4
EPSILON = 1e-05
THETA = 10000.0
LOG2E = 1.4426950408889634
MESH = pl.DeviceIdType.MESH
ANY = pl.BlockSpec(memory_space=pl.ANY)


def remote(src, dst, send_sem, recv_sem, device):
    return pltpu.make_async_remote_copy(
        src_ref=src,
        dst_ref=dst,
        send_sem=send_sem,
        recv_sem=recv_sem,
        device_id=device,
        device_id_type=MESH,
    )


def fused_kernel(
    n_seq, n_tp, slots, merged,
    owner_ref, lengths_ref, w_query, w_keyval, pool, hid, w_out, gain, table, route_idx, route_gate, out,
    w_all, pre_all, pre_own, hid_all, meta, meta_all, w_outs, gathered, spread, staged, landed,
    local_sem, w_send, w_recv, p_send, p_recv, h_send, h_recv, m_send, m_recv, t_send, t_recv,
    x_send, x_recv, a_send, a_recv, o_send, o_recv, o_local,
):
    groups = n_seq // GROUP
    seq = lax.axis_index("seq")
    tp = lax.axis_index("tp")
    group = seq // GROUP
    base = group * GROUP
    rank = seq % GROUP
    count, width = hid_all.shape[2:]
    experts = w_query.shape[0]
    chunks, _, wide = w_outs.shape
    places = landed.shape[0]
    cuts = chunks // groups

    def lanes(index):
        return pl.ds(pl.multiple_of(index * HD, HD), HD)

    tokens = lax.broadcasted_iota(jnp.int32, (1, count), 1)
    segment = jnp.zeros((1, count), jnp.int32)
    position = tokens
    end = 0
    for j in range(lengths_ref.shape[1]):
        length = lengths_ref[0, j]
        end = end + length
        past = tokens >= end
        segment = segment + jnp.where(past, 1, 0)
        position = position - jnp.where(past, length, 0)
    meta[0:slots] = route_idx[...].astype(jnp.float32)
    meta[slots : 2 * slots] = route_gate[...]
    meta[4:5] = position.astype(jnp.float32)
    meta[5:6] = segment.astype(jnp.float32)
    meta[6:8] = jnp.zeros((2, count), jnp.float32)

    def member(step):
        return ((group + step // GROUP) % groups) * GROUP + (rank + step % GROUP) % GROUP

    def peer(step):
        return (rank + step) % GROUP

    barrier = pltpu.get_barrier_semaphore()

    def greet(step, carry):
        pl.semaphore_signal(barrier, inc=1, device_id=(member(step), tp), device_id_type=MESH)
        return carry

    lax.fori_loop(1, n_seq, greet, 0)
    for step in range(GROUP):
        for turn in range(1, n_tp):
            pl.semaphore_signal(
                barrier, inc=1, device_id=(base + peer(step), (tp + turn) % n_tp), device_id_type=MESH
            )
    pl.semaphore_wait(barrier, n_seq - 1 + GROUP * (n_tp - 1))

    def hid_copy(step):
        return remote(hid, hid_all.at[tp, rank], h_send.at[step], h_recv.at[rank], (base + peer(step), tp))

    def meta_copy(step):
        return remote(meta, meta_all.at[rank], m_send.at[step], m_recv.at[rank], (base + peer(step), tp))

    beside = rank + 1 - 2 * (rank % 2)
    across = (rank + 2) % GROUP
    owner = owner_ref[group]

    def pool_copy(step):
        if step == 0:
            head, place, partner = beside, 0, beside
        elif step == 1:
            head, place, partner = (beside + 2) % GROUP, 1, beside
        else:
            return remote(
                pre_all.at[3], pre_all.at[2], p_send.at[2], p_recv.at[2], (base + across, tp)
            )
        return remote(
            pool.at[:, :, lanes(head)], pre_all.at[place], p_send.at[step], p_recv.at[step], (base + partner, tp)
        )

    def w_part(part, head, place):
        if part == 0:
            return w_query.at[:, :, lanes(head)], w_all.at[place, 0:experts]
        return w_keyval.at[:, :, lanes(head)], w_all.at[place, experts : experts + 2]

    def w_copy(part, step):
        dest = member(step)
        src, dst = w_part(part, dest % GROUP, seq)
        return remote(src, dst, w_send.at[part, step], w_recv.at[part, seq], (dest, tp))

    def tp_copy(block, src, back, step):
        return remote(
            src, hid_all.at[tp, block], t_send.at[back, step], t_recv.at[tp, back], (seq, (tp + step) % n_tp)
        )

    def out_map_copy(step, cut):
        dest = ((group + step) % groups) * GROUP + rank
        chunk = group * cuts + cut
        return remote(
            w_out.at[:, cut * wide : (cut + 1) * wide], w_outs.at[chunk],
            x_send.at[step * cuts + cut], x_recv.at[chunk], (dest, tp),
        )

    def w_start(step, carry):
        for part in range(2):
            w_copy(part, step).start()
        return carry

    def w_wait(step, carry):
        source = member(step)
        for part in range(2):
            src, dst = w_part(part, 0, source)
            remote(src, dst, w_send.at[part, step], w_recv.at[part, source], (source, tp)).wait_recv()
        return carry

    for step in range(1, GROUP):
        hid_copy(step).start()
    for step in range(1, n_tp):
        tp_copy(rank, hid, 0, step).start()
    for step in range(1, GROUP):
        meta_copy(step).start()
    for step in (1, 0):
        pool_copy(step).start()
    lax.fori_loop(GROUP, n_seq, w_start, 0)
    lax.fori_loop(1, GROUP, w_start, 0)
    own = [
        pltpu.make_async_copy(hid, hid_all.at[tp, rank], local_sem.at[0]),
        pltpu.make_async_copy(meta, meta_all.at[rank], local_sem.at[1]),
        pltpu.make_async_copy(*w_part(0, rank, seq), local_sem.at[2]),
        pltpu.make_async_copy(*w_part(1, rank, seq), local_sem.at[3]),
        pltpu.make_async_copy(pool.at[:, :, lanes(rank)], pre_own.at[0], local_sem.at[4]),
        pltpu.make_async_copy(pool.at[:, :, lanes(across)], pre_own.at[1], local_sem.at[5 + cuts]),
    ]
    if merged:
        own.append(pltpu.make_async_copy(w_out, w_outs, local_sem.at[5]))
    else:
        for cut in range(cuts):
            own.append(
                pltpu.make_async_copy(
                    w_out.at[:, cut * wide : (cut + 1) * wide],
                    w_outs.at[group * cuts + cut],
                    local_sem.at[5 + cut],
                )
            )
    for copy in own:
        copy.start()

    for back in range(1, GROUP):
        source = (rank + GROUP - back) % GROUP
        remote(hid, hid_all.at[tp, source], h_send.at[back], h_recv.at[source], (base + source, tp)).wait_recv()
        for step in range(1, n_tp):
            tp_copy(source, hid_all.at[tp, source], back, step).start()

    for copy in own:
        copy.wait()
    pool_copy(0).wait_recv()
    pool_copy(1).wait_recv()
    pre_all[3] = jnp.where(owner == rank, pre_own[1], pre_all[1])
    pool_copy(2).start()
    near_owner = jnp.where(owner == rank, pre_own[0], pre_all[0])
    pre_own[0] = near_owner
    lax.fori_loop(GROUP, n_seq, w_wait, 0)
    if not merged:
        for cut in range(cuts):
            for step in range(1, groups):
                out_map_copy(step, cut).start()
    for step in range(1, GROUP):
        source = peer(step)
        from_peer = (base + source, tp)
        remote(meta, meta_all.at[source], m_send.at[step], m_recv.at[source], from_peer).wait_recv()
    for back in range(GROUP):
        block = (rank + GROUP - back) % GROUP
        for step in range(1, n_tp):
            source = (tp + step) % n_tp
            remote(
                hid, hid_all.at[source, block], t_send.at[back, step], t_recv.at[source, back], (seq, source)
            ).wait_recv()
    lax.fori_loop(1, GROUP, w_wait, 0)
    pool_copy(2).wait_recv()
    pre_own[0] = jnp.where(owner // 2 == rank // 2, pre_own[0], pre_all[2])

    def att_copy(b, step):
        return remote(
            gathered.at[rank, b], gathered.at[rank, b], a_send.at[b, step], a_recv.at[rank, b],
            (base + peer(step), tp),
        )

    share = n_seq // n_tp
    contract = (((1,), (1,)), ((), ()))
    factor = LOG2E * HD ** (-0.5)

    def attend(b, carry):
        rows = [hid_all[t, b].astype(jnp.float32) for t in range(n_tp)]
        squares = sum(jnp.sum(x * x, axis=1, keepdims=True) for x in rows)
        inverse = lax.rsqrt(squares * (1.0 / (n_tp * width)) + EPSILON)
        acc = None
        for t in range(n_tp):
            normed = (rows[t] * inverse * gain[t]).astype(jnp.bfloat16)
            piece = jnp.concatenate(
                [w_all[t * share : (t + 1) * share, e].reshape(width, HD) for e in range(experts + 2)], axis=1
            )
            part = jnp.dot(normed, piece, preferred_element_type=jnp.float32)
            acc = part if acc is None else acc + part
        row = meta_all[b]
        col = row.T
        first = lax.broadcasted_iota(jnp.int32, (count, count), 0)
        second = lax.broadcasted_iota(jnp.int32, (count, count), 1)
        hot = (col[:, 4:5] == second.astype(jnp.float32)).astype(jnp.bfloat16)
        looked = jnp.dot(hot, table[...], preferred_element_type=jnp.float32)
        looked = looked[:, : 2 * HD] + looked[:, 2 * HD : 4 * HD] + looked[:, 4 * HD :]
        cos = looked[:, :HD]
        sin = looked[:, HD:]

        def rotate(value):
            return value * cos + pltpu.roll(value, HD // 2, 1) * sin

        new_key = rotate(acc[:, experts * HD : (experts + 1) * HD]).astype(jnp.bfloat16)
        new_value = acc[:, (experts + 1) * HD :].astype(jnp.bfloat16)
        seen = (col[:, 5:6] == row[5:6, :]) & (second <= first)
        for k in range(slots):
            index = col[:, k : k + 1]
            chosen = jnp.zeros((count, HD), jnp.float32)
            for e in range(experts):
                chosen = jnp.where(index == float(e), acc[:, e * HD : (e + 1) * HD], chosen)
            query = rotate(chosen).astype(jnp.bfloat16)
            far = lax.dot_general(query, pre_own[0, 0], contract, preferred_element_type=jnp.float32)
            near = lax.dot_general(query, new_key, contract, preferred_element_type=jnp.float32)
            near = jnp.where(seen, near, -1e30)
            top = jnp.maximum(jnp.max(far, axis=1, keepdims=True), jnp.max(near, axis=1, keepdims=True))
            far = jnp.exp2((far - top) * factor)
            near = jnp.where(seen, jnp.exp2((near - top) * factor), 0.0)
            total = jnp.sum(far, axis=1, keepdims=True) + jnp.sum(near, axis=1, keepdims=True)
            numer = jnp.dot(far.astype(jnp.bfloat16), pre_own[0, 1], preferred_element_type=jnp.float32)
            numer += jnp.dot(near.astype(jnp.bfloat16), new_value, preferred_element_type=jnp.float32)
            gathered[rank, b, k] = (numer * (col[:, slots + k : slots + k + 1] / total)).astype(jnp.bfloat16)
        for step in range(1, GROUP):
            att_copy(b, step).start()
        return carry

    lax.fori_loop(0, GROUP, attend, 0)

    def target(c):
        if merged:
            return c, rank
        feature = (c // cuts) * GROUP + rank
        return feature // groups, (feature % groups) * cuts + c % cuts

    def out_copy(b, c):
        column, place = target(c)
        return remote(
            staged.at[b, c], landed.at[place, tp], o_send.at[b, c], o_recv.at[place, tp], (base + b, column)
        )

    def own_copy(b, c):
        column, place = target(c)
        return pltpu.make_async_copy(staged.at[b, c], landed.at[place, tp], o_local.at[c])

    def is_own(b, c):
        return (b == rank) & (target(c)[0] == tp)

    def expand(i, carry):
        b = (rank + 1 + i) % GROUP
        for step in range(1, GROUP):
            source = peer(step)
            remote(
                gathered.at[rank, b], gathered.at[source, b], a_send.at[b, step], a_recv.at[source, b],
                (base + source, tp),
            ).wait_recv()
        col = meta_all[b].T
        depth = GROUP * HD
        for e in range(experts):
            hot = [(col[:, k : k + 1] == float(e)).astype(jnp.bfloat16) for k in range(slots)]
            for s in range(GROUP):
                spread[b, :, e * depth + s * HD : e * depth + (s + 1) * HD] = sum(
                    gathered[s, b, k] * hot[k] for k in range(slots)
                )
        return carry

    lax.fori_loop(0, GROUP, expand, 0)

    for j in range(chunks):
        c = j if merged else (group * cuts + j) % chunks
        if not merged and j >= cuts:
            remote(
                w_out.at[:, 0:wide], w_outs.at[c], x_send.at[0], x_recv.at[c], ((c // cuts) * GROUP + rank, tp)
            ).wait_recv()

        def project(i, carry):
            b = (rank + 1 + i) % GROUP
            staged[b, c] = jnp.dot(spread[b], w_outs[c], preferred_element_type=jnp.float32).astype(
                staged.dtype
            )

            @pl.when(is_own(b, c))
            def _():
                own_copy(b, c).start()

            @pl.when(jnp.logical_not(is_own(b, c)))
            def _():
                out_copy(b, c).start()

            return carry

        lax.fori_loop(0, GROUP, project, 0)

    for step in range(1, GROUP):
        hid_copy(step).wait_send()
        meta_copy(step).wait_send()
        for b in range(GROUP):
            att_copy(b, step).wait_send()

    for step in range(3):
        pool_copy(step).wait_send()

    def w_sent(step, carry):
        for part in range(2):
            w_copy(part, step).wait_send()
        return carry

    lax.fori_loop(1, n_seq, w_sent, 0)
    for back in range(GROUP):
        for step in range(1, n_tp):
            tp_copy((rank + GROUP - back) % GROUP, hid, back, step).wait_send()
    if not merged:
        for cut in range(cuts):
            for step in range(1, groups):
                out_map_copy(step, cut).wait_send()

    for place in range(places):
        if merged:
            source_rank, chunk = place, tp
        else:
            feature = tp * groups + place // cuts
            source_rank, chunk = feature % GROUP, (feature // GROUP) * cuts + place % cuts
        total = None
        for t in range(n_tp):
            mine = (source_rank == rank) & (tp == t)

            @pl.when(mine)
            def _():
                pltpu.make_async_copy(
                    staged.at[rank, chunk], landed.at[place, t], o_local.at[chunk]
                ).wait()

            @pl.when(jnp.logical_not(mine))
            def _():
                remote(
                    staged.at[0, 0], landed.at[place, t], o_send.at[0, 0], o_recv.at[place, t],
                    (base + source_rank, t),
                ).wait_recv()

            value = landed[place, t].astype(jnp.float32)
            total = value if total is None else total + value
        out[:, place * wide : (place + 1) * wide] = total.astype(out.dtype)

    for b in range(GROUP):
        for c in range(chunks):

            @pl.when(jnp.logical_not(is_own(b, c)))
            def _():
                out_copy(b, c).wait_send()


def fused(
    n_seq, n_tp, merged, owner, lengths, w_query, w_keyval, pool, hid, w_out, gain, table, route_idx, route_gate
):
    groups = n_seq // GROUP
    count = hid.shape[0]
    slots = route_idx.shape[0]
    experts, rows, _ = w_query.shape
    depth = w_out.shape[-2]
    dma = pltpu.SemaphoreType.DMA
    vmem = pl.BlockSpec(memory_space=pltpu.VMEM)
    smem = pl.BlockSpec(memory_space=pltpu.SMEM)
    wide = HD
    cuts = 1 if merged else w_out.shape[1] // wide
    chunks = w_out.shape[0] if merged else groups * cuts
    places = GROUP if merged else groups * cuts
    return pl.pallas_call(
        functools.partial(fused_kernel, n_seq, n_tp, slots, merged),
        out_shape=jax.ShapeDtypeStruct((count, places * wide), jnp.bfloat16),
        in_specs=[smem] * 2 + [ANY] * 5 + [vmem] * 4,
        out_specs=vmem,
        scratch_shapes=[
            pltpu.VMEM((n_seq, experts + 2, rows, HD), w_query.dtype),
            pltpu.VMEM((4, 2, pool.shape[1], HD), pool.dtype),
            pltpu.VMEM((2, 2, pool.shape[1], HD), pool.dtype),
            pltpu.VMEM((n_tp, GROUP) + hid.shape, hid.dtype),
            pltpu.VMEM((8, count), jnp.float32),
            pltpu.VMEM((GROUP, 8, count), jnp.float32),
            pltpu.VMEM((chunks, depth, wide), w_out.dtype),
            pltpu.VMEM((GROUP, GROUP, slots, count, HD), jnp.bfloat16),
            pltpu.VMEM((GROUP, count, depth), jnp.bfloat16),
            pltpu.VMEM((GROUP, chunks, count, wide), jnp.bfloat16),
            pltpu.VMEM((places, n_tp, count, wide), jnp.bfloat16),
            dma((6 + cuts,)),
            dma((2, n_seq)),
            dma((2, n_seq)),
            dma((GROUP,)),
            dma((GROUP,)),
            dma((GROUP,)),
            dma((GROUP,)),
            dma((GROUP,)),
            dma((GROUP,)),
            dma((GROUP, n_tp)),
            dma((n_tp, GROUP)),
            dma((groups * cuts,)),
            dma((chunks,)),
            dma((GROUP, GROUP)),
            dma((GROUP, GROUP)),
            dma((GROUP, chunks)),
            dma((places, n_tp)),
            dma((chunks,)),
        ],
        compiler_params=pltpu.CompilerParams(
            collective_id=0, has_side_effects=True, vmem_limit_bytes=48 << 20
        ),
        name="fused",
    )(owner, lengths, w_query, w_keyval, pool, hid, w_out, gain, table, route_idx, route_gate)


def paired_kernel(
    n_seq, n_tp, slots,
    owner_ref, lengths_ref, w_query, w_keyval, pool, hid, w_out, gain, table, route_idx, route_gate, out,
    w_all, pre_all, pre_own, hid_all, meta, meta_all, w_outs, normed, acc, att, spread, kept, y_out, y_in, r_out, r_in, f_out, f_in,
    local_sem, w_send, w_recv, p_send, p_recv, h_send, h_recv, m_send, m_recv, t_send, t_recv,
    x_send, x_recv, a_send, a_recv, k_send, k_recv, y_send, y_recv, r_send, r_recv, f_send, f_recv,
):
    groups = n_seq // GROUP
    seq = lax.axis_index("seq")
    tp = lax.axis_index("tp")
    group = seq // GROUP
    base = group * GROUP
    rank = seq % GROUP
    count, width = hid_all.shape[2:]
    experts = w_query.shape[0]
    core = tp % 2
    across_y = tp // 2
    other_core = tp + 1 - 2 * core
    other_y = (tp + 2) % n_tp
    other = (base + GROUP) % n_seq
    half = w_outs.shape[-1]

    def lanes(index):
        return pl.ds(pl.multiple_of(index * HD, HD), HD)

    def member(step):
        return ((group + step // GROUP) % groups) * GROUP + (rank + step % GROUP) % GROUP

    def peer(step):
        return (rank + step) % GROUP

    barrier = pltpu.get_barrier_semaphore()

    def greet(step, carry):
        pl.semaphore_signal(barrier, inc=1, device_id=(member(step), tp), device_id_type=MESH)
        return carry

    lax.fori_loop(1, n_seq, greet, 0)
    for step in range(GROUP):
        for turn in range(1, n_tp):
            pl.semaphore_signal(
                barrier, inc=1, device_id=(base + peer(step), (tp + turn) % n_tp), device_id_type=MESH
            )
    pl.semaphore_signal(barrier, inc=1, device_id=(other + rank, other_y), device_id_type=MESH)
    tokens = lax.broadcasted_iota(jnp.int32, (1, count), 1)
    segment = jnp.zeros((1, count), jnp.int32)
    position = tokens
    end = 0
    for j in range(lengths_ref.shape[1]):
        length = lengths_ref[0, j]
        end = end + length
        past = tokens >= end
        segment = segment + jnp.where(past, 1, 0)
        position = position - jnp.where(past, length, 0)
    meta[0:slots] = route_idx[...].astype(jnp.float32)
    meta[slots : 2 * slots] = route_gate[...]
    meta[4:5] = position.astype(jnp.float32)
    meta[5:6] = segment.astype(jnp.float32)
    meta[6:8] = jnp.zeros((2, count), jnp.float32)

    pl.semaphore_wait(barrier, n_seq + GROUP * (n_tp - 1))

    def hid_copy(step):
        return remote(hid, hid_all.at[tp, rank], h_send.at[step], h_recv.at[rank], (base + peer(step), tp))

    def meta_copy(step):
        return remote(meta, meta_all.at[seq], m_send.at[step], m_recv.at[seq], (member(step), tp))

    beside = rank + 1 - 2 * (rank % 2)
    across = (rank + 2) % GROUP
    owner = owner_ref[group]

    def pool_copy(step):
        if step == 0:
            head, place, partner = beside, 0, beside
        elif step == 1:
            head, place, partner = (beside + 2) % GROUP, 1, beside
        else:
            return remote(
                pre_all.at[3], pre_all.at[2], p_send.at[2], p_recv.at[2], (base + across, tp)
            )
        return remote(
            pool.at[:, :, lanes(head)], pre_all.at[place], p_send.at[step], p_recv.at[step], (base + partner, tp)
        )

    def w_part(part, head, place):
        if part == 0:
            return w_query.at[:, :, lanes(head)], w_all.at[place, 0:experts]
        return w_keyval.at[:, :, lanes(head)], w_all.at[place, experts : experts + 2]

    def w_copy(part, step):
        dest = member(step)
        src, dst = w_part(part, dest % GROUP, seq)
        return remote(src, dst, w_send.at[part, step], w_recv.at[part, seq], (dest, tp))

    def tp_copy(block, src, back, step):
        return remote(
            src, hid_all.at[tp, block], t_send.at[back, step], t_recv.at[tp, back], (seq, (tp + step) % n_tp)
        )

    def out_map_copy(step):
        return remote(
            w_out.at[:, lanes(peer(step))], w_outs.at[rank % 2, core], x_send.at[step], x_recv.at[rank % 2, core],
            (base + peer(step), 2 * across_y + rank // 2),
        )

    def own_map_copy():
        return pltpu.make_async_copy(w_out.at[:, lanes(rank)], w_outs.at[rank % 2, core], local_sem.at[5])

    def w_start(step, carry):
        for part in range(2):
            w_copy(part, step).start()
        return carry

    def w_wait(step, carry):
        source = member(step)
        for part in range(2):
            src, dst = w_part(part, 0, source)
            remote(src, dst, w_send.at[part, step], w_recv.at[part, source], (source, tp)).wait_recv()
        return carry

    lax.fori_loop(GROUP, n_seq, w_start, 0)
    for step in range(1, GROUP):
        hid_copy(step).start()
    for step in range(1, n_tp):
        tp_copy(rank, hid, 0, step).start()
    for step in range(1, n_seq):
        meta_copy(step).start()
    for step in (1, 0):
        pool_copy(step).start()
    lax.fori_loop(1, GROUP, w_start, 0)
    own = [
        pltpu.make_async_copy(hid, hid_all.at[tp, rank], local_sem.at[0]),
        pltpu.make_async_copy(meta, meta_all.at[seq], local_sem.at[1]),
        pltpu.make_async_copy(*w_part(0, rank, seq), local_sem.at[2]),
        pltpu.make_async_copy(*w_part(1, rank, seq), local_sem.at[3]),
        pltpu.make_async_copy(pool.at[:, :, lanes(rank)], pre_own.at[0], local_sem.at[4]),
        pltpu.make_async_copy(pool.at[:, :, lanes(across)], pre_own.at[1], local_sem.at[6]),
    ]
    for copy in own:
        copy.start()

    for back in range(1, GROUP):
        source = (rank + GROUP - back) % GROUP
        remote(hid, hid_all.at[tp, source], h_send.at[back], h_recv.at[source], (base + source, tp)).wait_recv()
        for step in range(1, n_tp):
            tp_copy(source, hid_all.at[tp, source], back, step).start()

    for copy in own:
        copy.wait()
    pool_copy(0).wait_recv()
    pool_copy(1).wait_recv()
    pre_all[3] = jnp.where(owner == rank, pre_own[1], pre_all[1])
    pool_copy(2).start()
    for step in range(1, GROUP):
        out_map_copy(step).start()

    @pl.when(rank // 2 == core)
    def _():
        own_map_copy().start()

    @pl.when(rank // 2 != core)
    def _():
        out_map_copy(0).start()

    near_owner = jnp.where(owner == rank, pre_own[0], pre_all[0])
    pre_own[0] = near_owner
    for step in range(1, n_seq):
        source = member(step)
        remote(meta, meta_all.at[source], m_send.at[step], m_recv.at[source], (source, tp)).wait_recv()
    for back in range(GROUP):
        block = (rank + GROUP - back) % GROUP
        for step in range(1, n_tp):
            source = (tp + step) % n_tp
            remote(
                hid, hid_all.at[source, block], t_send.at[back, step], t_recv.at[source, back], (seq, source)
            ).wait_recv()
    share = n_seq // n_tp

    def normalise(b, carry):
        rows = [hid_all[t, b].astype(jnp.float32) for t in range(n_tp)]
        squares = sum(jnp.sum(x * x, axis=1, keepdims=True) for x in rows)
        inverse = lax.rsqrt(squares * (1.0 / (n_tp * width)) + EPSILON)
        for t in range(n_tp):
            normed[t, b] = (rows[t] * inverse * gain[t]).astype(normed.dtype)
        return carry

    lax.fori_loop(0, GROUP, normalise, 0)

    def project_rows(first, b):
        total = None
        for i in range(n_tp // 2):
            t = first + i
            piece = jnp.concatenate(
                [w_all[pl.ds(t * share, share), e].reshape(width, HD) for e in range(experts + 2)], axis=1
            )
            part = jnp.dot(normed[t, b], piece, preferred_element_type=jnp.float32)
            total = part if total is None else total + part
        return total

    def project_near(b, carry):
        acc[b] = project_rows(group * (n_tp // 2), b)
        return carry

    lax.fori_loop(1, GROUP, w_wait, 0)
    lax.fori_loop(0, GROUP, project_near, 0)
    lax.fori_loop(GROUP, n_seq, w_wait, 0)
    pool_copy(2).wait_recv()
    pre_own[0] = jnp.where(owner // 2 == rank // 2, pre_own[0], pre_all[2])

    def cross_copy(b):
        return remote(att.at[core, 0, b], att.at[core, 1, b], a_send.at[b], a_recv.at[b], (other + rank, tp))

    def core_copy(side, b):
        return remote(
            att.at[core, side, b], att.at[core, side, b], k_send.at[side, b], k_recv.at[side, b], (seq, other_core)
        )

    def core_wait(side, b):
        remote(
            att.at[core, side, b], att.at[1 - core, side, b], k_send.at[side, b], k_recv.at[side, b],
            (seq, other_core),
        ).wait_recv()

    contract = (((1,), (1,)), ((), ()))
    factor = LOG2E * HD ** (-0.5)

    def attend(i, carry):
        b = (rank + 1 + i) % GROUP
        both = acc[b] + project_rows((1 - group) * (n_tp // 2), b)
        row = meta_all[base + b]
        col = row.T
        first = lax.broadcasted_iota(jnp.int32, (count, count), 0)
        second = lax.broadcasted_iota(jnp.int32, (count, count), 1)
        hot = (col[:, 4:5] == second.astype(jnp.float32)).astype(jnp.bfloat16)
        looked = jnp.dot(hot, table[...], preferred_element_type=jnp.float32)
        looked = looked[:, : 2 * HD] + looked[:, 2 * HD : 4 * HD] + looked[:, 4 * HD :]
        cos = looked[:, :HD]
        sin = looked[:, HD:]

        def rotate(value):
            return value * cos + pltpu.roll(value, HD // 2, 1) * sin

        new_key = rotate(both[:, experts * HD : (experts + 1) * HD]).astype(jnp.bfloat16)
        new_value = both[:, (experts + 1) * HD :].astype(jnp.bfloat16)
        seen = (col[:, 5:6] == row[5:6, :]) & (second <= first)
        for k in range(slots):
            index = col[:, k : k + 1]
            chosen = jnp.zeros((count, HD), jnp.float32)
            for e in range(experts):
                chosen = jnp.where(index == float(e), both[:, e * HD : (e + 1) * HD], chosen)
            query = rotate(chosen).astype(jnp.bfloat16)
            far = lax.dot_general(query, pre_own[0, 0], contract, preferred_element_type=jnp.float32)
            near = lax.dot_general(query, new_key, contract, preferred_element_type=jnp.float32)
            near = jnp.where(seen, near, -1e30)
            top = jnp.maximum(jnp.max(far, axis=1, keepdims=True), jnp.max(near, axis=1, keepdims=True))
            far = jnp.exp2((far - top) * factor)
            near = jnp.where(seen, jnp.exp2((near - top) * factor), 0.0)
            total = jnp.sum(far, axis=1, keepdims=True) + jnp.sum(near, axis=1, keepdims=True)
            numer = jnp.dot(far.astype(jnp.bfloat16), pre_own[0, 1], preferred_element_type=jnp.float32)
            numer += jnp.dot(near.astype(jnp.bfloat16), new_value, preferred_element_type=jnp.float32)
            att[core, 0, b, k] = (numer * (col[:, slots + k : slots + k + 1] / total)).astype(jnp.bfloat16)
        cross_copy(b).start()
        core_copy(0, b).start()
        return carry

    tall = count // 2

    def y_copy(side, b, h):
        rows = pl.ds(h * tall, tall)
        return remote(
            y_out.at[side, b, rows], y_in.at[side, b, rows], y_send.at[side, b, h], y_recv.at[side, b, h],
            (seq, other_y),
        )

    def r_copy(side, b):
        return remote(
            r_out.at[side, b], r_in.at[side, rank], r_send.at[side, b], r_recv.at[side, rank], (base + b, tp)
        )

    def f_copy(side, h):
        return remote(
            f_out.at[side, pl.ds(h * tall, tall)], f_in.at[side, across_y, pl.ds(h * tall, tall)],
            f_send.at[side, h], f_recv.at[side, across_y, h],
            ((base if side == 0 else other) + rank, 2 * group + core),
        )

    def project(side, b):
        col = meta_all[b + (base if side == 0 else other)].T
        depth = experts * HD
        for e in range(experts):
            hot = [(col[:, k : k + 1] == float(e)).astype(jnp.bfloat16) for k in range(slots)]
            for s in range(2):
                spread[side, :, s * depth + e * HD : s * depth + (e + 1) * HD] = sum(
                    att[s, side, b, k] * hot[k] for k in range(slots)
                )
        for h in range(2):
            rows = slice(h * tall, (h + 1) * tall)
            y_out[side, b, rows] = jnp.dot(
                spread[side, rows], w_outs[1 - across_y].reshape(2 * depth, half),
                preferred_element_type=jnp.float32,
            ).astype(y_out.dtype)
            y_copy(side, b, h).start()
        kept[side, b] = jnp.dot(
            spread[side], w_outs[across_y].reshape(2 * depth, half), preferred_element_type=jnp.float32
        )

    def reduce(side, b):
        for h in range(2):
            y_copy(side, b, h).wait_recv()
        return kept[side, b] + y_in[side, b].astype(jnp.float32)

    def map_wait():
        for place in range(2):
            for source_core in range(2):
                from_rank = 2 * core + place
                mine = (from_rank == rank) & (source_core == core)

                @pl.when(mine)
                def _():
                    own_map_copy().wait()

                @pl.when(jnp.logical_not(mine))
                def _():
                    remote(
                        w_out.at[:, lanes(rank)], w_outs.at[place, source_core], x_send.at[0],
                        x_recv.at[place, source_core], (base + from_rank, 2 * across_y + source_core),
                    ).wait_recv()

    def near(i, carry):
        b = (rank + 1 + i) % GROUP
        core_wait(0, b)
        project(0, b)
        return carry

    def both(i, carry):
        attend(i, carry)

        return carry

    lax.fori_loop(0, GROUP, both, 0)
    map_wait()
    lax.fori_loop(0, GROUP, near, 0)

    def scatter(side, i):
        b = (rank + 1 + i) % GROUP
        r_out[side, b] = reduce(side, b).astype(r_out.dtype)
        r_copy(side, b).start()

    def finish(side):
        for step in range(1, GROUP):
            source = peer(step)
            remote(
                r_out.at[side, rank], r_in.at[side, source], r_send.at[side, rank], r_recv.at[side, source],
                (base + source, tp),
            ).wait_recv()
        for h in range(2):
            rows = slice(h * tall, (h + 1) * tall)
            total = kept[side, rank, rows]
            for step in range(1, GROUP):
                total = total + r_in[side, peer(step), rows].astype(jnp.float32)
            y_copy(side, rank, h).wait_recv()
            total = total + y_in[side, rank, rows].astype(jnp.float32)
            f_out[side, rows] = total.astype(f_out.dtype)
            if side == 0:

                @pl.when(across_y != group)
                def _():
                    f_copy(0, h).start()

            else:
                f_copy(1, h).start()

    def far(i, carry):
        b = (rank + 1 + i) % GROUP
        cross_copy(b).wait_recv()
        core_copy(1, b).start()

        @pl.when(i < GROUP - 1)
        def _():
            scatter(0, i)

        core_wait(1, b)
        project(1, b)

        @pl.when(i > 0)
        def _():
            scatter(1, i - 1)

        return carry

    lax.fori_loop(0, GROUP, far, 0)
    finish(0)
    finish(1)

    for step in range(1, GROUP):
        hid_copy(step).wait_send()
        for side in range(2):
            r_copy(side, peer(step)).wait_send()
        out_map_copy(step).wait_send()
    for step in range(1, n_seq):
        meta_copy(step).wait_send()

    @pl.when(rank // 2 != core)
    def _():
        out_map_copy(0).wait_send()

    for b in range(GROUP):
        cross_copy(b).wait_send()
        core_copy(0, b).wait_send()
        core_copy(1, b).wait_send()
        for side in range(2):
            for h in range(2):
                y_copy(side, b, h).wait_send()

    for step in range(3):
        pool_copy(step).wait_send()

    def w_sent(step, carry):
        for part in range(2):
            w_copy(part, step).wait_send()
        return carry

    lax.fori_loop(1, n_seq, w_sent, 0)
    for back in range(GROUP):
        for step in range(1, n_tp):
            tp_copy((rank + GROUP - back) % GROUP, hid, back, step).wait_send()

    def land(side, y, column):
        for h in range(2):
            rows = slice(h * tall, (h + 1) * tall)
            remote(
                f_out.at[0, rows], f_in.at[side, y, rows], f_send.at[0, h], f_recv.at[side, y, h],
                (seq if side == 0 else other + rank, 2 * y + core),
            ).wait_recv()
            out[rows, column * half : (column + 1) * half] = f_in[side, y, rows]

    @pl.when(across_y == group)
    def _():
        for y in range(2):
            @pl.when(across_y == y)
            def _():
                out[:, y * half : (y + 1) * half] = f_out[0]

            @pl.when(across_y != y)
            def _():
                land(0, y, y)

    @pl.when(across_y != group)
    def _():
        for y in range(2):
            land(1, y, y)
        for h in range(2):
            f_copy(0, h).wait_send()

    for h in range(2):
        f_copy(1, h).wait_send()


def paired(n_seq, n_tp, owner, lengths, w_query, w_keyval, pool, hid, w_out, gain, table, route_idx, route_gate):
    count, width = hid.shape
    slots = route_idx.shape[0]
    experts, rows, _ = w_query.shape
    half = w_out.shape[-1]
    dma = pltpu.SemaphoreType.DMA
    vmem = pl.BlockSpec(memory_space=pltpu.VMEM)
    smem = pl.BlockSpec(memory_space=pltpu.SMEM)
    low = jnp.bfloat16
    return pl.pallas_call(
        functools.partial(paired_kernel, n_seq, n_tp, slots),
        out_shape=jax.ShapeDtypeStruct((count, width), low),
        in_specs=[smem] * 2 + [ANY] * 5 + [vmem] * 4,
        out_specs=vmem,
        scratch_shapes=[
            pltpu.VMEM((n_seq, experts + 2, rows, HD), w_query.dtype),
            pltpu.VMEM((4, 2, pool.shape[1], HD), pool.dtype),
            pltpu.VMEM((2, 2, pool.shape[1], HD), pool.dtype),
            pltpu.VMEM((n_tp, GROUP) + hid.shape, hid.dtype),
            pltpu.VMEM((8, count), jnp.float32),
            pltpu.VMEM((n_seq, 8, count), jnp.float32),
            pltpu.VMEM((2, 2, experts, HD, half), w_out.dtype),
            pltpu.VMEM((n_tp, GROUP) + hid.shape, low),
            pltpu.VMEM((GROUP, count, (experts + 2) * HD), jnp.float32),
            pltpu.VMEM((2, 2, GROUP, slots, count, HD), low),
            pltpu.VMEM((2, count, 2 * experts * HD), low),
            pltpu.VMEM((2, GROUP, count, half), jnp.float32),
            pltpu.VMEM((2, GROUP, count, half), low),
            pltpu.VMEM((2, GROUP, count, half), low),
            pltpu.VMEM((2, GROUP, count, half), low),
            pltpu.VMEM((2, GROUP, count, half), low),
            pltpu.VMEM((2, count, half), low),
            pltpu.VMEM((2, 2, count, half), low),
            dma((7,)),
            dma((2, n_seq)),
            dma((2, n_seq)),
            dma((GROUP,)),
            dma((GROUP,)),
            dma((GROUP,)),
            dma((GROUP,)),
            dma((n_seq,)),
            dma((n_seq,)),
            dma((GROUP, n_tp)),
            dma((n_tp, GROUP)),
            dma((GROUP,)),
            dma((2, 2)),
            dma((GROUP,)),
            dma((GROUP,)),
            dma((2, GROUP)),
            dma((2, GROUP)),
            dma((2, GROUP, 2)),
            dma((2, GROUP, 2)),
            dma((2, GROUP)),
            dma((2, GROUP)),
            dma((2, 2)),
            dma((2, 2, 2)),
        ],
        compiler_params=pltpu.CompilerParams(
            collective_id=0, has_side_effects=True, vmem_limit_bytes=48 << 20
        ),
        name="paired",
    )(owner, lengths, w_query, w_keyval, pool, hid, w_out, gain, table, route_idx, route_gate)


def rope_table(count, prefix):
    freqs = np.float32(THETA) ** (-(np.arange(HD // 2, dtype=np.float32) * np.float32(2.0)) / np.float32(HD))
    angles = (np.arange(count) + prefix).astype(np.float32)[:, None] * freqs[None, :].astype(np.float32)
    cosine = np.cos(angles.astype(np.float64))
    sine = np.sin(angles.astype(np.float64))
    rest = np.concatenate([cosine, cosine, -sine, sine], axis=1).astype(np.float32)
    parts = []
    for _ in range(3):
        part = rest.astype(ml_dtypes.bfloat16)
        parts.append(part)
        rest = rest - part.astype(np.float32)
    return np.concatenate(parts, axis=1)


def per_device(
    n_seq, n_tp, hidden, lengths, cache_owner, cache_pool, norm_gain, route_idx, route_gate,
    w_query, w_keyval, w_out,
):
    groups = n_seq // GROUP
    count = hidden.shape[0]
    rows, experts, width = w_query.shape
    prefix = cache_pool.shape[1]
    assert width == GROUP * HD
    wide = w_out.shape[2]
    merged = wide < HD
    if n_seq == 2 * GROUP and n_tp == 4:
        return paired(
            n_seq, n_tp, cache_owner, lengths, w_query.swapaxes(0, 1), w_keyval.swapaxes(0, 1),
            cache_pool[0].swapaxes(0, 1), hidden, w_out, norm_gain.reshape(n_tp, 1, -1),
            jnp.asarray(rope_table(count, prefix)), route_idx.T, route_gate.T,
        )
    if merged:
        same_rank = [[g * GROUP + r for g in range(groups)] for r in range(GROUP)]
        per = groups // n_tp
        w_out = lax.all_gather(w_out, "seq", axis=0, axis_index_groups=same_rank)
        w_out = w_out.reshape(n_tp, per, experts, width, wide).transpose(0, 2, 3, 1, 4)
        w_out = w_out.reshape(n_tp, experts * width, per * wide)
    else:
        w_out = w_out.reshape(experts * width, wide)
    out = fused(
        n_seq, n_tp, merged, cache_owner, lengths, w_query.swapaxes(0, 1), w_keyval.swapaxes(0, 1),
        cache_pool[0].swapaxes(0, 1), hidden, w_out, norm_gain.reshape(n_tp, 1, -1),
        jnp.asarray(rope_table(count, prefix)), route_idx.T, route_gate.T,
    )
    if merged:
        out = out.reshape(count, GROUP, groups // n_tp, wide).transpose(0, 2, 1, 3).reshape(count, -1)
    return out


def solution(mesh):
    placed = (
        P("seq", "tp"),
        P("seq", None),
        P(),
        P("seq", None, None, "tp"),
        P(),
        P("seq", None),
        P("seq", None),
        P("seq", None, "tp"),
        P("seq", None, "tp"),
        P(None, "tp", "seq"),
    )
    body = functools.partial(per_device, mesh.shape["seq"], mesh.shape["tp"])
    return jax.shard_map(body, mesh=mesh, in_specs=placed, out_specs=P("seq", "tp"), check_vma=False)
```
